32 devices in a mesh: gx: 8 (over z, x), gy: 4 (over y, core).
Axes of the slice: x: 2, y: 2, z: 4, core: 2. Of those that a mesh axis runs over, the one named last changes fastest.
Arguments:
- forcing: float32 [3, 64, 64, 512], P(None, 'gx', 'gy'), may hold values from -6.5 to 6.5
- phase_ids: int32 [64, 64, 512], P('gx', 'gy'), may hold values from 0 to 3
Outputs:
- velocity: float32 [3, 64, 64, 512], P(None, 'gx', 'gy')
The draws below stay inside these ranges and needn't reach their ends.
All inputs are finite; a program needn't handle non-finite values.
Results may differ from the reference program's by a relative error of at most 0.0003.
Values sent between devices are 32-bit elements; how exact they have to be, the bound alone decides.
A program may use at most 128 MiB of HBM per device.

```python
import jax
import jax.numpy as jnp
from jax import lax

NZ = 512
COARSE_SWEEPS = 6
NX = 64
NY = 64


def draw_forcing(key, part):
    base = jax.random.normal(key, (3, NX, NY, NZ), jnp.float32)
    return jnp.clip(base, -6.0, 6.0)


def with_ends(array, key, low, top_value):
    shape = array.shape
    place = [jax.random.randint(jax.random.fold_in(key, axis), (), 0, shape[axis]) for axis in range(len(shape))]
    array = array.at[tuple(place)].set(low)
    longest = shape.index(max(shape))
    place[longest] = (place[longest] + 1) % shape[longest]
    return array.at[tuple(place)].set(top_value)


def setup_inputs(seed: int = 0) -> dict:
    arg_keys = jax.random.split(jax.random.key(seed), 3)
    forcing = draw_forcing(jax.random.fold_in(arg_keys[2], 71), 0)
    phase_ids = with_ends(jax.random.randint(arg_keys[1], (NX, NY, NZ), 0, 4), jax.random.fold_in(arg_keys[1], 1), 0, 3).astype(jnp.int32)
    return {"forcing": forcing, "phase_ids": phase_ids}


viscosities = (0.2, 0.6, 1.5, 4.0)
relax_weight = 2.0 / 3.0


def lookup(phase_ids):
    viscosity = jnp.zeros(phase_ids.shape, jnp.float32)
    for material, visc_value in enumerate(viscosities):
        viscosity = viscosity + jnp.where(phase_ids == material, jnp.float32(visc_value), jnp.float32(0.0))
    return viscosity


def restrict(values):
    extent = values.shape
    leading = extent[:-3]
    blocks = values.reshape(leading + (extent[-3] // 2, 2, extent[-2] // 2, 2, extent[-1] // 2, 2))
    return jnp.mean(blocks, axis=(-5, -3, -1))


def prolong(values):
    return jnp.repeat(jnp.repeat(jnp.repeat(values, 2, axis=-3), 2, axis=-2), 2, axis=-1)


def pad_plane(values, width):
    padding = [(0, 0)] * (values.ndim - 3) + [(width, width), (width, width), (0, 0)]
    return jnp.pad(values, padding)


def face_set(wide_visc, spacing):
    center = wide_visc[1:-1, 1:-1, :]
    z_padded = jnp.pad(center, ((0, 0), (0, 0), (1, 1)))
    besides = (wide_visc[2:, 1:-1, :], wide_visc[:-2, 1:-1, :], wide_visc[1:-1, 2:, :],
               wide_visc[1:-1, :-2, :], z_padded[:, :, 2:], z_padded[:, :, :-2])
    coeffs = tuple(jnp.where(beside > 0.0, 0.5 * (center + beside), center) / spacing for beside in besides)
    diagonal = coeffs[0]
    for entry in coeffs[1:]:
        diagonal = diagonal + entry
    inside = center > 0.0
    inverse = jnp.where(inside, 1.0 / jnp.where(inside, diagonal, 1.0), 0.0)
    return coeffs, inverse


def apply_operator(wide_field, coeffs):
    center = wide_field[..., 1:-1, 1:-1, :]
    padding = [(0, 0)] * (center.ndim - 1) + [(1, 1)]
    z_padded = jnp.pad(center, padding)
    besides = (wide_field[..., 2:, 1:-1, :], wide_field[..., :-2, 1:-1, :], wide_field[..., 1:-1, 2:, :],
               wide_field[..., 1:-1, :-2, :], z_padded[..., 2:], z_padded[..., :-2])
    summed = jnp.zeros_like(center)
    for face_coeff, beside in zip(coeffs, besides):
        summed = summed + face_coeff * (center - beside)
    return summed


def reference(forcing, phase_ids):
    viscosity = lookup(phase_ids)
    level_sets = []
    for level_index in range(3):
        level_sets.append(face_set(pad_plane(viscosity, 1), 4.0 ** level_index))
        if level_index < 2:
            viscosity = restrict(viscosity)

    def jacobi_sweep(current, source, level_set):
        coeffs, inverse = level_set
        return current + relax_weight * (source - apply_operator(pad_plane(current, 1), coeffs)) * inverse

    def descend(source, level_set):
        coeffs, inverse = level_set
        current = relax_weight * source * inverse
        current = jacobi_sweep(current, source, level_set)
        residual = source - apply_operator(pad_plane(current, 1), coeffs)
        return current, restrict(residual)

    def single(source):
        fine_velocity, source_one = descend(source, level_sets[0])
        middle, source_two = descend(source_one, level_sets[1])
        coarse = relax_weight * source_two * level_sets[2][1]
        for repeat in range(COARSE_SWEEPS - 1):
            coarse = jacobi_sweep(coarse, source_two, level_sets[2])
        middle = middle + prolong(coarse)
        middle = jacobi_sweep(middle, source_one, level_sets[1])
        middle = jacobi_sweep(middle, source_one, level_sets[1])
        fine_velocity = fine_velocity + prolong(middle)
        fine_velocity = jacobi_sweep(fine_velocity, source, level_sets[0])
        fine_velocity = jacobi_sweep(fine_velocity, source, level_sets[0])
        return fine_velocity

    return lax.map(single, forcing)
```

```python
import functools

import jax
import jax.numpy as jnp
from jax import lax
from jax.experimental import pallas as pl
from jax.experimental.pallas import tpu as pltpu
from jax.sharding import PartitionSpec as P

COARSE_SWEEPS = 6
VISCOSITIES = (0.2, 0.6, 1.5, 4.0)
WEIGHT = 2.0 / 3.0
MESH = pl.DeviceIdType.MESH
WINDOW = [(dx, dy) for dx in range(-2, 3) for dy in range(-1, 2) if (dx, dy) != (0, 0)]
TOP = 0


def up8(n):
    return -(-n // 8) * 8


def side_slices(step, first, length, lo, hi):
    if step > 0:
        return (first + length - hi, first - hi)
    return (first + lo - 1, first + length + lo - 1)


class Kernel:
    def __init__(self, sizes, comps, grid):
        self.X, self.Y, self.Z = sizes
        self.C = comps
        self.grid = grid
        self.scratch = {}
        self.n_sems = 0
        self.plan()

    def buf(self, name, shape, dtype=jnp.float32):
        self.scratch[name] = pltpu.VMEM(tuple(shape), dtype)

    def halo(self, name, target, comps, px, X, Y, Z, lo, hi, diag, base=0):
        w = hi - lo + 1
        msgs = []
        for dx in (1, -1):
            s, d = side_slices(dx, px, X, lo, hi)
            msgs.append(("x", dx, 0, s, d, self.n_sems))
            self.n_sems += 1
        n = comps * X * w
        self.buf(name + "_sy", (2, up8(n), Z))
        self.buf(name + "_ry", (2, up8(n), Z))
        for k, dy in enumerate((1, -1)):
            s, d = side_slices(dy, TOP, Y, lo, hi)
            d %= Y + 8
            msgs.append(("y", k, dy, s, d, self.n_sems))
            self.n_sems += 1
        if diag:
            n = comps * len(diag)
            self.buf(name + "_sd", (4, n, 1, Z))
            self.buf(name + "_rd", (4, n, 1, Z))
            for k, (dx, dy) in enumerate([(1, 1), (1, -1), (-1, 1), (-1, -1)]):
                cells = [[], []]
                for a, b in diag:
                    sx, tx = side_slices(dx, px, X, a, a)
                    sy, ty = side_slices(dy, TOP, Y, b, b)
                    cells[0].append((sx, sy))
                    cells[1].append((tx, ty % (Y + 8)))
                msgs.append(("d", k, (dx, dy), cells[0], cells[1], self.n_sems))
                self.n_sems += 1
        return dict(name=name, base=base, target=target, comps=comps, px=px, X=X, Y=Y, w=w, diag=diag, msgs=msgs)

    def ring(self, name, source, px, X, Y, Z, w):
        C = self.C
        dirs = [(dx, dy) for dx in (0, 1, -1) for dy in (0, 1, -1) if (dx, dy) != (0, 0)]
        msgs = []
        for dx, dy in dirs:
            px_count, rows = (w if dx else X), (w if dy else Y)
            key = "%s_%d%d" % (name, dx + 1, dy + 1)
            n = up8(C * px_count * rows)
            self.buf(key + "_s", (n, Z))
            self.buf(key + "_r", (n, Z))
            out = (px + (X if dx > 0 else -w if dx < 0 else 0), Y if dy > 0 else -w if dy < 0 else 0)
            into = (X - w if dx < 0 else 0, Y - w if dy < 0 else 0)
            msgs.append((key, dx, dy, px_count, rows, out, into, self.n_sems))
            self.n_sems += 1
        return dict(source=source, msgs=msgs)

    def plan(self):
        X, Y, Z, C = self.X, self.Y, self.Z, self.C
        self.P0, self.R0 = X + 4, Y + 8
        self.X1, self.Y1, self.Z1 = X // 2, Y // 2, Z // 2
        self.P1, self.R1 = self.X1 + 6, self.Y1 + 8
        self.X2, self.Y2, self.Z2 = X // 4, Y // 4, Z // 4
        self.P2, self.R2 = self.X2 + 8, up8(self.Y2 * 3)
        b = self.buf
        b("ph", (X, Y, Z), jnp.int32)
        b("E0", (1, self.P0, self.R0, Z))
        b("C0", (8, self.P0, self.R0, Z))
        for n in ("F0", "A0", "V0", "B0"):
            b(n, (C, self.P0, self.R0, Z))
        b("O0", (C, X, Y, Z))
        b("T0", (C * (self.X1 + 2) * self.R0, Z))
        b("E1", (1, self.P1, self.R1, self.Z1))
        b("C1", (8, self.P1, self.R1, self.Z1))
        for n in ("F1", "G1", "A1", "V1", "B1"):
            b(n, (C, self.P1, self.R1, self.Z1))
        b("T1", (C * (self.X2 + 4) * self.R1, self.Z1))
        b("E2", (1, self.P2, self.R2, self.Z2))
        b("C2", (8, self.P2, self.R2, self.Z2))
        for n in ("F2", "A2", "B2"):
            b(n, (C, self.P2, self.R2, self.Z2))
        blk = self.X2 * self.Y2
        for n, c in (("e2", 1), ("f2", C), ("v2", C)):
            b("S" + n, (c * blk, self.Z2))
            b("R" + n, (len(WINDOW), c * blk, self.Z2))
        b("Q2", (C, self.X2 + 4, self.R1 // 2, self.Z2))
        b("UZ1", (self.R2 * C * (self.X2 + 4), self.Z1))
        b("UZ0", (self.R1 * C * (self.X1 + 2), self.Z))
        reach = [(1, 1), (1, 2), (2, 1), (1, 3), (2, 2), (3, 1)]
        self.hE0 = self.halo("hE0", "E0", 1, 2, X, Y, Z, 1, 2, [(1, 1)])
        self.hF0 = [self.halo("hFc%d" % c, "F0", 1, 2, X, Y, Z, 1, 1, [], c) for c in range(C)]
        self.hV0 = [self.halo("hVc%d" % c, "V0", 1, 2, X, Y, Z, 1, 2, [(1, 1)], c) for c in range(C)]
        self.hE1 = self.halo("hE1", "E1", 1, 3, self.X1, self.Y1, self.Z1, 1, 3, reach)
        self.hF1 = self.halo("hF1", "F1", C, 3, self.X1, self.Y1, self.Z1, 1, 2, reach[:3])
        self.hV1 = self.halo("hV1", "V1", C, 3, self.X1, self.Y1, self.Z1, 2, 3, reach[1:])
        self.aG1 = self.ring("aG1", "G1", 3, self.X1, self.Y1, self.Z1, 1)
        self.aQ2 = self.ring("aQ2", "Q2", 2, self.X2, self.Y2, self.Z2, 2)
        self.win = {}
        for n in ("e2", "f2", "v2"):
            self.win[n] = self.n_sems
            self.n_sems += len(WINDOW)

    def exists(self, dx, dy):
        ok = None
        for step, me, size in ((dx, self.gx, self.grid[0]), (dy, self.gy, self.grid[1])):
            if step:
                t = (me + step >= 0) & (me + step < size)
                ok = t if ok is None else ok & t
        return ok

    def copy(self, src, dst, sem, dx, dy):
        return pltpu.make_async_remote_copy(
            src_ref=src, dst_ref=dst, send_sem=self.ssem.at[sem], recv_sem=self.rsem.at[sem],
            device_id=(self.gx + dx, self.gy + dy), device_id_type=MESH)

    def halo_copies(self, h, kinds="xyd"):
        r = self.r
        ref = r[h["target"]]
        rows = pl.ds(TOP, h["Y"])
        out = []
        for m in h["msgs"]:
            if m[0] not in kinds:
                continue
            if m[0] == "x":
                _, dx, dy, s, d, sem = m
                comps = pl.ds(h["base"], h["comps"])
                c = self.copy(ref.at[comps, pl.ds(s, h["w"]), rows, :], ref.at[comps, pl.ds(d, h["w"]), rows, :],
                              sem, dx, 0)
                out.append((c, dx, 0))
            elif m[0] == "y":
                _, k, dy, s, d, sem = m
                out.append((self.copy(r[h["name"] + "_sy"].at[k], r[h["name"] + "_ry"].at[k], sem, 0, dy), 0, dy))
            else:
                _, k, (dx, dy), _, _, sem = m
                out.append((self.copy(r[h["name"] + "_sd"].at[k], r[h["name"] + "_rd"].at[k], sem, dx, dy), dx, dy))
        return out

    def rows_of(self, h, m, which):
        if m[0] == "y":
            start = m[3 + which]
            return m[1], "y", [(c + h["base"], h["px"] + p, start + q) for c in range(h["comps"])
                               for p in range(h["X"]) for q in range(h["w"])]
        return m[1], "d", [(c + h["base"], p, q) for c in range(h["comps"]) for p, q in m[3 + which]]

    def halo_start(self, h, kinds="xyd"):
        ref = self.r[h["target"]]
        for m in h["msgs"]:
            if m[0] == "x" or m[0] not in kinds:
                continue
            k, kind, rows = self.rows_of(h, m, 0)
            stage = self.r[h["name"] + "_s" + kind]
            for i, (c, p, q) in enumerate(rows):
                row = ref[c, p, q:q + 1, :]
                if kind == "d":
                    stage[k, i] = row
                else:
                    stage[k, i:i + 1, :] = row
        for c, dx, dy in self.halo_copies(h, kinds):
            pl.when(self.exists(dx, dy))(c.start)

    def halo_wait(self, h, kinds="xyd"):
        ref = self.r[h["target"]]
        for c, dx, dy in self.halo_copies(h, kinds):
            pl.when(self.exists(-dx, -dy))(c.wait_recv)
        for m in h["msgs"]:
            if m[0] == "x" or m[0] not in kinds:
                continue
            k, kind, rows = self.rows_of(h, m, 1)
            stage = self.r[h["name"] + "_r" + kind]
            for i, (c, p, q) in enumerate(rows):
                ref[c, p, q:q + 1, :] = stage[k, i] if kind == "d" else stage[k, i:i + 1, :]

    def halo_sent(self, h):
        for c, dx, dy in self.halo_copies(h):
            pl.when(self.exists(dx, dy))(c.wait_send)

    def ring_copies(self, h):
        r = self.r
        return [(self.copy(r[m[0] + "_s"], r[m[0] + "_r"], m[7], m[1], m[2]), m[1], m[2]) for m in h["msgs"]]

    def ring_start(self, h):
        S = self.r[h["source"]]
        for key, dx, dy, planes, rows, (p, q), _, _ in h["msgs"]:
            q %= S.shape[2]
            i = 0
            for c in range(self.C):
                for k in range(planes):
                    self.r[key + "_s"][i:i + rows, :] = S[c, p + k, q:q + rows, :]
                    i += rows
        for c, dx, dy in self.ring_copies(h):
            pl.when(self.exists(dx, dy))(c.start)

    def ring_wait(self, h):
        for c, dx, dy in self.ring_copies(h):
            pl.when(self.exists(-dx, -dy))(c.wait_recv)

    def ring_add(self, h, place):
        for key, dx, dy, planes, rows, _, (p, q), _ in h["msgs"]:
            i = 0
            for c in range(self.C):
                for k in range(planes):
                    ref, idx = place(c, p + k, q, rows)
                    ref[idx] = ref[idx] + self.r[key + "_r"][i:i + rows, :]
                    i += rows

    def ring_sent(self, h):
        for c, dx, dy in self.ring_copies(h):
            pl.when(self.exists(dx, dy))(c.wait_send)

    def win_copies(self, n):
        src, dst = self.r["S" + n], self.r["R" + n]
        return [(self.copy(src, dst.at[k], self.win[n] + k, dx, dy), dx, dy) for k, (dx, dy) in enumerate(WINDOW)]

    def win_start(self, n):
        for c, dx, dy in self.win_copies(n):
            pl.when(self.exists(dx, dy))(c.start)

    def win_wait(self, n, target):
        copies = self.win_copies(n)
        for c, dx, dy in copies:
            pl.when(self.exists(-dx, -dy))(c.wait_recv)
        ref = self.r[target]
        X2, Y2 = self.X2, self.Y2
        for k, (dx, dy) in enumerate(WINDOW + [(0, 0)]):
            for c in range(ref.shape[0]):
                for p in range(X2):
                    i = (c * X2 + p) * Y2
                    if (dx, dy) == (0, 0):
                        v = self.r["S" + n][i:i + Y2, :]
                    else:
                        v = self.r["R" + n][k, i:i + Y2, :]
                    ref[c, 4 + p - dx * X2, Y2 * (1 - dy):Y2 * (2 - dy), :] = v

    def win_sent(self, n):
        for c, dx, dy in self.win_copies(n):
            pl.when(self.exists(dx, dy))(c.wait_send)

    def coefs(self, E, K, a, b, scale):
        E, K = self.r[E], self.r[K]
        Z = E.shape[-1]
        shape = E.shape[-2:]
        R = shape[0]
        s = 1.0 / scale

        @pl.loop(a, b)
        def _(i):
            z = lax.broadcasted_iota(jnp.int32, shape, 1)
            e = E[0, i]

            def face(o):
                t = e + o
                return jnp.where(jnp.minimum(e, o) > 0.0, t * (0.5 * s), t * s)

            zp = jnp.where(z == Z - 1, 0.0, pltpu.roll(e, Z - 1, 1))
            zm = jnp.where(z == 0, 0.0, pltpu.roll(e, 1, 1))
            others = (E[0, i + 1], E[0, i - 1], pltpu.roll(e, R - 1, 0), pltpu.roll(e, 1, 0), zp, zm)
            diag = None
            for k, o in enumerate(others):
                c = face(o)
                diag = c if diag is None else diag + c
                if k == 4:
                    c = jnp.where(z == Z - 1, 0.0, c)
                if k == 5:
                    c = jnp.where(z == 0, 0.0, c)
                K[k, i] = c
            inside = e > 0.0
            K[6, i] = jnp.where(inside, WEIGHT / jnp.where(inside, diag, 1.0), 0.0)
            K[7, i] = diag

    def face(self, E, K, i, o, k, scale):
        e, f = self.r[E][0, i], self.r[E][0, o]
        t, s = e + f, 1.0 / scale
        self.r[K][k, i] = jnp.where(jnp.minimum(e, f) > 0.0, t * (0.5 * s), t * s)

    def stencil(self, V, K, G, i, c, rows):
        R, Z = V.shape[-2:]
        n = rows.stop - rows.start
        v = V[c, i, rows, :]
        if n == R:
            yp, ym = pltpu.roll(v, R - 1, 0), pltpu.roll(v, 1, 0)
        else:
            yp, ym = V[c, i, 1:n + 1, :], pltpu.roll(V[c, i], 1, 0)[:n]
        acc = G[c, i, rows, :]
        parts = (V[c, i + 1, rows, :], V[c, i - 1, rows, :], yp, ym, pltpu.roll(v, Z - 1, 1), pltpu.roll(v, 1, 1))
        for k, o in enumerate(parts):
            acc = acc + K[k, i, rows, :] * o
        return v, acc

    def first(self, K, G, O, a, b, comps=None):
        K, G, O = (self.r[n] for n in (K, G, O))

        @pl.loop(a, b)
        def _(i):
            w = K[6, i]
            for c in comps or range(self.C):
                O[c, i] = w * G[c, i]

    def sweep(self, V, K, G, O, a, b, rows=None, shift=0, comps=None):
        V, K, G, O = (self.r[n] for n in (V, K, G, O))
        rows = rows or slice(0, V.shape[-2])
        out_rows = rows if shift == 0 else slice(0, rows.stop - rows.start)

        @pl.loop(a, b)
        def _(i):
            for c in comps or range(self.C):
                v, acc = self.stencil(V, K, G, i, c, rows)
                O[c, i - shift, out_rows, :] = (1.0 - WEIGHT) * v + K[6, i, rows, :] * acc

    def residual(self, V, K, G, T, px, Xc, ring):
        V, K, G, T = (self.r[n] for n in (V, K, G, T))
        R = V.shape[-2]
        rows = slice(0, R)
        n = Xc + 2 * ring

        def defect(i, c):
            v, acc = self.stencil(V, K, G, i, c, rows)
            return acc - K[7, i] * v

        @pl.loop(-(ring - 1), Xc + ring - 1)
        def _(j):
            for c in range(self.C):
                i = px + 2 * j
                start = pl.multiple_of((c * n + j + ring) * R, 8)
                T[pl.ds(start, R), :] = 0.5 * (defect(i, c) + defect(i + 1, c))

        last = px + 2 * Xc + 2 * ring - 2
        for c in range(self.C):
            for near, far, k, j in ((px - 2 * ring + 1, px - 2 * ring, 0, 0), (last, last + 1, 1, n - 1)):
                start = (c * n + j) * R
                if ring == 1:
                    step = 1 if k == 0 else -1
                    v = V[c, near]
                    acc = K[k, near] * V[c, near + step] - K[7, near] * v + K[k, far] * v
                    for f, o in ((2, pltpu.roll(v, R - 1, 0)), (3, pltpu.roll(v, 1, 0)),
                                 (4, pltpu.roll(v, v.shape[1] - 1, 1)), (5, pltpu.roll(v, 1, 1))):
                        acc = acc + K[f, near] * o
                else:
                    acc = K[k, near] * V[c, near + (1 if k == 0 else -1)]
                T[start:start + R, :] = 0.5 * acc

    def spread(self, V, K, G, i, o, k):
        V, K, O = (self.r[n] for n in (V, K, G))
        for c in range(self.C):
            O[c, i] = K[6, i] * (K[k, i] * V[c, o])

    def dot(self, a, b):
        return lax.dot_general(a, b, (((1,), (0,)), ((), ())), preferred_element_type=jnp.float32)

    def split(self, t):
        hi = t.astype(jnp.bfloat16)
        return hi, (t - hi.astype(jnp.float32)).astype(jnp.bfloat16)

    def right(self, t, m):
        hi, lo = self.split(t)
        return self.dot(hi, m) + self.dot(lo, m)

    def left(self, m, t):
        hi, lo = self.split(t)
        return self.dot(m, hi) + self.dot(m, lo)

    def pairs(self, n, m, value, fine_dim):
        r = lax.broadcasted_iota(jnp.int32, (n, m), 0)
        c = lax.broadcasted_iota(jnp.int32, (n, m), 1)
        hit = (r >> 1) == c if fine_dim == 0 else (c >> 1) == r
        return jnp.where(hit, value, 0.0).astype(jnp.bfloat16)

    def squeeze(self, t):
        rows, Z = t.shape
        half = self.right(t, self.pairs(Z, Z // 2, 0.5, 0))
        return self.left(self.pairs(rows // 2, rows, 0.5, 1), half)

    def squeeze0(self, n):
        T, Z, R, R1, Y1 = self.r["T0"], self.Z, self.R0, self.R1, self.Y1
        half = self.right(T[...], self.pairs(Z, Z // 2, 0.5, 0))
        o = lax.broadcasted_iota(jnp.int32, (n * R1, n * R), 0)
        f = lax.broadcasted_iota(jnp.int32, (n * R1, n * R), 1)
        bo, bf = jnp.zeros_like(o), jnp.zeros_like(f)
        for k in range(1, n):
            bo = bo + (o >= k * R1).astype(jnp.int32)
            bf = bf + (f >= k * R).astype(jnp.int32)
        q = o - bo * R1
        q = jnp.where(q <= Y1, q, jnp.where(q == R1 - 1, R // 2 - 1, -1))
        m = jnp.where((bo == bf) & (((f - bf * R) >> 1) == q), 0.5, 0.0).astype(jnp.bfloat16)
        return [self.left(m, half[c * n * R:(c + 1) * n * R]) for c in range(self.C)]

    def prolong(self, W, a, count, U, V, planes, coarse_of, offset):
        W, U, V = (self.r[n] for n in (W, U, V))
        C, _, Rc, Zc = W.shape
        Rf, Zf = V.shape[-2:]
        src = W[:, a:a + count].reshape(C * count * Rc, Zc)
        U[...] = self.right(src, self.pairs(Zc, Zf, 1.0, 1))
        r = lax.broadcasted_iota(jnp.int32, (Rf, Rc), 0)
        c = lax.broadcasted_iota(jnp.int32, (Rf, Rc), 1)
        r = jnp.where(r < Rf - 4, r, r - Rf)
        c = c - offset if offset else jnp.where(c < Rc - 4, c, c - Rc)
        lift = jnp.where((r >> 1) == c, 1.0, 0.0).astype(jnp.bfloat16)
        for comp in range(C):
            for k in range(count):
                start = (comp * count + k) * Rc
                block = self.left(lift, U[start:start + Rc, :])
                for p in planes:
                    if coarse_of(p) == a + k:
                        V[comp, p] = V[comp, p] + block

    def body(self, forcing, phase, out, *scratch):
        names = list(self.scratch)
        self.r = r = dict(zip(names, scratch))
        self.ssem, self.rsem, lsem = scratch[len(names):]
        self.gx, self.gy = lax.axis_index("gx"), lax.axis_index("gy")
        X, Y, Z, C = self.X, self.Y, self.Z, self.C
        X1, Y1 = self.X1, self.Y1
        block = (pl.ds(2, X), pl.ds(TOP, Y))
        load_p = pltpu.make_async_copy(phase, r["ph"], lsem.at[0])
        load_p.start()
        for n in ("F0", "V0"):
            ref = r[n]
            for c in range(C):
                for p in (0, 1, X + 2, X + 3):
                    ref[c, p, 0:Y, :] = jnp.zeros((Y, Z), jnp.float32)

                @pl.loop(0, self.P0)
                def _(i):
                    ref[c, i, Y:self.R0, :] = jnp.zeros((self.R0 - Y, Z), jnp.float32)
        for n, planes in (("A0", (1, X + 2)), ("A1", (0, X1 + 5)), ("B1", (0, X1 + 5))):
            for c in range(C):
                for p in planes:
                    r[n][c, p] = jnp.zeros(r[n].shape[2:], jnp.float32)
        for n in ("E0", "E1", "F1", "G1", "V1", "E2", "F2", "A2"):
            ref = r[n]
            for c in range(ref.shape[0]):
                @pl.loop(0, ref.shape[1])
                def _(i):
                    ref[c, i] = jnp.zeros(ref.shape[2:], jnp.float32)
        for n in list(r):
            if n.startswith("h") and n[-3:] in ("_ry", "_rd") or n in ("Re2", "Rf2", "Rv2"):
                ref = r[n]
                for k in range(ref.shape[0]):
                    ref[k] = jnp.zeros(ref.shape[1:], jnp.float32)
            if n.startswith("a") and n.endswith("_r"):
                r[n][...] = jnp.zeros(r[n].shape, jnp.float32)
        load_f = pltpu.make_async_copy(forcing, r["F0"].at[:, block[0], block[1], :], lsem.at[1])
        load_f.start()

        barrier = pltpu.get_barrier_semaphore()
        count = jnp.int32(0)
        for dx, dy in WINDOW:
            ok = self.exists(dx, dy)
            count = count + ok.astype(jnp.int32)

            @pl.when(ok)
            def _():
                pl.semaphore_signal(barrier, inc=1, device_id=(self.gx + dx, self.gy + dy), device_id_type=MESH)
        load_p.wait()

        @pl.loop(0, X)
        def _(i):
            ph = r["ph"][i]
            e = jnp.zeros(ph.shape, jnp.float32)
            for k, value in enumerate(VISCOSITIES):
                e = jnp.where(ph == k, jnp.float32(value), e)
            r["E0"][0, i + 2, TOP:TOP + Y, :] = e
        pl.semaphore_wait(barrier, count)
        self.halo_start(self.hE0)
        load_f.wait()
        for h in self.hF0:
            self.halo_start(h)

        for j in range(X1):
            r["T0"][j * Y:(j + 1) * Y, :] = 0.5 * (
                r["E0"][0, 2 + 2 * j, TOP:TOP + Y, :] + r["E0"][0, 3 + 2 * j, TOP:TOP + Y, :])
        e1 = self.squeeze(r["T0"][0:X1 * Y, :])
        for j in range(X1):
            r["E1"][0, 3 + j, TOP:TOP + Y1, :] = e1[j * Y1:(j + 1) * Y1]
        for j in range(self.X2):
            r["T1"][j * Y1:(j + 1) * Y1, :] = 0.5 * (
                e1[2 * j * Y1:(2 * j + 1) * Y1] + e1[(2 * j + 1) * Y1:(2 * j + 2) * Y1])
        r["Se2"][...] = self.squeeze(r["T1"][0:self.X2 * Y1, :])

        self.halo_start(self.hE1)
        self.win_start("e2")
        X2, Y2, R1 = self.X2, self.Y2, self.R1
        self.halo_wait(self.hE0, "y")
        self.coefs("E0", "C0", 3, X + 1, 1.0)
        self.first("C0", "F0", "A0", 3, X + 1)
        self.sweep("A0", "C0", "F0", "V0", 4, X)
        self.halo_wait(self.hE0, "xd")
        self.coefs("E0", "C0", 1, 3, 1.0)
        self.coefs("E0", "C0", X + 1, X + 3, 1.0)
        self.face("E0", "C0", 0, 1, 0, 1.0)
        self.face("E0", "C0", X + 3, X + 2, 1, 1.0)
        self.first("C0", "F0", "A0", 2, 3)
        self.first("C0", "F0", "A0", X + 1, X + 2)
        self.sweep("A0", "C0", "F0", "V0", 2, 4)
        self.sweep("A0", "C0", "F0", "V0", X, X + 2)
        self.spread("A0", "C0", "V0", 1, 2, 0)
        self.spread("A0", "C0", "V0", X + 2, X + 1, 1)
        self.residual("V0", "C0", "F0", "T0", 2, X1, 1)
        for c, f1 in enumerate(self.squeeze0(X1 + 2)):
            for j in range(X1 + 2):
                r["G1"][c, 2 + j] = f1[j * R1:(j + 1) * R1]
        self.ring_start(self.aG1)

        self.halo_wait(self.hE1)
        self.coefs("E1", "C1", 1, X1 + 5, 4.0)
        self.face("E1", "C1", 0, 1, 0, 4.0)
        self.face("E1", "C1", X1 + 5, X1 + 4, 1, 4.0)
        self.first("C1", "G1", "A1", 1, X1 + 5)
        self.sweep("A1", "C1", "G1", "B1", 1, X1 + 5)
        self.residual("B1", "C1", "G1", "T1", 3, X2, 2)
        f2 = self.squeeze(r["T1"][...])
        n = self.R1 // 2
        for c in range(C):
            for j in range(X2 + 4):
                s = (c * (X2 + 4) + j) * n
                r["Q2"][c, j] = f2[s:s + n]
        self.ring_start(self.aQ2)

        self.ring_wait(self.aG1)
        for c in range(C):
            for j in range(X1):
                r["F1"][c, 3 + j, 0:Y1, :] = r["G1"][c, 3 + j, 0:Y1, :]
        self.ring_add(self.aG1, lambda c, p, q, k: (r["F1"], (c, 3 + p, slice(q, q + k))))
        self.halo_start(self.hF1)

        for h in self.hF0:
            self.halo_wait(h)
        rows0 = slice(TOP, TOP + Y)
        self.first("C0", "F0", "A0", 1, X + 3)
        self.sweep("A0", "C0", "F0", "V0", 2, X + 2, rows0)

        self.ring_wait(self.aQ2)
        for c in range(C):
            for p in range(X2):
                i = (c * X2 + p) * Y2
                r["Sf2"][i:i + Y2, :] = r["Q2"][c, 2 + p, 0:Y2, :]

        def place(c, p, q, k):
            i = (c * X2 + p) * Y2 + q
            return r["Sf2"], (slice(i, i + k),)

        self.ring_add(self.aQ2, place)
        self.win_start("f2")
        self.halo_start(self.hV0[0])

        self.halo_wait(self.hF1)
        self.first("C1", "F1", "A1", 1, X1 + 5)
        self.sweep("A1", "C1", "F1", "B1", 2, X1 + 4)
        for c in range(C):
            for j in range(X1):
                r["V1"][c, 3 + j, TOP:TOP + Y1, :] = r["B1"][c, 3 + j, TOP:TOP + Y1, :]
            for dx in (2, X1 + 3):
                r["V1"][c, dx, 0:Y1, :] = r["B1"][c, dx, 0:Y1, :]
            for j in range(-1, X1 + 1):
                for q in (self.R1 - 1, Y1):
                    r["V1"][c, 3 + j, q:q + 1, :] = r["B1"][c, 3 + j, q:q + 1, :]
        self.halo_start(self.hV1)

        self.win_wait("e2", "E2")
        self.coefs("E2", "C2", 1, self.X2 + 7, 16.0)
        self.win_wait("f2", "F2")
        p2 = self.P2
        self.first("C2", "F2", "A2", 1, p2 - 1)
        self.sweep("A2", "C2", "F2", "B2", 2, p2 - 2)
        self.sweep("B2", "C2", "F2", "A2", 3, p2 - 3)
        self.sweep("A2", "C2", "F2", "B2", 4, p2 - 4)
        for c in range(C):
            for p in range(self.X2):
                i = (c * self.X2 + p) * self.Y2
                r["Sv2"][i:i + self.Y2, :] = r["B2"][c, 4 + p, self.Y2:2 * self.Y2, :]
        self.win_start("v2")
        for h in self.hV0[1:]:
            self.halo_start(h)
        self.win_wait("v2", "A2")
        self.sweep("A2", "C2", "F2", "B2", 1, p2 - 1)
        self.sweep("B2", "C2", "F2", "A2", 2, p2 - 2)

        self.halo_wait(self.hV1)
        self.halo_sent(self.hV1)
        self.prolong("A2", 2, self.X2 + 4, "UZ1", "V1", range(self.P1),
                     lambda p: 4 + (p - 3) // 2, self.Y2)
        self.sweep("V1", "C1", "F1", "A1", 1, X1 + 5)
        self.sweep("A1", "C1", "F1", "B1", 2, X1 + 4)

        for h in self.hV0:
            self.halo_wait(h)
            self.halo_sent(h)
        self.prolong("B1", 2, X1 + 2, "UZ0", "V0", range(self.P0),
                     lambda p: 3 + (p - 2) // 2, 0)
        self.sweep("V0", "C0", "F0", "B0", 1, X + 3)
        self.sweep("B0", "C0", "F0", "O0", 2, X + 2, rows0, shift=2)
        store = pltpu.make_async_copy(r["O0"], out, lsem.at[0])
        store.start()
        for h in (self.hE0, *self.hF0, self.hE1, self.hF1):
            self.halo_sent(h)
        for h in (self.aG1, self.aQ2):
            self.ring_sent(h)
        for n in ("e2", "f2", "v2"):
            self.win_sent(n)
        store.wait()

    def __call__(self, forcing, phase):
        any_space = pl.BlockSpec(memory_space=pl.ANY)
        sems = [pltpu.SemaphoreType.DMA((self.n_sems,)), pltpu.SemaphoreType.DMA((self.n_sems,)),
                pltpu.SemaphoreType.DMA((2,))]
        return pl.pallas_call(
            self.body,
            out_shape=jax.ShapeDtypeStruct(forcing.shape, jnp.float32),
            in_specs=[any_space, any_space],
            out_specs=any_space,
            scratch_shapes=list(self.scratch.values()) + sems,
            compiler_params=pltpu.CompilerParams(
                collective_id=0, has_side_effects=True, vmem_limit_bytes=60 * 1024 * 1024),
            name="vcycle",
        )(forcing, phase)


def solution(mesh):
    grid = (mesh.shape["gx"], mesh.shape["gy"])

    def per_device(forcing, phase_ids):
        return Kernel(phase_ids.shape, forcing.shape[0], grid)(forcing, phase_ids)

    return jax.shard_map(
        per_device,
        mesh=mesh,
        in_specs=(P(None, "gx", "gy", None), P("gx", "gy", None)),
        out_specs=P(None, "gx", "gy", None),
        check_vma=False,
    )
```

```python
import functools

import jax
import jax.numpy as jnp
from jax import lax
from jax.experimental import pallas as pl
from jax.experimental.pallas import tpu as pltpu
from jax.sharding import PartitionSpec as P

COARSE_SWEEPS = 6
VISCOSITIES = (0.2, 0.6, 1.5, 4.0)
WEIGHT = 2.0 / 3.0
MESH = pl.DeviceIdType.MESH
WINDOW = [(dx, dy) for dx in (-2, 0, 2) for dy in (-1, 0, 1) if (dx, dy) != (0, 0)]
MEMBERS = [(dx, t, dy) for dx in (-2, 0, 2) for t in (0, 1) for dy in (-1, 0, 1) if (dx, t, dy) != (0, 0, 0)]
ROWS = (0, 1, -1)
TOP = 0


def up8(n):
    return -(-n // 8) * 8


def side_slices(step, first, length, lo, hi):
    if step > 0:
        return (first + length - hi, first - hi)
    return (first + lo - 1, first + length + lo - 1)


class Kernel:
    def __init__(self, sizes, comps, grid):
        self.X, self.Y, self.Z = sizes
        self.C = comps
        self.grid = grid
        self.scratch = {}
        self.n_sems = 0
        self.plan()

    def buf(self, name, shape, dtype=jnp.float32):
        self.scratch[name] = pltpu.VMEM(tuple(shape), dtype)

    def halo(self, name, target, comps, px, X, Y, Z, lo, hi, diag, base=0, land=None, only="xyd"):
        w = hi - lo + 1
        msgs = []
        for dx in (1, -1) if "x" in only else ():
            s, d = side_slices(dx, px, X, lo, hi)
            msgs.append(("x", dx, 0, s, d, self.n_sems))
            self.n_sems += 1
        n = comps * X * w
        if "y" in only:
            self.buf(name + "_sy", (2, up8(n), Z))
            self.buf(name + "_ry", (2, up8(n), Z))
        for k, dy in enumerate((1, -1)) if "y" in only else ():
            s, d = side_slices(dy, TOP, Y, lo, hi)
            d %= Y + 8
            msgs.append(("y", k, dy, s, d, self.n_sems))
            self.n_sems += 1
        if diag:
            n = comps * len(diag)
            self.buf(name + "_sd", (4, n, 1, Z))
            self.buf(name + "_rd", (4, n, 1, Z))
            for k, (dx, dy) in enumerate([(1, 1), (1, -1), (-1, 1), (-1, -1)]):
                cells = [[], []]
                for a, b in diag:
                    sx, tx = side_slices(dx, px, X, a, a)
                    sy, ty = side_slices(dy, TOP, Y, b, b)
                    cells[0].append((sx, sy))
                    cells[1].append((tx, ty % (Y + 8)))
                msgs.append(("d", k, (dx, dy), cells[0], cells[1], self.n_sems))
                self.n_sems += 1
        if land:
            self.buf(name + "_lx", (2, comps, w, Y, Z))
        return dict(name=name, land=land, base=base, target=target, comps=comps, px=px, X=X, Y=Y, w=w, diag=diag, msgs=msgs)

    def ring(self, name, source, px, X, Y, Z, w):
        C = self.C
        dirs = [(dx, dy) for dx in (0, 1, -1) for dy in (0, 1, -1) if (dx, dy) != (0, 0)]
        msgs = []
        for dx, dy in dirs:
            px_count, rows = (w if dx else X), (w if dy else Y)
            key = "%s_%d%d" % (name, dx + 1, dy + 1)
            n = up8(C * px_count * rows)
            self.buf(key + "_s", (n, Z))
            self.buf(key + "_r", (n, Z))
            out = (px + (X if dx > 0 else -w if dx < 0 else 0), Y if dy > 0 else -w if dy < 0 else 0)
            into = (X - w if dx < 0 else 0, Y - w if dy < 0 else 0)
            msgs.append((key, dx, dy, px_count, rows, out, into, self.n_sems))
            self.n_sems += 1
        return dict(source=source, msgs=msgs)

    def plan(self):
        X, Y, Z, C = self.X, self.Y, self.Z, self.C
        self.P0, self.R0 = X + 4, Y + 8
        self.X1, self.Y1, self.Z1 = X // 2, Y // 2, Z // 2
        self.P1, self.R1 = self.X1 + 6, self.Y1 + 8
        self.X2, self.Y2, self.Z2 = X // 4, Y // 4, Z // 4
        self.P2, self.R2 = 2 * self.X2 + 8, up8(self.Y2 * 3)
        b = self.buf
        b("ph", (X, Y, Z), jnp.int32)
        b("E0", (1, self.P0, self.R0, Z))
        b("C0", (8, self.P0, self.R0, Z))
        for n in ("F0", "A0", "V0", "B0"):
            b(n, (C, self.P0, self.R0, Z))
        b("T0", (C * (self.X1 + 2) * self.R0, Z))
        b("E1", (1, self.P1, self.R1, self.Z1))
        b("C1", (8, self.P1, self.R1, self.Z1))
        for n in ("F1", "G1", "A1", "V1", "B1"):
            b(n, (C, self.P1, self.R1, self.Z1))
        b("T1", (C * (self.X2 + 4) * self.R1, self.Z1))
        b("E2", (1, self.P2, self.R2, self.Z2))
        b("C2", (8, self.P2, self.R2, self.Z2))
        for n in ("F2", "A2", "B2"):
            b(n, (C, self.P2, self.R2, self.Z2))
        blk = self.X2 * self.Y2
        b("Se2", (blk, self.Z2))
        b("Re2", (len(MEMBERS), blk, self.Z2))
        for n in ("f2", "v2"):
            b("S" + n, (2 * C * blk, self.Z2))
            b("R" + n, (len(WINDOW), 2 * C * blk, self.Z2))
        near, far = up8(C * (self.X2 + 2) * self.Y2), up8(C * 2 * self.Y2)
        b("Sn2", (3, near, self.Z2))
        b("Rn2", (6, near, self.Z2))
        b("Sd2", (3, far, self.Z2))
        b("Rd2", (6, far, self.Z2))
        b("W2", (C, 2 * self.X2, 8, self.Z2))
        b("Q2", (C, self.X2 + 4, self.R1 // 2, self.Z2))
        b("UZ1", (self.R2 * C * (self.X2 + 4), self.Z1))
        b("UZ0", (self.R1 * C * (self.X1 + 2), self.Z))
        reach = [(1, 1), (1, 2), (2, 1), (1, 3), (2, 2), (3, 1)]
        self.hE0 = self.halo("hE0", "E0", 1, 2, X, Y, Z, 1, 2, [(1, 1)], only="yd")
        self.hE0x = [self.halo("hE0x%d" % k, "E0", 1, 2, X, Y, Z, k, k, [], only="x") for k in (1, 2)]
        self.hF0 = [self.halo("hFc%d" % c, "F0", 1, 2, X, Y, Z, 1, 1, [], c) for c in range(C)]
        self.hV0 = [self.halo("hVc%d" % c, "V0", 1, 2, X, Y, Z, 1, 2, [(1, 1)], c, "B0") for c in range(C)]
        self.hE1 = self.halo("hE1", "E1", 1, 3, self.X1, self.Y1, self.Z1, 1, 3, reach)
        self.hF1 = self.halo("hF1", "F1", C, 3, self.X1, self.Y1, self.Z1, 1, 2, reach[:3])
        self.hV1 = self.halo("hV1", "V1", C, 3, self.X1, self.Y1, self.Z1, 2, 3, reach[1:])
        self.aG1 = self.ring("aG1", "G1", 3, self.X1, self.Y1, self.Z1, 1)
        self.win = {}
        for n, k in (("e2", len(MEMBERS)), ("f2", len(WINDOW)), ("v2", len(WINDOW)), ("n2", 6), ("d2", 6)):
            self.win[n] = self.n_sems
            self.n_sems += k

    def exists(self, dx, dy):
        ok = None
        for step, me, size in ((dx, self.gx, self.grid[0]), (dy, self.gy, self.grid[1])):
            if step:
                t = (me + step >= 0) & (me + step < size)
                ok = t if ok is None else ok & t
        return ok

    def copy(self, src, dst, sem, dx, dy, into=None):
        into = sem if into is None else into
        return pltpu.make_async_remote_copy(
            src_ref=src, dst_ref=dst, send_sem=self.ssem.at[sem], recv_sem=self.rsem.at[into],
            device_id=(self.gx + dx, self.gy + dy), device_id_type=MESH)

    def halo_copies(self, h, kinds="xyd"):
        r = self.r
        ref = r[h["target"]]
        rows = pl.ds(TOP, h["Y"])
        out = []
        for m in h["msgs"]:
            if m[0] not in kinds:
                continue
            if m[0] == "x":
                _, dx, dy, s, d, sem = m
                comps = pl.ds(h["base"], h["comps"])
                src, dst = ref, ref.at[comps, pl.ds(d, h["w"]), rows, :]
                if h["land"]:
                    src, dst = r[h["land"]], r[h["name"] + "_lx"].at[0 if dx > 0 else 1]
                c = self.copy(src.at[comps, pl.ds(s, h["w"]), rows, :], dst, sem, dx, 0)
                out.append((c, dx, 0))
            elif m[0] == "y":
                _, k, dy, s, d, sem = m
                out.append((self.copy(r[h["name"] + "_sy"].at[k], r[h["name"] + "_ry"].at[k], sem, 0, dy), 0, dy))
            else:
                _, k, (dx, dy), _, _, sem = m
                out.append((self.copy(r[h["name"] + "_sd"].at[k], r[h["name"] + "_rd"].at[k], sem, dx, dy), dx, dy))
        return out

    def rows_of(self, h, m, which):
        if m[0] == "y":
            start = m[3 + which]
            return m[1], "y", [(c + h["base"], h["px"] + p, start + q) for c in range(h["comps"])
                               for p in range(h["X"]) for q in range(h["w"])]
        return m[1], "d", [(c + h["base"], p, q) for c in range(h["comps"]) for p, q in m[3 + which]]

    def halo_start(self, h, kinds="xyd"):
        ref = self.r[h["target"]]
        for m in h["msgs"]:
            if m[0] == "x" or m[0] not in kinds:
                continue
            k, kind, rows = self.rows_of(h, m, 0)
            stage = self.r[h["name"] + "_s" + kind]
            for i, (c, p, q) in enumerate(rows):
                row = ref[c, p, q:q + 1, :]
                if kind == "d":
                    stage[k, i] = row
                else:
                    stage[k, i:i + 1, :] = row
        for c, dx, dy in self.halo_copies(h, kinds):
            pl.when(self.exists(dx, dy))(c.start)

    def halo_wait(self, h, kinds="xyd"):
        for c, dx, dy in self.halo_copies(h, kinds):
            pl.when(self.exists(-dx, -dy))(c.wait_recv)
        self.halo_place(h, kinds)

    def halo_place(self, h, kinds="xyd"):
        ref = self.r[h["target"]]
        for m in h["msgs"]:
            if m[0] == "x" or m[0] not in kinds:
                continue
            k, kind, rows = self.rows_of(h, m, 1)
            stage = self.r[h["name"] + "_r" + kind]
            for i, (c, p, q) in enumerate(rows):
                ref[c, p, q:q + 1, :] = stage[k, i] if kind == "d" else stage[k, i:i + 1, :]

    def halo_sent(self, h, kinds="xyd"):
        for c, dx, dy in self.halo_copies(h, kinds):
            pl.when(self.exists(dx, dy))(c.wait_send)

    def ring_copies(self, h):
        r = self.r
        return [(self.copy(r[m[0] + "_s"], r[m[0] + "_r"], m[7], m[1], m[2]), m[1], m[2]) for m in h["msgs"]]

    def ring_start(self, h):
        S = self.r[h["source"]]
        for key, dx, dy, planes, rows, (p, q), _, _ in h["msgs"]:
            q %= S.shape[2]
            i = 0
            for c in range(self.C):
                for k in range(planes):
                    self.r[key + "_s"][i:i + rows, :] = S[c, p + k, q:q + rows, :]
                    i += rows
        for c, dx, dy in self.ring_copies(h):
            pl.when(self.exists(dx, dy))(c.start)

    def ring_wait(self, h):
        for c, dx, dy in self.ring_copies(h):
            pl.when(self.exists(-dx, -dy))(c.wait_recv)

    def ring_add(self, h, place):
        for key, dx, dy, planes, rows, _, (p, q), _ in h["msgs"]:
            i = 0
            for c in range(self.C):
                for k in range(planes):
                    ref, idx = place(c, p + k, q, rows)
                    ref[idx] = ref[idx] + self.r[key + "_r"][i:i + rows, :]
                    i += rows

    def ring_sent(self, h):
        for c, dx, dy in self.ring_copies(h):
            pl.when(self.exists(dx, dy))(c.wait_send)

    def when(self, dx, dy, f):
        if (dx, dy) == (0, 0):
            f()
        else:
            pl.when(self.exists(dx, dy))(f)

    def member_copies(self):
        r = self.r
        return [(self.copy(r["Se2"], r["Re2"].at[k], self.win["e2"] + k, dx + t * (1 - 2 * self.m), dy), dx, t, dy)
                for k, (dx, t, dy) in enumerate(MEMBERS)]

    def member_start(self):
        for c, dx, t, dy in self.member_copies():
            self.when(dx, dy, c.start)

    def member_wait(self):
        for c, dx, t, dy in self.member_copies():
            self.when(-dx, -dy, c.wait_recv)
        E, X2, Y2 = self.r["E2"], self.X2, self.Y2
        for k, (dx, t, dy) in enumerate(MEMBERS + [(0, 0, 0)]):
            member = 1 - self.m if t else self.m
            for p in range(X2):
                v = self.r["Se2"][p * Y2:(p + 1) * Y2] if k == len(MEMBERS) else self.r["Re2"][k, p * Y2:(p + 1) * Y2]
                E[0, 4 + p - dx * X2 + member * X2, Y2 * (1 - dy):Y2 * (2 - dy), :] = v

    def member_sent(self):
        for c, dx, t, dy in self.member_copies():
            self.when(dx, dy, c.wait_send)

    def near_copies(self):
        r, b = self.r, self.win["n2"]
        return [(self.copy(r["Sn2"].at[k], r["Rn2"].at[3 * t + k], b + 3 * t + k, t * (1 - 2 * self.m), dy), t, k, dy)
                for t in (1, 0) for k, dy in enumerate(ROWS) if (t, dy) != (0, 0)]

    def far_sends(self):
        r, b, m = self.r, self.win["d2"], self.m
        return [(self.copy(r["Sd2"].at[k], r["Rd2"].at[3 * m + k], b + 3 * t + k, (2 * m - 1) * (2 - t), dy, b + 3 * m + k), dy)
                for t in (1, 0) for k, dy in enumerate(ROWS)]

    def far_recvs(self):
        r, b = self.r, self.win["d2"]
        return [(self.copy(r["Sd2"].at[k], r["Rd2"].at[3 * s + k], b + 3 * s + k, 2, dy), 2 - 4 * s, k, dy)
                for s in (0, 1) for k, dy in enumerate(ROWS)]

    def far_exists(self, dy):
        x = self.gx + 2 * (2 * self.m - 1)
        ok = (x >= 0) & (x < self.grid[0])
        return ok & self.exists(0, dy) if dy else ok

    def share_start(self):
        r, C, X2, Y2 = self.r, self.C, self.X2, self.Y2
        Q = r["Q2"]
        R = Q.shape[2]
        for k, dy in enumerate(ROWS):
            q, n = ((0, Y2), (Y2, 2), (R - 2, 2))[k]
            i = 0
            for c in range(C):
                for p in range(X2 + 2):
                    r["Sn2"][k, i:i + n, :] = Q[c, 2 * (1 - self.m) + p, q:q + n, :]
                    i += n
            i = 0
            for c in range(C):
                for p in range(2):
                    r["Sd2"][k, i:i + n, :] = Q[c, self.m * (X2 + 2) + p, q:q + n, :]
                    i += n
        for c, t, k, dy in self.near_copies():
            self.when(0, dy, c.start)
        for c, dy in self.far_sends():
            pl.when(self.far_exists(dy))(c.start)

    def share_wait(self):
        r, C, X2, Y2 = self.r, self.C, self.X2, self.Y2
        W, Q = r["W2"], r["Q2"]
        for c, t, k, dy in self.near_copies():
            self.when(0, -dy, c.wait_recv)
        for c, dx, k, dy in self.far_recvs():
            self.when(dx, -dy, c.wait_recv)
        W[...] = jnp.zeros(W.shape, jnp.float32)
        spots = ((0, Y2), (0, 2), (Y2 - 2, 2))
        base = [0, 0] if X2 == 2 else [self.m * (X2 - 2), (1 - self.m) * (X2 - 2)]
        for c in range(C):
            for p in range(X2 + 2):
                W[c, base[0] + p, 0:Y2, :] = W[c, base[0] + p, 0:Y2, :] + Q[c, 2 * (1 - self.m) + p, 0:Y2, :]
        for _, t, k, dy in self.near_copies():
            q, n = spots[k]
            for c in range(C):
                for p in range(X2 + 2):
                    i = (c * (X2 + 2) + p) * n
                    W[c, base[t] + p, q:q + n, :] = W[c, base[t] + p, q:q + n, :] + r["Rn2"][3 * t + k, i:i + n, :]
        for s in (0, 1):
            for k, dy in enumerate(ROWS):
                q, n = spots[k]
                for c in range(C):
                    for p in range(2):
                        i, o = (c * 2 + p) * n, (p if s else 2 * X2 - 2 + p)
                        W[c, o, q:q + n, :] = W[c, o, q:q + n, :] + r["Rd2"][3 * s + k, i:i + n, :]
        for c in range(C):
            for p in range(2 * X2):
                i = (c * 2 * X2 + p) * Y2
                r["Sf2"][i:i + Y2, :] = W[c, p, 0:Y2, :]

    def share_sent(self):
        for c, t, k, dy in self.near_copies():
            self.when(0, dy, c.wait_send)
        for c, dy in self.far_sends():
            pl.when(self.far_exists(dy))(c.wait_send)

    def win_copies(self, n):
        src, dst = self.r["S" + n], self.r["R" + n]
        return [(self.copy(src, dst.at[k], self.win[n] + k, dx, dy), dx, dy) for k, (dx, dy) in enumerate(WINDOW)]

    def win_start(self, n):
        for c, dx, dy in self.win_copies(n):
            pl.when(self.exists(dx, dy))(c.start)

    def win_wait(self, n, target):
        copies = self.win_copies(n)
        for c, dx, dy in copies:
            pl.when(self.exists(-dx, -dy))(c.wait_recv)
        ref = self.r[target]
        X2, Y2 = self.X2, self.Y2
        for k, (dx, dy) in enumerate(WINDOW + [(0, 0)]):
            for c in range(ref.shape[0]):
                for p in range(2 * X2):
                    i = (c * 2 * X2 + p) * Y2
                    if (dx, dy) == (0, 0):
                        v = self.r["S" + n][i:i + Y2, :]
                    else:
                        v = self.r["R" + n][k, i:i + Y2, :]
                    ref[c, 4 + p - dx * X2, Y2 * (1 - dy):Y2 * (2 - dy), :] = v

    def win_sent(self, n):
        for c, dx, dy in self.win_copies(n):
            pl.when(self.exists(dx, dy))(c.wait_send)

    def coefs(self, E, K, a, b, scale):
        E, K = self.r[E], self.r[K]
        Z = E.shape[-1]
        shape = E.shape[-2:]
        R = shape[0]
        s = 1.0 / scale

        @pl.loop(a, b)
        def _(i):
            z = lax.broadcasted_iota(jnp.int32, shape, 1)
            e = E[0, i]

            def face(o):
                t = e + o
                return jnp.where(jnp.minimum(e, o) > 0.0, t * (0.5 * s), t * s)

            zp = jnp.where(z == Z - 1, 0.0, pltpu.roll(e, Z - 1, 1))
            zm = jnp.where(z == 0, 0.0, pltpu.roll(e, 1, 1))
            others = (E[0, i + 1], E[0, i - 1], pltpu.roll(e, R - 1, 0), pltpu.roll(e, 1, 0), zp, zm)
            diag = None
            for k, o in enumerate(others):
                c = face(o)
                diag = c if diag is None else diag + c
                if k == 4:
                    c = jnp.where(z == Z - 1, 0.0, c)
                if k == 5:
                    c = jnp.where(z == 0, 0.0, c)
                K[k, i] = c
            inside = e > 0.0
            K[6, i] = jnp.where(inside, WEIGHT / jnp.where(inside, diag, 1.0), 0.0)
            K[7, i] = diag

    def face(self, E, K, i, o, k, scale):
        e, f = self.r[E][0, i], self.r[E][0, o]
        t, s = e + f, 1.0 / scale
        self.r[K][k, i] = jnp.where(jnp.minimum(e, f) > 0.0, t * (0.5 * s), t * s)

    def stencil(self, V, K, G, i, c, rows):
        R, Z = V.shape[-2:]
        n = rows.stop - rows.start
        v = V[c, i, rows, :]
        if n == R:
            yp, ym = pltpu.roll(v, R - 1, 0), pltpu.roll(v, 1, 0)
        else:
            yp, ym = V[c, i, 1:n + 1, :], pltpu.roll(V[c, i], 1, 0)[:n]
        acc = G[c, i, rows, :]
        parts = (V[c, i + 1, rows, :], V[c, i - 1, rows, :], yp, ym, pltpu.roll(v, Z - 1, 1), pltpu.roll(v, 1, 1))
        for k, o in enumerate(parts):
            acc = acc + K[k, i, rows, :] * o
        return v, acc

    def first(self, K, G, O, a, b, comps=None):
        K, G, O = (self.r[n] for n in (K, G, O))

        @pl.loop(a, b)
        def _(i):
            w = K[6, i]
            for c in comps or range(self.C):
                O[c, i] = w * G[c, i]

    def sweep(self, V, K, G, O, a, b, rows=None, shift=0, comps=None):
        V, K, G = (self.r[n] for n in (V, K, G))
        O = self.r[O] if isinstance(O, str) else O
        rows = rows or slice(0, V.shape[-2])
        out_rows = rows if shift == 0 else slice(0, rows.stop - rows.start)

        @pl.loop(a, b)
        def _(i):
            for c in comps or range(self.C):
                v, acc = self.stencil(V, K, G, i, c, rows)
                O[c, i - shift, out_rows, :] = (1.0 - WEIGHT) * v + K[6, i, rows, :] * acc

    def clear(self):
        r, C, X, Y, X1, Y1 = self.r, self.C, self.X, self.Y, self.X1, self.Y1

        def zero(ref, *idx):
            ref[idx] = jnp.zeros(ref.at[idx].shape, ref.dtype)

        for n, rows in (("E0", Y), ("F0", Y), ("V0", Y), ("E1", Y1), ("F1", Y1), ("V1", Y1), ("G1", 0), ("E2", 0), ("F2", 0), ("A2", 0)):
            ref = r[n]

            @pl.loop(0, ref.shape[1])
            def _(i):
                for c in range(ref.shape[0]):
                    zero(ref, c, i, slice(rows, ref.shape[2]))
        for n, planes in (("V0", (0, 1, X + 2, X + 3)), ("A0", (1, X + 2)), ("F1", (0, X1 + 5)),
                          ("A1", (0, X1 + 5)), ("B1", (0, X1 + 5))):
            for c in range(C):
                for p in planes:
                    zero(r[n], c, p)
        absent = {}

        def when_absent(dx, dy, ref, *idx):
            absent.setdefault((dx, dy), []).append((ref, idx))

        for h in (*self.hE0x, self.hE0, self.hE1, *self.hF0, self.hF1, self.hV1, *self.hV0):
            ref = r[h["target"]]
            for m in h["msgs"]:
                if m[0] == "x" and h["land"]:
                    k = 0 if m[1] > 0 else 1
                    for c in range(h["comps"]):
                        for p in range(h["w"]):
                            when_absent(m[1], 0, r[h["name"] + "_lx"], k, c, p)
                elif m[0] == "x":
                    for c in range(h["base"], h["base"] + h["comps"]):
                        for p in range(m[4], m[4] + h["w"]):
                            when_absent(m[1], 0, ref, c, p, slice(0, h["Y"]))
                elif m[0] == "y":
                    when_absent(0, m[2], r[h["name"] + "_ry"], m[1])
                else:
                    when_absent(*m[2], r[h["name"] + "_rd"], m[1])
        for m in self.aG1["msgs"]:
            when_absent(m[1], m[2], r[m[0] + "_r"], slice(None))
        for k, (dx, t, dy) in enumerate(MEMBERS):
            if dx or dy:
                when_absent(dx, dy, r["Re2"], k)
        for k, (dx, dy) in enumerate(WINDOW):
            for n in ("Rf2", "Rv2"):
                when_absent(dx, dy, r[n], k)
        for k, dy in enumerate(ROWS):
            for t in (0, 1):
                if dy:
                    when_absent(0, dy, r["Rn2"], 3 * t + k)
                when_absent(4 * t - 2, dy, r["Rd2"], 3 * t + k)
        for (dx, dy), spots in absent.items():
            @pl.when(jnp.logical_not(self.exists(-dx, -dy)))
            def _():
                for ref, idx in spots:
                    zero(ref, *idx)

    def edges(self):
        r, C, X, Y, R = self.r, self.C, self.X, self.Y, self.R0
        K = r["C0"]
        for h in self.hF0:
            for c, dx, dy in self.halo_copies(h, "y"):
                pl.when(self.exists(-dx, -dy))(c.wait_recv)
        for c in range(C):
            stage = r[self.hF0[c]["name"] + "_ry"]
            for p in (2, 3, X, X + 1):
                r["B0"][c, p, 0:Y, :] = r["V0"][c, p, 0:Y, :]
                for k, q, f, o in ((0, 0, 3, R - 1), (1, Y - 1, 2, Y)):
                    a = K[6, p, o:o + 1, :] * stage[k, p - 2:p - 1, :]
                    r["B0"][c, p, q:q + 1, :] = r["V0"][c, p, q:q + 1, :] + (
                        K[6, p, q:q + 1, :] * (K[f, p, q:q + 1, :] * a))

    def residual(self, V, K, G, T, px, Xc, ring, a, b):
        V, K, G, T = (self.r[n] for n in (V, K, G, T))
        R = V.shape[-2]
        rows = slice(0, R)
        n = Xc + 2 * ring

        def defect(i, c):
            v, acc = self.stencil(V, K, G, i, c, rows)
            return acc - K[7, i] * v

        @pl.loop(a, b)
        def _(j):
            for c in range(self.C):
                i = px + 2 * j
                start = pl.multiple_of((c * n + j + ring) * R, 8)
                T[pl.ds(start, R), :] = 0.5 * (defect(i, c) + defect(i + 1, c))

    def ring_residual(self, V, K, T, px, Xc, ring):
        V, K, T = (self.r[n] for n in (V, K, T))
        R, n = V.shape[-2], Xc + 2 * ring
        last = px + 2 * Xc + 2 * ring - 2
        for c in range(self.C):
            for near, far, k, j in ((px - 2 * ring + 1, px - 2 * ring, 0, 0), (last, last + 1, 1, n - 1)):
                start = (c * n + j) * R
                if ring == 1:
                    step = 1 if k == 0 else -1
                    v = V[c, near]
                    acc = K[k, near] * V[c, near + step] - K[7, near] * v + K[k, far] * v
                    for f, o in ((2, pltpu.roll(v, R - 1, 0)), (3, pltpu.roll(v, 1, 0)),
                                 (4, pltpu.roll(v, v.shape[1] - 1, 1)), (5, pltpu.roll(v, 1, 1))):
                        acc = acc + K[f, near] * o
                else:
                    acc = K[k, near] * V[c, near + (1 if k == 0 else -1)]
                T[start:start + R, :] = 0.5 * acc

    def spread(self, V, K, G, i, o, k):
        V, K, O = (self.r[n] for n in (V, K, G))
        for c in range(self.C):
            O[c, i] = K[6, i] * (K[k, i] * V[c, o])

    def dot(self, a, b):
        return lax.dot_general(a, b, (((1,), (0,)), ((), ())), preferred_element_type=jnp.float32)

    def split(self, t):
        hi = t.astype(jnp.bfloat16)
        return hi, (t - hi.astype(jnp.float32)).astype(jnp.bfloat16)

    def right(self, t, m):
        hi, lo = self.split(t)
        return self.dot(hi, m) + self.dot(lo, m)

    def left(self, m, t):
        hi, lo = self.split(t)
        return self.dot(m, hi) + self.dot(m, lo)

    def pairs(self, n, m, value, fine_dim):
        r = lax.broadcasted_iota(jnp.int32, (n, m), 0)
        c = lax.broadcasted_iota(jnp.int32, (n, m), 1)
        hit = (r >> 1) == c if fine_dim == 0 else (c >> 1) == r
        return jnp.where(hit, value, 0.0).astype(jnp.bfloat16)

    def squeeze(self, t):
        rows, Z = t.shape
        half = self.right(t, self.pairs(Z, Z // 2, 0.5, 0))
        return self.left(self.pairs(rows // 2, rows, 0.5, 1), half)

    def squeeze0(self, n):
        T, Z, R, R1, Y1 = self.r["T0"], self.Z, self.R0, self.R1, self.Y1
        half = self.right(T[...], self.pairs(Z, Z // 2, 0.5, 0))
        o = lax.broadcasted_iota(jnp.int32, (n * R1, n * R), 0)
        f = lax.broadcasted_iota(jnp.int32, (n * R1, n * R), 1)
        bo, bf = jnp.zeros_like(o), jnp.zeros_like(f)
        for k in range(1, n):
            bo = bo + (o >= k * R1).astype(jnp.int32)
            bf = bf + (f >= k * R).astype(jnp.int32)
        q = o - bo * R1
        q = jnp.where(q <= Y1, q, jnp.where(q == R1 - 1, R // 2 - 1, -1))
        m = jnp.where((bo == bf) & (((f - bf * R) >> 1) == q), 0.5, 0.0).astype(jnp.bfloat16)
        return [self.left(m, half[c * n * R:(c + 1) * n * R]) for c in range(self.C)]

    def prolong(self, W, a, count, U, V, planes, coarse_of, offset, shift=0):
        W, U, V = (self.r[n] for n in (W, U, V))
        C, _, Rc, Zc = W.shape
        Rf, Zf = V.shape[-2:]
        src = W[:, pl.ds(a + shift, count)].reshape(C * count * Rc, Zc)
        U[...] = self.right(src, self.pairs(Zc, Zf, 1.0, 1))
        r = lax.broadcasted_iota(jnp.int32, (Rf, Rc), 0)
        c = lax.broadcasted_iota(jnp.int32, (Rf, Rc), 1)
        r = jnp.where(r < Rf - 4, r, r - Rf)
        c = c - offset if offset else jnp.where(c < Rc - 4, c, c - Rc)
        lift = jnp.where((r >> 1) == c, 1.0, 0.0).astype(jnp.bfloat16)
        for comp in range(C):
            for k in range(count):
                start = (comp * count + k) * Rc
                block = self.left(lift, U[start:start + Rc, :])
                for p in planes:
                    if coarse_of(p) == a + k:
                        V[comp, p] = V[comp, p] + block

    def body(self, forcing, phase, out, *scratch):
        names = list(self.scratch)
        self.r = r = dict(zip(names, scratch))
        self.ssem, self.rsem, lsem = scratch[len(names):]
        self.gx, self.gy = lax.axis_index("gx"), lax.axis_index("gy")
        self.m = lax.rem(self.gx, 2)
        X, Y, Z, C = self.X, self.Y, self.Z, self.C
        X1, Y1 = self.X1, self.Y1
        block = (pl.ds(2, X), pl.ds(TOP, Y))
        load_p = pltpu.make_async_copy(phase, r["ph"], lsem.at[0])
        load_p.start()
        load_f = pltpu.make_async_copy(forcing, r["F0"].at[:, block[0], block[1], :], lsem.at[1])
        load_f.start()

        barrier = pltpu.get_barrier_semaphore()
        count = jnp.int32(0)
        for dx, t, dy in MEMBERS:
            ok = self.exists(dx, dy) if dx or dy else self.gx >= 0
            count = count + ok.astype(jnp.int32)

            @pl.when(ok)
            def _():
                pl.semaphore_signal(barrier, inc=1, device_id=(self.gx + dx + t * (1 - 2 * self.m), self.gy + dy),
                                    device_id_type=MESH)
        self.clear()
        load_p.wait()

        @pl.loop(0, X)
        def _(i):
            ph = r["ph"][i]
            e = jnp.zeros(ph.shape, jnp.float32)
            for k, value in enumerate(VISCOSITIES):
                e = jnp.where(ph == k, jnp.float32(value), e)
            r["E0"][0, i + 2, TOP:TOP + Y, :] = e
        pl.semaphore_wait(barrier, count)
        self.halo_start(self.hE0x[0])
        self.halo_start(self.hE0)
        load_f.wait()
        for h in self.hF0:
            self.halo_start(h, "y")

        for j in range(X1):
            r["T0"][j * Y:(j + 1) * Y, :] = 0.5 * (
                r["E0"][0, 2 + 2 * j, TOP:TOP + Y, :] + r["E0"][0, 3 + 2 * j, TOP:TOP + Y, :])
        e1 = self.squeeze(r["T0"][0:X1 * Y, :])
        for j in range(X1):
            r["E1"][0, 3 + j, TOP:TOP + Y1, :] = e1[j * Y1:(j + 1) * Y1]
        for j in range(self.X2):
            r["T1"][j * Y1:(j + 1) * Y1, :] = 0.5 * (
                e1[2 * j * Y1:(2 * j + 1) * Y1] + e1[(2 * j + 1) * Y1:(2 * j + 2) * Y1])
        r["Se2"][...] = self.squeeze(r["T1"][0:self.X2 * Y1, :])

        self.halo_start(self.hE1)
        self.halo_start(self.hE0x[1])
        self.member_start()
        for h in self.hF0:
            self.halo_start(h, "x")
        X2, Y2, R1 = self.X2, self.Y2, self.R1
        self.halo_wait(self.hE0, "y")
        self.coefs("E0", "C0", 3, X + 1, 1.0)
        self.first("C0", "F0", "A0", 3, X + 1)
        self.sweep("A0", "C0", "F0", "V0", 4, X)
        self.halo_wait(self.hE0x[0])
        self.halo_wait(self.hE0, "d")
        for p in (2, X + 1):
            self.coefs("E0", "C0", p, p + 1, 1.0)
            self.first("C0", "F0", "A0", p, p + 1)
        self.sweep("A0", "C0", "F0", "V0", 2, 4)
        self.sweep("A0", "C0", "F0", "V0", X, X + 2)
        self.residual("V0", "C0", "F0", "T0", 2, X1, 1, 1, X1 - 1)
        self.halo_wait(self.hE1)
        self.coefs("E1", "C1", 1, X1 + 5, 4.0)
        self.face("E1", "C1", 0, 1, 0, 4.0)
        self.face("E1", "C1", X1 + 5, X1 + 4, 1, 4.0)
        self.halo_wait(self.hE0x[1])
        for p, o, k in ((1, 0, 0), (X + 2, X + 3, 1)):
            self.coefs("E0", "C0", p, p + 1, 1.0)
            self.face("E0", "C0", o, p, k, 1.0)
        self.spread("A0", "C0", "V0", 1, 2, 0)
        self.spread("A0", "C0", "V0", X + 2, X + 1, 1)
        self.edges()
        self.residual("V0", "C0", "F0", "T0", 2, X1, 1, 0, 1)
        self.residual("V0", "C0", "F0", "T0", 2, X1, 1, X1 - 1, X1)
        self.ring_residual("V0", "C0", "T0", 2, X1, 1)
        for c, f1 in enumerate(self.squeeze0(X1 + 2)):
            for j in range(X1 + 2):
                r["G1"][c, 2 + j] = f1[j * R1:(j + 1) * R1]
        self.ring_start(self.aG1)

        self.first("C1", "G1", "A1", 1, X1 + 5)
        self.sweep("A1", "C1", "G1", "B1", 1, X1 + 5)
        self.residual("B1", "C1", "G1", "T1", 3, X2, 2, -1, X2 + 1)
        self.ring_residual("B1", "C1", "T1", 3, X2, 2)
        f2 = self.squeeze(r["T1"][...])
        n = self.R1 // 2
        for c in range(C):
            for j in range(X2 + 4):
                s = (c * (X2 + 4) + j) * n
                r["Q2"][c, j] = f2[s:s + n]
        self.share_start()

        self.ring_wait(self.aG1)
        for c in range(C):
            for j in range(X1):
                r["F1"][c, 3 + j, 0:Y1, :] = r["G1"][c, 3 + j, 0:Y1, :]
        self.ring_add(self.aG1, lambda c, p, q, k: (r["F1"], (c, 3 + p, slice(q, q + k))))
        self.halo_start(self.hF1)

        for h in self.hF0:
            self.halo_wait(h, "x")
            self.halo_place(h)
        rows0 = slice(TOP, TOP + Y)
        self.first("C0", "F0", "A0", 1, X + 3)
        self.sweep("A0", "C0", "F0", "V0", 2, X + 2, rows0)
        for h in self.hV0:
            self.halo_start(h, "yd")

        self.share_wait()
        self.win_start("f2")
        self.halo_start(self.hV0[0], "x")

        self.halo_wait(self.hF1)
        self.first("C1", "F1", "A1", 1, X1 + 5)
        self.sweep("A1", "C1", "F1", "B1", 2, X1 + 4)
        for c in range(C):
            for j in range(X1):
                r["V1"][c, 3 + j, TOP:TOP + Y1, :] = r["B1"][c, 3 + j, TOP:TOP + Y1, :]
            for dx in (2, X1 + 3):
                r["V1"][c, dx, 0:Y1, :] = r["B1"][c, dx, 0:Y1, :]
            for j in range(-1, X1 + 1):
                for q in (self.R1 - 1, Y1):
                    r["V1"][c, 3 + j, q:q + 1, :] = r["B1"][c, 3 + j, q:q + 1, :]
        self.halo_start(self.hV1)

        self.member_wait()
        self.coefs("E2", "C2", 1, self.P2 - 1, 16.0)
        self.win_wait("f2", "F2")
        p2 = self.P2
        self.first("C2", "F2", "A2", 1, p2 - 1)
        self.sweep("A2", "C2", "F2", "B2", 2, p2 - 2)
        self.sweep("B2", "C2", "F2", "A2", 3, p2 - 3)
        self.sweep("A2", "C2", "F2", "B2", 4, p2 - 4)
        for c in range(C):
            for p in range(2 * self.X2):
                i = (c * 2 * self.X2 + p) * self.Y2
                r["Sv2"][i:i + self.Y2, :] = r["B2"][c, 4 + p, self.Y2:2 * self.Y2, :]
        self.win_start("v2")
        self.halo_start(self.hV0[1], "x")
        self.halo_start(self.hV0[2], "x")
        self.win_wait("v2", "A2")
        self.sweep("A2", "C2", "F2", "B2", 1, p2 - 1)
        self.sweep("B2", "C2", "F2", "A2", 2, p2 - 2)

        self.halo_wait(self.hV1)
        self.halo_sent(self.hV1)
        self.prolong("A2", 2, self.X2 + 4, "UZ1", "V1", range(self.P1),
                     lambda p: 4 + (p - 3) // 2, self.Y2, self.m * self.X2)
        self.sweep("V1", "C1", "F1", "A1", 1, X1 + 5)
        self.sweep("A1", "C1", "F1", "B1", 2, X1 + 4)

        for c, h in enumerate(self.hV0):
            self.halo_wait(h)
            self.halo_sent(h)
            lx, V = r[h["name"] + "_lx"], r["V0"]
            V[c, 0, 0:Y, :] = lx[0, 0, 0]
            V[c, 1, 0:Y, :] = V[c, 1, 0:Y, :] + lx[0, 0, 1]
            V[c, X + 2, 0:Y, :] = V[c, X + 2, 0:Y, :] + lx[1, 0, 0]
            V[c, X + 3, 0:Y, :] = lx[1, 0, 1]
        self.prolong("B1", 2, X1 + 2, "UZ0", "V0", range(self.P0),
                     lambda p: 3 + (p - 2) // 2, 0)
        self.sweep("V0", "C0", "F0", "B0", 1, X + 3)
        self.sweep("B0", "C0", "F0", out, 2, X + 2, rows0, shift=2)
        for h in (self.hE0, *self.hE0x, *self.hF0, self.hE1, self.hF1):
            self.halo_sent(h)
        self.ring_sent(self.aG1)
        self.share_sent()
        self.member_sent()
        for n in ("f2", "v2"):
            self.win_sent(n)

    def __call__(self, forcing, phase):
        any_space = pl.BlockSpec(memory_space=pl.ANY)
        sems = [pltpu.SemaphoreType.DMA((self.n_sems,)), pltpu.SemaphoreType.DMA((self.n_sems,)),
                pltpu.SemaphoreType.DMA((2,))]
        return pl.pallas_call(
            self.body,
            out_shape=pltpu.VMEM(forcing.shape, jnp.float32),
            in_specs=[any_space, any_space],
            out_specs=pl.BlockSpec(memory_space=pltpu.VMEM),
            scratch_shapes=list(self.scratch.values()) + sems,
            compiler_params=pltpu.CompilerParams(
                collective_id=0, has_side_effects=True, vmem_limit_bytes=60 * 1024 * 1024),
            name="vcycle",
        )(forcing, phase)


def solution(mesh):
    grid = (mesh.shape["gx"], mesh.shape["gy"])

    def per_device(forcing, phase_ids):
        return Kernel(phase_ids.shape, forcing.shape[0], grid)(forcing, phase_ids)

    return jax.shard_map(
        per_device,
        mesh=mesh,
        in_specs=(P(None, "gx", "gy", None), P("gx", "gy", None)),
        out_specs=P(None, "gx", "gy", None),
        check_vma=False,
    )
```

```python
import functools

import jax
import jax.numpy as jnp
from jax import lax
from jax.experimental import pallas as pl
from jax.experimental.pallas import tpu as pltpu
from jax.sharding import PartitionSpec as P

COARSE_SWEEPS = 6
VISCOSITIES = (0.2, 0.6, 1.5, 4.0)
WEIGHT = 2.0 / 3.0
MESH = pl.DeviceIdType.MESH
WINDOW = [(dx, dy) for dx in (-2, 0, 2) for dy in (-1, 0, 1) if (dx, dy) != (0, 0)]
MEMBERS = [(dx, t, dy) for dx in (-2, 0, 2) for t in (0, 1) for dy in (-1, 0, 1) if (dx, t, dy) != (0, 0, 0)]
ROWS = (0, 1, -1)
TOP = 0


def up8(n):
    return -(-n // 8) * 8


def side_slices(step, first, length, lo, hi):
    if step > 0:
        return (first + length - hi, first - hi)
    return (first + lo - 1, first + length + lo - 1)


class Kernel:
    def __init__(self, sizes, comps, grid):
        self.X, self.Y, self.Z = sizes
        self.C = comps
        self.grid = grid
        self.scratch = {}
        self.n_sems = 0
        self.plan()

    def buf(self, name, shape, dtype=jnp.float32):
        self.scratch[name] = pltpu.VMEM(tuple(shape), dtype)

    def halo(self, name, target, comps, px, X, Y, Z, lo, hi, diag, base=0, land=None, only="xyd"):
        w = hi - lo + 1
        msgs = []
        for dx in (1, -1) if "x" in only else ():
            s, d = side_slices(dx, px, X, lo, hi)
            msgs.append(("x", dx, 0, s, d, self.n_sems))
            self.n_sems += 1
        n = comps * X * w
        if "y" in only:
            self.buf(name + "_sy", (2, up8(n), Z))
            self.buf(name + "_ry", (2, up8(n), Z))
        for k, dy in enumerate((1, -1)) if "y" in only else ():
            s, d = side_slices(dy, TOP, Y, lo, hi)
            d %= Y + 8
            msgs.append(("y", k, dy, s, d, self.n_sems))
            self.n_sems += 1
        if diag:
            n = comps * len(diag)
            self.buf(name + "_sd", (4, n, 1, Z))
            self.buf(name + "_rd", (4, n, 1, Z))
            for k, (dx, dy) in enumerate([(1, 1), (1, -1), (-1, 1), (-1, -1)]):
                cells = [[], []]
                for a, b in diag:
                    sx, tx = side_slices(dx, px, X, a, a)
                    sy, ty = side_slices(dy, TOP, Y, b, b)
                    cells[0].append((sx, sy))
                    cells[1].append((tx, ty % (Y + 8)))
                msgs.append(("d", k, (dx, dy), cells[0], cells[1], self.n_sems))
                self.n_sems += 1
        if land:
            self.buf(name + "_lx", (2, comps, w, Y, Z))
        return dict(name=name, land=land, base=base, target=target, comps=comps, px=px, X=X, Y=Y, w=w, diag=diag, msgs=msgs)

    def ring(self, name, source, px, X, Y, Z, w):
        C = self.C
        dirs = [(dx, dy) for dx in (0, 1, -1) for dy in (0, 1, -1) if (dx, dy) != (0, 0)]
        msgs = []
        for dx, dy in dirs:
            px_count, rows = (w if dx else X), (w if dy else Y)
            key = "%s_%d%d" % (name, dx + 1, dy + 1)
            n = up8(C * px_count * rows)
            self.buf(key + "_s", (n, Z))
            self.buf(key + "_r", (n, Z))
            out = (px + (X if dx > 0 else -w if dx < 0 else 0), Y if dy > 0 else -w if dy < 0 else 0)
            into = (X - w if dx < 0 else 0, Y - w if dy < 0 else 0)
            msgs.append((key, dx, dy, px_count, rows, out, into, self.n_sems))
            self.n_sems += 1
        return dict(source=source, msgs=msgs)

    def plan(self):
        X, Y, Z, C = self.X, self.Y, self.Z, self.C
        self.P0, self.R0 = X + 4, Y + 8
        self.X1, self.Y1, self.Z1 = X // 2, Y // 2, Z // 2
        self.P1, self.R1 = self.X1 + 6, self.Y1 + 8
        self.X2, self.Y2, self.Z2 = X // 4, Y // 4, Z // 4
        self.P2, self.R2 = 2 * self.X2 + 8, up8(self.Y2 * 3)
        b = self.buf
        b("ph", (X, Y, Z), jnp.int32)
        b("E0", (1, self.P0, self.R0, Z))
        b("C0", (8, self.P0, self.R0, Z))
        for n in ("F0", "A0", "V0", "B0", "D0"):
            b(n, (C, self.P0, self.R0, Z))
        b("T0", (C * (self.X1 + 2) * self.R0, Z))
        b("E1", (1, self.P1, self.R1, self.Z1))
        b("C1", (8, self.P1, self.R1, self.Z1))
        for n in ("F1", "G1", "A1", "V1", "B1"):
            b(n, (C, self.P1, self.R1, self.Z1))
        b("T1", (C * (self.X2 + 4) * self.R1, self.Z1))
        b("E2", (1, self.P2, self.R2, self.Z2))
        b("C2", (8, self.P2, self.R2, self.Z2))
        for n in ("F2", "A2", "B2"):
            b(n, (C, self.P2, self.R2, self.Z2))
        blk = self.X2 * self.Y2
        b("Se2", (blk, self.Z2))
        b("Re2", (len(MEMBERS), blk, self.Z2))
        for n in ("f2", "v2"):
            b("S" + n, (2 * C * blk, self.Z2))
            b("R" + n, (len(WINDOW), 2 * C * blk, self.Z2))
        near, far = up8(C * (self.X2 + 2) * self.Y2), up8(C * 2 * self.Y2)
        b("Sn2", (3, near, self.Z2))
        b("Rn2", (6, near, self.Z2))
        b("Sd2", (3, far, self.Z2))
        b("Rd2", (6, far, self.Z2))
        b("W2", (C, 2 * self.X2, 8, self.Z2))
        b("Q2", (C, self.X2 + 4, self.R1 // 2, self.Z2))
        b("UZ1", (self.R2 * C * (self.X2 + 4), self.Z1))
        b("UZ0", (self.R1 * C * (self.X1 + 2), self.Z))
        reach = [(1, 1), (1, 2), (2, 1), (1, 3), (2, 2), (3, 1)]
        self.hE0 = self.halo("hE0", "E0", 1, 2, X, Y, Z, 1, 2, [(1, 1)], only="yd")
        self.hE0x = [self.halo("hE0x%d" % k, "E0", 1, 2, X, Y, Z, k, k, [], only="x") for k in (1, 2)]
        self.hF0 = [self.halo("hFc%d" % c, "F0", 1, 2, X, Y, Z, 1, 1, [], c) for c in range(C)]
        self.hV0 = [self.halo("hVc%d" % c, "V0", 1, 2, X, Y, Z, 1, 2, [(1, 1)], c, "D0") for c in range(C)]
        self.hE1 = self.halo("hE1", "E1", 1, 3, self.X1, self.Y1, self.Z1, 1, 3, reach)
        self.hF1 = self.halo("hF1", "F1", C, 3, self.X1, self.Y1, self.Z1, 1, 2, reach[:3])
        self.hV1 = self.halo("hV1", "V1", C, 3, self.X1, self.Y1, self.Z1, 2, 3, reach[1:])
        self.aG1 = self.ring("aG1", "G1", 3, self.X1, self.Y1, self.Z1, 1)
        self.win = {}
        for n, k in (("e2", len(MEMBERS)), ("f2", len(WINDOW)), ("v2", len(WINDOW)), ("n2", 6), ("d2", 6)):
            self.win[n] = self.n_sems
            self.n_sems += k

    def exists(self, dx, dy):
        ok = None
        for step, me, size in ((dx, self.gx, self.grid[0]), (dy, self.gy, self.grid[1])):
            if step:
                t = (me + step >= 0) & (me + step < size)
                ok = t if ok is None else ok & t
        return ok

    def copy(self, src, dst, sem, dx, dy, into=None):
        into = sem if into is None else into
        return pltpu.make_async_remote_copy(
            src_ref=src, dst_ref=dst, send_sem=self.ssem.at[sem], recv_sem=self.rsem.at[into],
            device_id=(self.gx + dx, self.gy + dy), device_id_type=MESH)

    def halo_copies(self, h, kinds="xyd"):
        r = self.r
        ref = r[h["target"]]
        rows = pl.ds(TOP, h["Y"])
        out = []
        for m in h["msgs"]:
            if m[0] not in kinds:
                continue
            if m[0] == "x":
                _, dx, dy, s, d, sem = m
                comps = pl.ds(h["base"], h["comps"])
                src, dst = ref, ref.at[comps, pl.ds(d, h["w"]), rows, :]
                if h["land"]:
                    src, dst = r[h["land"]], r[h["name"] + "_lx"].at[0 if dx > 0 else 1]
                c = self.copy(src.at[comps, pl.ds(s, h["w"]), rows, :], dst, sem, dx, 0)
                out.append((c, dx, 0))
            elif m[0] == "y":
                _, k, dy, s, d, sem = m
                out.append((self.copy(r[h["name"] + "_sy"].at[k], r[h["name"] + "_ry"].at[k], sem, 0, dy), 0, dy))
            else:
                _, k, (dx, dy), _, _, sem = m
                out.append((self.copy(r[h["name"] + "_sd"].at[k], r[h["name"] + "_rd"].at[k], sem, dx, dy), dx, dy))
        return out

    def rows_of(self, h, m, which):
        if m[0] == "y":
            start = m[3 + which]
            return m[1], "y", [(c + h["base"], h["px"] + p, start + q) for c in range(h["comps"])
                               for p in range(h["X"]) for q in range(h["w"])]
        return m[1], "d", [(c + h["base"], p, q) for c in range(h["comps"]) for p, q in m[3 + which]]

    def halo_start(self, h, kinds="xyd"):
        ref = self.r[h["target"]]
        for m in h["msgs"]:
            if m[0] == "x" or m[0] not in kinds:
                continue
            k, kind, rows = self.rows_of(h, m, 0)
            stage = self.r[h["name"] + "_s" + kind]
            for i, (c, p, q) in enumerate(rows):
                row = ref[c, p, q:q + 1, :]
                if kind == "d":
                    stage[k, i] = row
                else:
                    stage[k, i:i + 1, :] = row
        for c, dx, dy in self.halo_copies(h, kinds):
            pl.when(self.exists(dx, dy))(c.start)

    def halo_wait(self, h, kinds="xyd"):
        for c, dx, dy in self.halo_copies(h, kinds):
            pl.when(self.exists(-dx, -dy))(c.wait_recv)
        self.halo_place(h, kinds)

    def halo_place(self, h, kinds="xyd"):
        ref = self.r[h["target"]]
        for m in h["msgs"]:
            if m[0] == "x" or m[0] not in kinds:
                continue
            k, kind, rows = self.rows_of(h, m, 1)
            stage = self.r[h["name"] + "_r" + kind]
            for i, (c, p, q) in enumerate(rows):
                ref[c, p, q:q + 1, :] = stage[k, i] if kind == "d" else stage[k, i:i + 1, :]

    def halo_sent(self, h, kinds="xyd"):
        for c, dx, dy in self.halo_copies(h, kinds):
            pl.when(self.exists(dx, dy))(c.wait_send)

    def ring_copies(self, h):
        r = self.r
        return [(self.copy(r[m[0] + "_s"], r[m[0] + "_r"], m[7], m[1], m[2]), m[1], m[2]) for m in h["msgs"]]

    def ring_start(self, h):
        S = self.r[h["source"]]
        for key, dx, dy, planes, rows, (p, q), _, _ in h["msgs"]:
            q %= S.shape[2]
            i = 0
            for c in range(self.C):
                for k in range(planes):
                    self.r[key + "_s"][i:i + rows, :] = S[c, p + k, q:q + rows, :]
                    i += rows
        for c, dx, dy in self.ring_copies(h):
            pl.when(self.exists(dx, dy))(c.start)

    def ring_wait(self, h):
        for c, dx, dy in self.ring_copies(h):
            pl.when(self.exists(-dx, -dy))(c.wait_recv)

    def ring_add(self, h, place):
        for key, dx, dy, planes, rows, _, (p, q), _ in h["msgs"]:
            i = 0
            for c in range(self.C):
                for k in range(planes):
                    ref, idx = place(c, p + k, q, rows)
                    ref[idx] = ref[idx] + self.r[key + "_r"][i:i + rows, :]
                    i += rows

    def ring_sent(self, h):
        for c, dx, dy in self.ring_copies(h):
            pl.when(self.exists(dx, dy))(c.wait_send)

    def when(self, dx, dy, f):
        if (dx, dy) == (0, 0):
            f()
        else:
            pl.when(self.exists(dx, dy))(f)

    def member_copies(self):
        r = self.r
        return [(self.copy(r["Se2"], r["Re2"].at[k], self.win["e2"] + k, dx + t * (1 - 2 * self.m), dy), dx, t, dy)
                for k, (dx, t, dy) in enumerate(MEMBERS)]

    def member_start(self):
        for c, dx, t, dy in self.member_copies():
            self.when(dx, dy, c.start)

    def member_wait(self):
        for c, dx, t, dy in self.member_copies():
            self.when(-dx, -dy, c.wait_recv)
        E, X2, Y2 = self.r["E2"], self.X2, self.Y2
        for k, (dx, t, dy) in enumerate(MEMBERS + [(0, 0, 0)]):
            member = 1 - self.m if t else self.m
            for p in range(X2):
                v = self.r["Se2"][p * Y2:(p + 1) * Y2] if k == len(MEMBERS) else self.r["Re2"][k, p * Y2:(p + 1) * Y2]
                E[0, 4 + p - dx * X2 + member * X2, Y2 * (1 - dy):Y2 * (2 - dy), :] = v

    def member_sent(self):
        for c, dx, t, dy in self.member_copies():
            self.when(dx, dy, c.wait_send)

    def near_copies(self):
        r, b = self.r, self.win["n2"]
        return [(self.copy(r["Sn2"].at[k], r["Rn2"].at[3 * t + k], b + 3 * t + k, t * (1 - 2 * self.m), dy), t, k, dy)
                for t in (1, 0) for k, dy in enumerate(ROWS) if (t, dy) != (0, 0)]

    def far_sends(self):
        r, b, m = self.r, self.win["d2"], self.m
        return [(self.copy(r["Sd2"].at[k], r["Rd2"].at[3 * m + k], b + 3 * t + k, (2 * m - 1) * (2 - t), dy, b + 3 * m + k), dy)
                for t in (1, 0) for k, dy in enumerate(ROWS)]

    def far_recvs(self):
        r, b = self.r, self.win["d2"]
        return [(self.copy(r["Sd2"].at[k], r["Rd2"].at[3 * s + k], b + 3 * s + k, 2, dy), 2 - 4 * s, k, dy)
                for s in (0, 1) for k, dy in enumerate(ROWS)]

    def far_exists(self, dy):
        x = self.gx + 2 * (2 * self.m - 1)
        ok = (x >= 0) & (x < self.grid[0])
        return ok & self.exists(0, dy) if dy else ok

    def share_start(self):
        r, C, X2, Y2 = self.r, self.C, self.X2, self.Y2
        Q = r["Q2"]
        R = Q.shape[2]
        for k, dy in enumerate(ROWS):
            q, n = ((0, Y2), (Y2, 2), (R - 2, 2))[k]
            i = 0
            for c in range(C):
                for p in range(X2 + 2):
                    r["Sn2"][k, i:i + n, :] = Q[c, 2 * (1 - self.m) + p, q:q + n, :]
                    i += n
            i = 0
            for c in range(C):
                for p in range(2):
                    r["Sd2"][k, i:i + n, :] = Q[c, self.m * (X2 + 2) + p, q:q + n, :]
                    i += n
        for c, t, k, dy in self.near_copies():
            self.when(0, dy, c.start)
        for c, dy in self.far_sends():
            pl.when(self.far_exists(dy))(c.start)

    def share_wait(self):
        r, C, X2, Y2 = self.r, self.C, self.X2, self.Y2
        W, Q = r["W2"], r["Q2"]
        for c, t, k, dy in self.near_copies():
            self.when(0, -dy, c.wait_recv)
        for c, dx, k, dy in self.far_recvs():
            self.when(dx, -dy, c.wait_recv)
        W[...] = jnp.zeros(W.shape, jnp.float32)
        spots = ((0, Y2), (0, 2), (Y2 - 2, 2))
        base = [0, 0] if X2 == 2 else [self.m * (X2 - 2), (1 - self.m) * (X2 - 2)]
        for c in range(C):
            for p in range(X2 + 2):
                W[c, base[0] + p, 0:Y2, :] = W[c, base[0] + p, 0:Y2, :] + Q[c, 2 * (1 - self.m) + p, 0:Y2, :]
        for _, t, k, dy in self.near_copies():
            q, n = spots[k]
            for c in range(C):
                for p in range(X2 + 2):
                    i = (c * (X2 + 2) + p) * n
                    W[c, base[t] + p, q:q + n, :] = W[c, base[t] + p, q:q + n, :] + r["Rn2"][3 * t + k, i:i + n, :]
        for s in (0, 1):
            for k, dy in enumerate(ROWS):
                q, n = spots[k]
                for c in range(C):
                    for p in range(2):
                        i, o = (c * 2 + p) * n, (p if s else 2 * X2 - 2 + p)
                        W[c, o, q:q + n, :] = W[c, o, q:q + n, :] + r["Rd2"][3 * s + k, i:i + n, :]
        for c in range(C):
            for p in range(2 * X2):
                i = (c * 2 * X2 + p) * Y2
                r["Sf2"][i:i + Y2, :] = W[c, p, 0:Y2, :]

    def share_sent(self):
        for c, t, k, dy in self.near_copies():
            self.when(0, dy, c.wait_send)
        for c, dy in self.far_sends():
            pl.when(self.far_exists(dy))(c.wait_send)

    def win_copies(self, n):
        src, dst = self.r["S" + n], self.r["R" + n]
        return [(self.copy(src, dst.at[k], self.win[n] + k, dx, dy), dx, dy) for k, (dx, dy) in enumerate(WINDOW)]

    def win_start(self, n):
        for c, dx, dy in self.win_copies(n):
            pl.when(self.exists(dx, dy))(c.start)

    def win_wait(self, n, target):
        copies = self.win_copies(n)
        for c, dx, dy in copies:
            pl.when(self.exists(-dx, -dy))(c.wait_recv)
        ref = self.r[target]
        X2, Y2 = self.X2, self.Y2
        for k, (dx, dy) in enumerate(WINDOW + [(0, 0)]):
            for c in range(ref.shape[0]):
                for p in range(2 * X2):
                    i = (c * 2 * X2 + p) * Y2
                    if (dx, dy) == (0, 0):
                        v = self.r["S" + n][i:i + Y2, :]
                    else:
                        v = self.r["R" + n][k, i:i + Y2, :]
                    ref[c, 4 + p - dx * X2, Y2 * (1 - dy):Y2 * (2 - dy), :] = v

    def win_sent(self, n):
        for c, dx, dy in self.win_copies(n):
            pl.when(self.exists(dx, dy))(c.wait_send)

    def coefs(self, E, K, a, b, scale):
        E, K = self.r[E], self.r[K]
        Z = E.shape[-1]
        shape = E.shape[-2:]
        R = shape[0]
        s = 1.0 / scale

        @pl.loop(a, b)
        def _(i):
            z = lax.broadcasted_iota(jnp.int32, shape, 1)
            e = E[0, i]

            def face(o):
                t = e + o
                return jnp.where(jnp.minimum(e, o) > 0.0, t * (0.5 * s), t * s)

            zp = jnp.where(z == Z - 1, 0.0, pltpu.roll(e, Z - 1, 1))
            zm = jnp.where(z == 0, 0.0, pltpu.roll(e, 1, 1))
            others = (E[0, i + 1], E[0, i - 1], pltpu.roll(e, R - 1, 0), pltpu.roll(e, 1, 0), zp, zm)
            diag = None
            for k, o in enumerate(others):
                c = face(o)
                diag = c if diag is None else diag + c
                if k == 4:
                    c = jnp.where(z == Z - 1, 0.0, c)
                if k == 5:
                    c = jnp.where(z == 0, 0.0, c)
                K[k, i] = c
            inside = e > 0.0
            K[6, i] = jnp.where(inside, WEIGHT / jnp.where(inside, diag, 1.0), 0.0)
            K[7, i] = diag

    def face(self, E, K, i, o, k, scale):
        e, f = self.r[E][0, i], self.r[E][0, o]
        t, s = e + f, 1.0 / scale
        self.r[K][k, i] = jnp.where(jnp.minimum(e, f) > 0.0, t * (0.5 * s), t * s)

    def stencil(self, V, K, G, i, c, rows):
        R, Z = V.shape[-2:]
        n = rows.stop - rows.start
        v = V[c, i, rows, :]
        if n == R:
            yp, ym = pltpu.roll(v, R - 1, 0), pltpu.roll(v, 1, 0)
        else:
            yp, ym = V[c, i, 1:n + 1, :], pltpu.roll(V[c, i], 1, 0)[:n]
        acc = G[c, i, rows, :]
        parts = (V[c, i + 1, rows, :], V[c, i - 1, rows, :], yp, ym, pltpu.roll(v, Z - 1, 1), pltpu.roll(v, 1, 1))
        for k, o in enumerate(parts):
            acc = acc + K[k, i, rows, :] * o
        return v, acc

    def first(self, K, G, O, a, b, comps=None):
        K, G, O = (self.r[n] for n in (K, G, O))

        @pl.loop(a, b, unroll=2 if (b - a) % 2 == 0 else 1)
        def _(i):
            w = K[6, i]
            for c in comps or range(self.C):
                O[c, i] = w * G[c, i]

    def sweep(self, V, K, G, O, a, b, rows=None, shift=0, comps=None):
        V, K, G = (self.r[n] for n in (V, K, G))
        O = self.r[O] if isinstance(O, str) else O
        rows = rows or slice(0, V.shape[-2])
        out_rows = rows if shift == 0 else slice(0, rows.stop - rows.start)

        @pl.loop(a, b, unroll=True)
        def _(i):
            for c in comps or range(self.C):
                v, acc = self.stencil(V, K, G, i, c, rows)
                O[c, i - shift, out_rows, :] = (1.0 - WEIGHT) * v + K[6, i, rows, :] * acc

    def clear(self):
        r, C, X, Y, X1, Y1 = self.r, self.C, self.X, self.Y, self.X1, self.Y1

        def zero(ref, *idx):
            ref[idx] = jnp.zeros(ref.at[idx].shape, ref.dtype)

        for n, rows in (("E0", Y), ("F0", Y), ("V0", Y), ("E1", Y1), ("F1", Y1), ("V1", Y1), ("G1", 0), ("E2", 0), ("F2", 0), ("A2", 0)):
            ref = r[n]

            @pl.loop(0, ref.shape[1])
            def _(i):
                for c in range(ref.shape[0]):
                    zero(ref, c, i, slice(rows, ref.shape[2]))
        for n, planes in (("V0", (0, 1, X + 2, X + 3)), ("A0", (1, X + 2)), ("F1", (0, X1 + 5)),
                          ("A1", (0, X1 + 5)), ("B1", (0, X1 + 5))):
            for c in range(C):
                for p in planes:
                    zero(r[n], c, p)
        absent = {}

        def when_absent(dx, dy, ref, *idx):
            absent.setdefault((dx, dy), []).append((ref, idx))

        for h in (*self.hE0x, self.hE0, self.hE1, *self.hF0, self.hF1, self.hV1, *self.hV0):
            ref = r[h["target"]]
            for m in h["msgs"]:
                if m[0] == "x" and h["land"]:
                    k = 0 if m[1] > 0 else 1
                    for c in range(h["comps"]):
                        for p in range(h["w"]):
                            when_absent(m[1], 0, r[h["name"] + "_lx"], k, c, p)
                elif m[0] == "x":
                    for c in range(h["base"], h["base"] + h["comps"]):
                        for p in range(m[4], m[4] + h["w"]):
                            when_absent(m[1], 0, ref, c, p, slice(0, h["Y"]))
                elif m[0] == "y":
                    when_absent(0, m[2], r[h["name"] + "_ry"], m[1])
                else:
                    when_absent(*m[2], r[h["name"] + "_rd"], m[1])
        for m in self.aG1["msgs"]:
            when_absent(m[1], m[2], r[m[0] + "_r"], slice(None))
        for k, (dx, t, dy) in enumerate(MEMBERS):
            if dx or dy:
                when_absent(dx, dy, r["Re2"], k)
        for k, (dx, dy) in enumerate(WINDOW):
            for n in ("Rf2", "Rv2"):
                when_absent(dx, dy, r[n], k)
        for k, dy in enumerate(ROWS):
            for t in (0, 1):
                if dy:
                    when_absent(0, dy, r["Rn2"], 3 * t + k)
                when_absent(4 * t - 2, dy, r["Rd2"], 3 * t + k)
        for (dx, dy), spots in absent.items():
            @pl.when(jnp.logical_not(self.exists(-dx, -dy)))
            def _():
                for ref, idx in spots:
                    zero(ref, *idx)

    def edges(self):
        r, C, X, Y, R = self.r, self.C, self.X, self.Y, self.R0
        K = r["C0"]
        for h in self.hF0:
            for c, dx, dy in self.halo_copies(h, "y"):
                pl.when(self.exists(-dx, -dy))(c.wait_recv)
        for c in range(C):
            stage = r[self.hF0[c]["name"] + "_ry"]
            for p in (2, 3, X, X + 1):
                r["D0"][c, p, 0:Y, :] = r["V0"][c, p, 0:Y, :]
                for k, q, f, o in ((0, 0, 3, R - 1), (1, Y - 1, 2, Y)):
                    a = K[6, p, o:o + 1, :] * stage[k, p - 2:p - 1, :]
                    r["D0"][c, p, q:q + 1, :] = r["V0"][c, p, q:q + 1, :] + (
                        K[6, p, q:q + 1, :] * (K[f, p, q:q + 1, :] * a))

    def residual(self, V, K, G, T, px, Xc, ring, a, b):
        V, K, G, T = (self.r[n] for n in (V, K, G, T))
        R = V.shape[-2]
        rows = slice(0, R)
        n = Xc + 2 * ring

        def defect(i, c):
            v, acc = self.stencil(V, K, G, i, c, rows)
            return acc - K[7, i] * v

        @pl.loop(a, b, unroll=True)
        def _(j):
            for c in range(self.C):
                i = px + 2 * j
                start = pl.multiple_of((c * n + j + ring) * R, 8)
                T[pl.ds(start, R), :] = 0.5 * (defect(i, c) + defect(i + 1, c))

    def ring_residual(self, V, K, T, px, Xc, ring):
        V, K, T = (self.r[n] for n in (V, K, T))
        R, n = V.shape[-2], Xc + 2 * ring
        last = px + 2 * Xc + 2 * ring - 2
        for c in range(self.C):
            for near, far, k, j in ((px - 2 * ring + 1, px - 2 * ring, 0, 0), (last, last + 1, 1, n - 1)):
                start = (c * n + j) * R
                if ring == 1:
                    step = 1 if k == 0 else -1
                    v = V[c, near]
                    acc = K[k, near] * V[c, near + step] - K[7, near] * v + K[k, far] * v
                    for f, o in ((2, pltpu.roll(v, R - 1, 0)), (3, pltpu.roll(v, 1, 0)),
                                 (4, pltpu.roll(v, v.shape[1] - 1, 1)), (5, pltpu.roll(v, 1, 1))):
                        acc = acc + K[f, near] * o
                else:
                    acc = K[k, near] * V[c, near + (1 if k == 0 else -1)]
                T[start:start + R, :] = 0.5 * acc

    def spread(self, V, K, G, i, o, k):
        V, K, O = (self.r[n] for n in (V, K, G))
        for c in range(self.C):
            O[c, i] = K[6, i] * (K[k, i] * V[c, o])

    def dot(self, a, b):
        return lax.dot_general(a, b, (((1,), (0,)), ((), ())), preferred_element_type=jnp.float32)

    def split(self, t):
        hi = t.astype(jnp.bfloat16)
        return hi, (t - hi.astype(jnp.float32)).astype(jnp.bfloat16)

    def right(self, t, m):
        hi, lo = self.split(t)
        return self.dot(hi, m) + self.dot(lo, m)

    def left(self, m, t):
        hi, lo = self.split(t)
        return self.dot(m, hi) + self.dot(m, lo)

    def pairs(self, n, m, value, fine_dim):
        r = lax.broadcasted_iota(jnp.int32, (n, m), 0)
        c = lax.broadcasted_iota(jnp.int32, (n, m), 1)
        hit = (r >> 1) == c if fine_dim == 0 else (c >> 1) == r
        return jnp.where(hit, value, 0.0).astype(jnp.bfloat16)

    def squeeze(self, t):
        rows, Z = t.shape
        half = self.right(t, self.pairs(Z, Z // 2, 0.5, 0))
        return self.left(self.pairs(rows // 2, rows, 0.5, 1), half)

    def squeeze0(self, n):
        T, Z, R, R1, Y1 = self.r["T0"], self.Z, self.R0, self.R1, self.Y1
        half = self.right(T[...], self.pairs(Z, Z // 2, 0.5, 0))
        o = lax.broadcasted_iota(jnp.int32, (n * R1, n * R), 0)
        f = lax.broadcasted_iota(jnp.int32, (n * R1, n * R), 1)
        bo, bf = jnp.zeros_like(o), jnp.zeros_like(f)
        for k in range(1, n):
            bo = bo + (o >= k * R1).astype(jnp.int32)
            bf = bf + (f >= k * R).astype(jnp.int32)
        q = o - bo * R1
        q = jnp.where(q <= Y1, q, jnp.where(q == R1 - 1, R // 2 - 1, -1))
        m = jnp.where((bo == bf) & (((f - bf * R) >> 1) == q), 0.5, 0.0).astype(jnp.bfloat16)
        return [self.left(m, half[c * n * R:(c + 1) * n * R]) for c in range(self.C)]

    def prolong(self, W, a, count, U, V, planes, coarse_of, offset, shift=0, widen=True):
        W, U, V = (self.r[n] for n in (W, U, V))
        C, _, Rc, Zc = W.shape
        Rf, Zf = V.shape[-2:]
        if widen:
            src = W[:, pl.ds(a + shift, count)].reshape(C * count * Rc, Zc)
            U[...] = self.right(src, self.pairs(Zc, Zf, 1.0, 1))
        r = lax.broadcasted_iota(jnp.int32, (Rf, Rc), 0)
        c = lax.broadcasted_iota(jnp.int32, (Rf, Rc), 1)
        r = jnp.where(r < Rf - 4, r, r - Rf)
        c = c - offset if offset else jnp.where(c < Rc - 4, c, c - Rc)
        lift = jnp.where((r >> 1) == c, 1.0, 0.0).astype(jnp.bfloat16)
        for comp in range(C):
            for k in range(count):
                if not any(coarse_of(p) == a + k for p in planes):
                    continue
                start = (comp * count + k) * Rc
                block = self.left(lift, U[start:start + Rc, :])
                for p in planes:
                    if coarse_of(p) == a + k:
                        V[comp, p] = V[comp, p] + block

    def body(self, forcing, phase, out, *scratch):
        names = list(self.scratch)
        self.r = r = dict(zip(names, scratch))
        self.ssem, self.rsem, lsem = scratch[len(names):]
        self.gx, self.gy = lax.axis_index("gx"), lax.axis_index("gy")
        self.m = lax.rem(self.gx, 2)
        X, Y, Z, C = self.X, self.Y, self.Z, self.C
        X1, Y1 = self.X1, self.Y1
        block = (pl.ds(2, X), pl.ds(TOP, Y))
        load_p = pltpu.make_async_copy(phase, r["ph"], lsem.at[0])
        load_p.start()
        load_f = pltpu.make_async_copy(forcing, r["F0"].at[:, block[0], block[1], :], lsem.at[1])
        load_f.start()

        barrier = pltpu.get_barrier_semaphore()
        count = jnp.int32(0)
        for dx, t, dy in MEMBERS:
            ok = self.exists(dx, dy) if dx or dy else self.gx >= 0
            count = count + ok.astype(jnp.int32)

            @pl.when(ok)
            def _():
                pl.semaphore_signal(barrier, inc=1, device_id=(self.gx + dx + t * (1 - 2 * self.m), self.gy + dy),
                                    device_id_type=MESH)
        self.clear()
        load_p.wait()

        @pl.loop(0, X)
        def _(i):
            ph = r["ph"][i]
            e = jnp.zeros(ph.shape, jnp.float32)
            for k, value in enumerate(VISCOSITIES):
                e = jnp.where(ph == k, jnp.float32(value), e)
            r["E0"][0, i + 2, TOP:TOP + Y, :] = e
        pl.semaphore_wait(barrier, count)
        self.halo_start(self.hE0x[0])
        self.halo_start(self.hE0)
        load_f.wait()
        for h in self.hF0:
            self.halo_start(h, "y")

        for j in range(X1):
            r["T0"][j * Y:(j + 1) * Y, :] = 0.5 * (
                r["E0"][0, 2 + 2 * j, TOP:TOP + Y, :] + r["E0"][0, 3 + 2 * j, TOP:TOP + Y, :])
        e1 = self.squeeze(r["T0"][0:X1 * Y, :])
        for j in range(X1):
            r["E1"][0, 3 + j, TOP:TOP + Y1, :] = e1[j * Y1:(j + 1) * Y1]
        for j in range(self.X2):
            r["T1"][j * Y1:(j + 1) * Y1, :] = 0.5 * (
                e1[2 * j * Y1:(2 * j + 1) * Y1] + e1[(2 * j + 1) * Y1:(2 * j + 2) * Y1])
        r["Se2"][...] = self.squeeze(r["T1"][0:self.X2 * Y1, :])

        self.halo_start(self.hE1)
        self.halo_start(self.hE0x[1])
        self.member_start()
        for h in self.hF0:
            self.halo_start(h, "x")
        X2, Y2, R1 = self.X2, self.Y2, self.R1
        self.halo_wait(self.hE0, "y")
        self.coefs("E0", "C0", 3, X + 1, 1.0)
        self.first("C0", "F0", "A0", 3, X + 1)
        self.sweep("A0", "C0", "F0", "V0", 4, X)
        self.halo_wait(self.hE0x[0])
        self.halo_wait(self.hE0, "d")
        for p in (2, X + 1):
            self.coefs("E0", "C0", p, p + 1, 1.0)
            self.first("C0", "F0", "A0", p, p + 1)
        self.sweep("A0", "C0", "F0", "V0", 2, 4)
        self.sweep("A0", "C0", "F0", "V0", X, X + 2)
        self.residual("V0", "C0", "F0", "T0", 2, X1, 1, 1, X1 - 1)
        self.halo_wait(self.hE1)
        self.coefs("E1", "C1", 1, X1 + 5, 4.0)
        self.face("E1", "C1", 0, 1, 0, 4.0)
        self.face("E1", "C1", X1 + 5, X1 + 4, 1, 4.0)
        self.halo_wait(self.hE0x[1])
        for p, o, k in ((1, 0, 0), (X + 2, X + 3, 1)):
            self.coefs("E0", "C0", p, p + 1, 1.0)
            self.face("E0", "C0", o, p, k, 1.0)
        self.spread("A0", "C0", "V0", 1, 2, 0)
        self.spread("A0", "C0", "V0", X + 2, X + 1, 1)
        self.edges()
        self.residual("V0", "C0", "F0", "T0", 2, X1, 1, 0, 1)
        self.residual("V0", "C0", "F0", "T0", 2, X1, 1, X1 - 1, X1)
        self.ring_residual("V0", "C0", "T0", 2, X1, 1)
        for c, f1 in enumerate(self.squeeze0(X1 + 2)):
            for j in range(X1 + 2):
                r["G1"][c, 2 + j] = f1[j * R1:(j + 1) * R1]
        self.ring_start(self.aG1)

        self.first("C1", "G1", "A1", 1, X1 + 5)
        self.sweep("A1", "C1", "G1", "B1", 1, X1 + 5)
        self.residual("B1", "C1", "G1", "T1", 3, X2, 2, -1, X2 + 1)
        self.ring_residual("B1", "C1", "T1", 3, X2, 2)
        f2 = self.squeeze(r["T1"][...])
        n = self.R1 // 2
        for c in range(C):
            for j in range(X2 + 4):
                s = (c * (X2 + 4) + j) * n
                r["Q2"][c, j] = f2[s:s + n]
        self.share_start()

        self.ring_wait(self.aG1)
        for c in range(C):
            for j in range(X1):
                r["F1"][c, 3 + j, 0:Y1, :] = r["G1"][c, 3 + j, 0:Y1, :]
        self.ring_add(self.aG1, lambda c, p, q, k: (r["F1"], (c, 3 + p, slice(q, q + k))))
        self.halo_start(self.hF1)

        for h in self.hF0:
            self.halo_wait(h, "x")
            self.halo_place(h)
        rows0 = slice(TOP, TOP + Y)
        self.first("C0", "F0", "A0", 1, X + 3)
        self.sweep("A0", "C0", "F0", "V0", 2, X + 2, rows0)
        for h in self.hV0:
            self.halo_start(h, "yd")

        self.share_wait()
        self.win_start("f2")
        self.halo_start(self.hV0[0], "x")

        self.halo_wait(self.hF1)
        self.first("C1", "F1", "A1", 1, X1 + 5)
        self.sweep("A1", "C1", "F1", "B1", 2, X1 + 4)
        for c in range(C):
            for j in range(X1):
                r["V1"][c, 3 + j, TOP:TOP + Y1, :] = r["B1"][c, 3 + j, TOP:TOP + Y1, :]
            for dx in (2, X1 + 3):
                r["V1"][c, dx, 0:Y1, :] = r["B1"][c, dx, 0:Y1, :]
            for j in range(-1, X1 + 1):
                for q in (self.R1 - 1, Y1):
                    r["V1"][c, 3 + j, q:q + 1, :] = r["B1"][c, 3 + j, q:q + 1, :]
        self.halo_start(self.hV1)

        self.member_wait()
        self.coefs("E2", "C2", 1, self.P2 - 1, 16.0)
        self.win_wait("f2", "F2")
        p2 = self.P2
        self.first("C2", "F2", "A2", 1, p2 - 1)
        self.sweep("A2", "C2", "F2", "B2", 2, p2 - 2)
        self.sweep("B2", "C2", "F2", "A2", 3, p2 - 3)
        self.sweep("A2", "C2", "F2", "B2", 4, p2 - 4)
        for c in range(C):
            for p in range(2 * self.X2):
                i = (c * 2 * self.X2 + p) * self.Y2
                r["Sv2"][i:i + self.Y2, :] = r["B2"][c, 4 + p, self.Y2:2 * self.Y2, :]
        self.win_start("v2")
        self.halo_start(self.hV0[1], "x")
        self.halo_start(self.hV0[2], "x")
        self.win_wait("v2", "A2")
        self.sweep("A2", "C2", "F2", "B2", 1, p2 - 1)
        self.sweep("B2", "C2", "F2", "A2", 2, p2 - 2)

        self.halo_wait(self.hV1)
        self.halo_sent(self.hV1)
        self.prolong("A2", 2, self.X2 + 4, "UZ1", "V1", range(self.P1),
                     lambda p: 4 + (p - 3) // 2, self.Y2, self.m * self.X2)
        self.sweep("V1", "C1", "F1", "A1", 1, X1 + 5)
        self.sweep("A1", "C1", "F1", "B1", 2, X1 + 4)

        for h in self.hV0:
            self.halo_wait(h, "yd")
            self.halo_sent(h, "yd")
        own = range(2, X + 2)
        ends = (0, 1, X + 2, X + 3)
        self.prolong("B1", 2, X1 + 2, "UZ0", "V0", own, lambda p: 3 + (p - 2) // 2, 0)
        self.sweep("V0", "C0", "F0", "B0", 3, X + 1)
        for c, h in enumerate(self.hV0):
            self.halo_wait(h, "x")
            lx, V = r[h["name"] + "_lx"], r["V0"]
            V[c, 0, 0:Y, :] = lx[0, 0, 0]
            V[c, 1, 0:Y, :] = V[c, 1, 0:Y, :] + lx[0, 0, 1]
            V[c, X + 2, 0:Y, :] = V[c, X + 2, 0:Y, :] + lx[1, 0, 0]
            V[c, X + 3, 0:Y, :] = lx[1, 0, 1]
        self.prolong("B1", 2, X1 + 2, "UZ0", "V0", ends, lambda p: 3 + (p - 2) // 2, 0, widen=False)
        self.sweep("V0", "C0", "F0", "B0", 1, 3)
        self.sweep("V0", "C0", "F0", "B0", X + 1, X + 3)
        self.sweep("B0", "C0", "F0", out, 2, X + 2, rows0, shift=2)
        for h in (self.hE0, *self.hE0x, *self.hF0, self.hE1, self.hF1):
            self.halo_sent(h)
        for h in self.hV0:
            self.halo_sent(h, "x")
        self.ring_sent(self.aG1)
        self.share_sent()
        self.member_sent()
        for n in ("f2", "v2"):
            self.win_sent(n)

    def __call__(self, forcing, phase):
        any_space = pl.BlockSpec(memory_space=pl.ANY)
        sems = [pltpu.SemaphoreType.DMA((self.n_sems,)), pltpu.SemaphoreType.DMA((self.n_sems,)),
                pltpu.SemaphoreType.DMA((2,))]
        return pl.pallas_call(
            self.body,
            out_shape=pltpu.VMEM(forcing.shape, jnp.float32),
            in_specs=[any_space, any_space],
            out_specs=pl.BlockSpec(memory_space=pltpu.VMEM),
            scratch_shapes=list(self.scratch.values()) + sems,
            compiler_params=pltpu.CompilerParams(
                collective_id=0, has_side_effects=True, vmem_limit_bytes=60 * 1024 * 1024),
            name="vcycle",
        )(forcing, phase)


def solution(mesh):
    grid = (mesh.shape["gx"], mesh.shape["gy"])

    def per_device(forcing, phase_ids):
        return Kernel(phase_ids.shape, forcing.shape[0], grid)(forcing, phase_ids)

    return jax.shard_map(
        per_device,
        mesh=mesh,
        in_specs=(P(None, "gx", "gy", None), P("gx", "gy", None)),
        out_specs=P(None, "gx", "gy", None),
        check_vma=False,
    )
```

```python
import functools

import jax
import jax.numpy as jnp
from jax import lax
from jax.experimental import pallas as pl
from jax.experimental.pallas import tpu as pltpu
from jax.sharding import PartitionSpec as P

COARSE_SWEEPS = 6
VISCOSITIES = (0.2, 0.6, 1.5, 4.0)
WEIGHT = 2.0 / 3.0
MESH = pl.DeviceIdType.MESH
WINDOW = [(dx, dy) for dx in (-2, 0, 2) for dy in (-1, 0, 1) if (dx, dy) != (0, 0)]
MEMBERS = [(dx, t, dy) for dx in (-2, 0, 2) for t in (0, 1) for dy in (-1, 0, 1) if (dx, t, dy) != (0, 0, 0)]
ROWS = (0, 1, -1)
TOP = 0


def up8(n):
    return -(-n // 8) * 8


def side_slices(step, first, length, lo, hi):
    if step > 0:
        return (first + length - hi, first - hi)
    return (first + lo - 1, first + length + lo - 1)


class Kernel:
    def __init__(self, sizes, comps, grid):
        self.X, self.Y, self.Z = sizes
        self.C = comps
        self.grid = grid
        self.scratch = {}
        self.n_sems = 0
        self.plan()

    def buf(self, name, shape, dtype=jnp.float32):
        self.scratch[name] = pltpu.VMEM(tuple(shape), dtype)

    def halo(self, name, target, comps, px, X, Y, Z, lo, hi, diag, base=0, land=None, only="xyd"):
        w = hi - lo + 1
        msgs = []
        for dx in (1, -1) if "x" in only else ():
            s, d = side_slices(dx, px, X, lo, hi)
            msgs.append(("x", dx, 0, s, d, self.n_sems))
            self.n_sems += 1
        n = comps * X * w
        if "y" in only:
            self.buf(name + "_sy", (2, up8(n), Z))
            self.buf(name + "_ry", (2, up8(n), Z))
        for k, dy in enumerate((1, -1)) if "y" in only else ():
            s, d = side_slices(dy, TOP, Y, lo, hi)
            d %= Y + 8
            msgs.append(("y", k, dy, s, d, self.n_sems))
            self.n_sems += 1
        if diag:
            n = comps * len(diag)
            self.buf(name + "_sd", (4, n, 1, Z))
            self.buf(name + "_rd", (4, n, 1, Z))
            for k, (dx, dy) in enumerate([(1, 1), (1, -1), (-1, 1), (-1, -1)]):
                cells = [[], []]
                for a, b in diag:
                    sx, tx = side_slices(dx, px, X, a, a)
                    sy, ty = side_slices(dy, TOP, Y, b, b)
                    cells[0].append((sx, sy))
                    cells[1].append((tx, ty % (Y + 8)))
                msgs.append(("d", k, (dx, dy), cells[0], cells[1], self.n_sems))
                self.n_sems += 1
        if land:
            self.buf(name + "_lx", (2, comps, w, Y, Z))
        return dict(name=name, land=land, base=base, target=target, comps=comps, px=px, X=X, Y=Y, w=w, diag=diag, msgs=msgs)

    def ring(self, name, source, px, X, Y, Z, w):
        C = self.C
        dirs = [(dx, dy) for dx in (0, 1, -1) for dy in (0, 1, -1) if (dx, dy) != (0, 0)]
        msgs = []
        for dx, dy in dirs:
            px_count, rows = (w if dx else X), (w if dy else Y)
            key = "%s_%d%d" % (name, dx + 1, dy + 1)
            n = up8(C * px_count * rows)
            self.buf(key + "_s", (n, Z))
            self.buf(key + "_r", (n, Z))
            out = (px + (X if dx > 0 else -w if dx < 0 else 0), Y if dy > 0 else -w if dy < 0 else 0)
            into = (X - w if dx < 0 else 0, Y - w if dy < 0 else 0)
            msgs.append((key, dx, dy, px_count, rows, out, into, self.n_sems))
            self.n_sems += 1
        return dict(source=source, msgs=msgs)

    def plan(self):
        X, Y, Z, C = self.X, self.Y, self.Z, self.C
        self.P0, self.R0 = X + 4, Y + 8
        self.X1, self.Y1, self.Z1 = X // 2, Y // 2, Z // 2
        self.P1, self.R1 = self.X1 + 6, self.Y1 + 8
        self.X2, self.Y2, self.Z2 = X // 4, Y // 4, Z // 4
        self.P2, self.R2 = 2 * self.X2 + 8, up8(self.Y2 * 3)
        b = self.buf
        b("ph", (X, Y, Z), jnp.int32)
        b("E0", (1, self.P0, self.R0, Z))
        b("C0", (8, self.P0, self.R0, Z))
        for n in ("F0", "A0", "V0", "B0", "D0"):
            b(n, (C, self.P0, self.R0, Z))
        b("T0", (C * (self.X1 + 2) * self.R0, Z))
        b("E1", (1, self.P1, self.R1, self.Z1))
        b("C1", (8, self.P1, self.R1, self.Z1))
        for n in ("F1", "G1", "A1", "V1", "B1"):
            b(n, (C, self.P1, self.R1, self.Z1))
        b("T1", (C * (self.X2 + 4) * self.R1, self.Z1))
        b("E2", (1, self.P2, self.R2, self.Z2))
        b("C2", (8, self.P2, self.R2, self.Z2))
        for n in ("F2", "A2", "B2"):
            b(n, (C, self.P2, self.R2, self.Z2))
        blk = self.X2 * self.Y2
        b("Se2", (blk, self.Z2))
        b("Re2", (len(MEMBERS), blk, self.Z2))
        for n in ("f2", "v2"):
            b("S" + n, (2 * C * blk, self.Z2))
            b("R" + n, (len(WINDOW), 2 * C * blk, self.Z2))
        near, far = up8(C * (self.X2 + 2) * self.Y2), up8(C * 2 * self.Y2)
        b("Sn2", (3, near, self.Z2))
        b("Rn2", (6, near, self.Z2))
        b("Sd2", (3, far, self.Z2))
        b("Rd2", (6, far, self.Z2))
        b("W2", (C, 2 * self.X2, 8, self.Z2))
        b("Q2", (C, self.X2 + 4, self.R1 // 2, self.Z2))
        b("UZ1", (self.R2 * C * (self.X2 + 4), self.Z1))
        b("UZ0", (self.R1 * C * (self.X1 + 2), self.Z))
        reach = [(1, 1), (1, 2), (2, 1), (1, 3), (2, 2), (3, 1)]
        self.hE0 = self.halo("hE0", "E0", 1, 2, X, Y, Z, 1, 2, [(1, 1)], only="yd")
        self.hE0x = [self.halo("hE0x%d" % k, "E0", 1, 2, X, Y, Z, k, k, [], only="x") for k in (1, 2)]
        self.hF0 = [self.halo("hFc%d" % c, "F0", 1, 2, X, Y, Z, 1, 1, [], c) for c in range(C)]
        self.hV0 = [self.halo("hVc%d" % c, "V0", 1, 2, X, Y, Z, 1, 2, [(1, 1)], c, "D0") for c in range(C)]
        self.hE1 = self.halo("hE1", "E1", 1, 3, self.X1, self.Y1, self.Z1, 1, 3, reach)
        self.hF1 = self.halo("hF1", "F1", C, 3, self.X1, self.Y1, self.Z1, 1, 2, reach[:3])
        self.hV1 = self.halo("hV1", "V1", C, 3, self.X1, self.Y1, self.Z1, 2, 3, reach[1:])
        self.aG1 = self.ring("aG1", "G1", 3, self.X1, self.Y1, self.Z1, 1)
        self.win = {}
        for n, k in (("e2", len(MEMBERS)), ("f2", len(WINDOW)), ("v2", len(WINDOW)), ("n2", 6), ("d2", 6)):
            self.win[n] = self.n_sems
            self.n_sems += k

    def exists(self, dx, dy):
        ok = None
        for step, me, size in ((dx, self.gx, self.grid[0]), (dy, self.gy, self.grid[1])):
            if step:
                t = (me + step >= 0) & (me + step < size)
                ok = t if ok is None else ok & t
        return ok

    def copy(self, src, dst, sem, dx, dy, into=None):
        into = sem if into is None else into
        return pltpu.make_async_remote_copy(
            src_ref=src, dst_ref=dst, send_sem=self.ssem.at[sem], recv_sem=self.rsem.at[into],
            device_id=(self.gx + dx, self.gy + dy), device_id_type=MESH)

    def halo_copies(self, h, kinds="xyd"):
        r = self.r
        ref = r[h["target"]]
        rows = pl.ds(TOP, h["Y"])
        out = []
        for m in h["msgs"]:
            if m[0] not in kinds:
                continue
            if m[0] == "x":
                _, dx, dy, s, d, sem = m
                comps = pl.ds(h["base"], h["comps"])
                src, dst = ref, ref.at[comps, pl.ds(d, h["w"]), rows, :]
                if h["land"]:
                    src, dst = r[h["land"]], r[h["name"] + "_lx"].at[0 if dx > 0 else 1]
                c = self.copy(src.at[comps, pl.ds(s, h["w"]), rows, :], dst, sem, dx, 0)
                out.append((c, dx, 0))
            elif m[0] == "y":
                _, k, dy, s, d, sem = m
                out.append((self.copy(r[h["name"] + "_sy"].at[k], r[h["name"] + "_ry"].at[k], sem, 0, dy), 0, dy))
            else:
                _, k, (dx, dy), _, _, sem = m
                out.append((self.copy(r[h["name"] + "_sd"].at[k], r[h["name"] + "_rd"].at[k], sem, dx, dy), dx, dy))
        return out

    def rows_of(self, h, m, which):
        if m[0] == "y":
            start = m[3 + which]
            return m[1], "y", [(c + h["base"], h["px"] + p, start + q) for c in range(h["comps"])
                               for p in range(h["X"]) for q in range(h["w"])]
        return m[1], "d", [(c + h["base"], p, q) for c in range(h["comps"]) for p, q in m[3 + which]]

    def halo_start(self, h, kinds="xyd"):
        ref = self.r[h["target"]]
        for m in h["msgs"]:
            if m[0] == "x" or m[0] not in kinds:
                continue
            k, kind, rows = self.rows_of(h, m, 0)
            stage = self.r[h["name"] + "_s" + kind]
            for i, (c, p, q) in enumerate(rows):
                row = ref[c, p, q:q + 1, :]
                if kind == "d":
                    stage[k, i] = row
                else:
                    stage[k, i:i + 1, :] = row
        for c, dx, dy in self.halo_copies(h, kinds):
            pl.when(self.exists(dx, dy))(c.start)

    def halo_wait(self, h, kinds="xyd"):
        for c, dx, dy in self.halo_copies(h, kinds):
            pl.when(self.exists(-dx, -dy))(c.wait_recv)
        self.halo_place(h, kinds)

    def halo_place(self, h, kinds="xyd"):
        ref = self.r[h["target"]]
        for m in h["msgs"]:
            if m[0] == "x" or m[0] not in kinds:
                continue
            k, kind, rows = self.rows_of(h, m, 1)
            stage = self.r[h["name"] + "_r" + kind]
            for i, (c, p, q) in enumerate(rows):
                ref[c, p, q:q + 1, :] = stage[k, i] if kind == "d" else stage[k, i:i + 1, :]

    def halo_sent(self, h, kinds="xyd"):
        for c, dx, dy in self.halo_copies(h, kinds):
            pl.when(self.exists(dx, dy))(c.wait_send)

    def ring_copies(self, h):
        r = self.r
        return [(self.copy(r[m[0] + "_s"], r[m[0] + "_r"], m[7], m[1], m[2]), m[1], m[2]) for m in h["msgs"]]

    def ring_start(self, h):
        S = self.r[h["source"]]
        for key, dx, dy, planes, rows, (p, q), _, _ in h["msgs"]:
            q %= S.shape[2]
            i = 0
            for c in range(self.C):
                for k in range(planes):
                    self.r[key + "_s"][i:i + rows, :] = S[c, p + k, q:q + rows, :]
                    i += rows
        for c, dx, dy in self.ring_copies(h):
            pl.when(self.exists(dx, dy))(c.start)

    def ring_wait(self, h):
        for c, dx, dy in self.ring_copies(h):
            pl.when(self.exists(-dx, -dy))(c.wait_recv)

    def ring_add(self, h, place):
        for key, dx, dy, planes, rows, _, (p, q), _ in h["msgs"]:
            i = 0
            for c in range(self.C):
                for k in range(planes):
                    ref, idx = place(c, p + k, q, rows)
                    ref[idx] = ref[idx] + self.r[key + "_r"][i:i + rows, :]
                    i += rows

    def ring_sent(self, h):
        for c, dx, dy in self.ring_copies(h):
            pl.when(self.exists(dx, dy))(c.wait_send)

    def when(self, dx, dy, f):
        if (dx, dy) == (0, 0):
            f()
        else:
            pl.when(self.exists(dx, dy))(f)

    def member_copies(self):
        r = self.r
        return [(self.copy(r["Se2"], r["Re2"].at[k], self.win["e2"] + k, dx + t * (1 - 2 * self.m), dy), dx, t, dy)
                for k, (dx, t, dy) in enumerate(MEMBERS)]

    def member_start(self):
        for c, dx, t, dy in self.member_copies():
            self.when(dx, dy, c.start)

    def member_wait(self):
        for c, dx, t, dy in self.member_copies():
            self.when(-dx, -dy, c.wait_recv)
        E, X2, Y2 = self.r["E2"], self.X2, self.Y2
        for k, (dx, t, dy) in enumerate(MEMBERS + [(0, 0, 0)]):
            member = 1 - self.m if t else self.m
            for p in range(X2):
                v = self.r["Se2"][p * Y2:(p + 1) * Y2] if k == len(MEMBERS) else self.r["Re2"][k, p * Y2:(p + 1) * Y2]
                E[0, 4 + p - dx * X2 + member * X2, Y2 * (1 - dy):Y2 * (2 - dy), :] = v

    def member_sent(self):
        for c, dx, t, dy in self.member_copies():
            self.when(dx, dy, c.wait_send)

    def near_copies(self):
        r, b = self.r, self.win["n2"]
        return [(self.copy(r["Sn2"].at[k], r["Rn2"].at[3 * t + k], b + 3 * t + k, t * (1 - 2 * self.m), dy), t, k, dy)
                for t in (1, 0) for k, dy in enumerate(ROWS) if (t, dy) != (0, 0)]

    def far_sends(self):
        r, b, m = self.r, self.win["d2"], self.m
        return [(self.copy(r["Sd2"].at[k], r["Rd2"].at[3 * m + k], b + 3 * t + k, (2 * m - 1) * (2 - t), dy, b + 3 * m + k), dy)
                for t in (1, 0) for k, dy in enumerate(ROWS)]

    def far_recvs(self):
        r, b = self.r, self.win["d2"]
        return [(self.copy(r["Sd2"].at[k], r["Rd2"].at[3 * s + k], b + 3 * s + k, 2, dy), 2 - 4 * s, k, dy)
                for s in (0, 1) for k, dy in enumerate(ROWS)]

    def far_exists(self, dy):
        x = self.gx + 2 * (2 * self.m - 1)
        ok = (x >= 0) & (x < self.grid[0])
        return ok & self.exists(0, dy) if dy else ok

    def share_start(self):
        r, C, X2, Y2 = self.r, self.C, self.X2, self.Y2
        Q = r["Q2"]
        R = Q.shape[2]
        for k, dy in enumerate(ROWS):
            q, n = ((0, Y2), (Y2, 2), (R - 2, 2))[k]
            i = 0
            for c in range(C):
                for p in range(X2 + 2):
                    r["Sn2"][k, i:i + n, :] = Q[c, 2 * (1 - self.m) + p, q:q + n, :]
                    i += n
            i = 0
            for c in range(C):
                for p in range(2):
                    r["Sd2"][k, i:i + n, :] = Q[c, self.m * (X2 + 2) + p, q:q + n, :]
                    i += n
        for c, t, k, dy in self.near_copies():
            self.when(0, dy, c.start)
        for c, dy in self.far_sends():
            pl.when(self.far_exists(dy))(c.start)

    def share_wait(self):
        r, C, X2, Y2 = self.r, self.C, self.X2, self.Y2
        W, Q = r["W2"], r["Q2"]
        for c, t, k, dy in self.near_copies():
            self.when(0, -dy, c.wait_recv)
        for c, dx, k, dy in self.far_recvs():
            self.when(dx, -dy, c.wait_recv)
        W[...] = jnp.zeros(W.shape, jnp.float32)
        spots = ((0, Y2), (0, 2), (Y2 - 2, 2))
        base = [0, 0] if X2 == 2 else [self.m * (X2 - 2), (1 - self.m) * (X2 - 2)]
        for c in range(C):
            for p in range(X2 + 2):
                W[c, base[0] + p, 0:Y2, :] = W[c, base[0] + p, 0:Y2, :] + Q[c, 2 * (1 - self.m) + p, 0:Y2, :]
        for _, t, k, dy in self.near_copies():
            q, n = spots[k]
            for c in range(C):
                for p in range(X2 + 2):
                    i = (c * (X2 + 2) + p) * n
                    W[c, base[t] + p, q:q + n, :] = W[c, base[t] + p, q:q + n, :] + r["Rn2"][3 * t + k, i:i + n, :]
        for s in (0, 1):
            for k, dy in enumerate(ROWS):
                q, n = spots[k]
                for c in range(C):
                    for p in range(2):
                        i, o = (c * 2 + p) * n, (p if s else 2 * X2 - 2 + p)
                        W[c, o, q:q + n, :] = W[c, o, q:q + n, :] + r["Rd2"][3 * s + k, i:i + n, :]
        for c in range(C):
            for p in range(2 * X2):
                i = (c * 2 * X2 + p) * Y2
                r["Sf2"][i:i + Y2, :] = W[c, p, 0:Y2, :]

    def share_sent(self):
        for c, t, k, dy in self.near_copies():
            self.when(0, dy, c.wait_send)
        for c, dy in self.far_sends():
            pl.when(self.far_exists(dy))(c.wait_send)

    def win_copies(self, n):
        src, dst = self.r["S" + n], self.r["R" + n]
        return [(self.copy(src, dst.at[k], self.win[n] + k, dx, dy), dx, dy) for k, (dx, dy) in enumerate(WINDOW)]

    def win_start(self, n):
        for c, dx, dy in self.win_copies(n):
            pl.when(self.exists(dx, dy))(c.start)

    def win_wait(self, n, target):
        copies = self.win_copies(n)
        for c, dx, dy in copies:
            pl.when(self.exists(-dx, -dy))(c.wait_recv)
        ref = self.r[target]
        X2, Y2 = self.X2, self.Y2
        for k, (dx, dy) in enumerate(WINDOW + [(0, 0)]):
            for c in range(ref.shape[0]):
                for p in range(2 * X2):
                    i = (c * 2 * X2 + p) * Y2
                    if (dx, dy) == (0, 0):
                        v = self.r["S" + n][i:i + Y2, :]
                    else:
                        v = self.r["R" + n][k, i:i + Y2, :]
                    ref[c, 4 + p - dx * X2, Y2 * (1 - dy):Y2 * (2 - dy), :] = v

    def win_sent(self, n):
        for c, dx, dy in self.win_copies(n):
            pl.when(self.exists(dx, dy))(c.wait_send)

    def coefs(self, E, K, a, b, scale):
        E, K = self.r[E], self.r[K]
        Z = E.shape[-1]
        shape = E.shape[-2:]
        R = shape[0]
        s = 1.0 / scale

        @pl.loop(a, b)
        def _(i):
            z = lax.broadcasted_iota(jnp.int32, shape, 1)
            e = E[0, i]

            def face(o):
                t = e + o
                return jnp.where(jnp.minimum(e, o) > 0.0, t * (0.5 * s), t * s)

            zp = jnp.where(z == Z - 1, 0.0, pltpu.roll(e, Z - 1, 1))
            zm = jnp.where(z == 0, 0.0, pltpu.roll(e, 1, 1))
            others = (E[0, i + 1], E[0, i - 1], pltpu.roll(e, R - 1, 0), pltpu.roll(e, 1, 0), zp, zm)
            diag = None
            for k, o in enumerate(others):
                c = face(o)
                diag = c if diag is None else diag + c
                if k == 4:
                    c = jnp.where(z == Z - 1, 0.0, c)
                if k == 5:
                    c = jnp.where(z == 0, 0.0, c)
                K[k, i] = c
            inside = e > 0.0
            K[6, i] = jnp.where(inside, WEIGHT / jnp.where(inside, diag, 1.0), 0.0)
            K[7, i] = diag

    def face(self, E, K, i, o, k, scale):
        e, f = self.r[E][0, i], self.r[E][0, o]
        t, s = e + f, 1.0 / scale
        self.r[K][k, i] = jnp.where(jnp.minimum(e, f) > 0.0, t * (0.5 * s), t * s)

    def stencil(self, V, K, G, i, c, rows):
        R, Z = V.shape[-2:]
        n = rows.stop - rows.start
        v = V[c, i, rows, :]
        if n == R:
            yp, ym = pltpu.roll(v, R - 1, 0), pltpu.roll(v, 1, 0)
        else:
            yp, ym = V[c, i, 1:n + 1, :], pltpu.roll(V[c, i], 1, 0)[:n]
        acc = G[c, i, rows, :]
        parts = (V[c, i + 1, rows, :], V[c, i - 1, rows, :], yp, ym, pltpu.roll(v, Z - 1, 1), pltpu.roll(v, 1, 1))
        for k, o in enumerate(parts):
            acc = acc + K[k, i, rows, :] * o
        return v, acc

    def first(self, K, G, O, a, b, comps=None):
        K, G, O = (self.r[n] for n in (K, G, O))

        @pl.loop(a, b, unroll=2 if (b - a) % 2 == 0 else 1)
        def _(i):
            w = K[6, i]
            for c in comps or range(self.C):
                O[c, i] = w * G[c, i]

    def sweep(self, V, K, G, O, a, b, rows=None, shift=0, comps=None, off=0):
        V, K, G = (self.r[n] for n in (V, K, G))
        O = self.r[O] if isinstance(O, str) else O
        rows = rows or slice(0, V.shape[-2])
        out_rows = rows if shift == 0 else slice(0, rows.stop - rows.start)

        @pl.loop(a, b, unroll=True)
        def _(i):
            i = i + off
            for c in comps or range(self.C):
                v, acc = self.stencil(V, K, G, i, c, rows)
                O[c, i - shift, out_rows, :] = (1.0 - WEIGHT) * v + K[6, i, rows, :] * acc

    def clear(self):
        r, C, X, Y, X1, Y1 = self.r, self.C, self.X, self.Y, self.X1, self.Y1

        def zero(ref, *idx):
            ref[idx] = jnp.zeros(ref.at[idx].shape, ref.dtype)

        for n, rows in (("E0", Y), ("F0", Y), ("V0", Y), ("E1", Y1), ("F1", Y1), ("V1", Y1), ("G1", 0), ("E2", 0), ("F2", 0), ("A2", 0)):
            ref = r[n]

            @pl.loop(0, ref.shape[1])
            def _(i):
                for c in range(ref.shape[0]):
                    zero(ref, c, i, slice(rows, ref.shape[2]))
        for n, planes in (("V0", (0, 1, X + 2, X + 3)), ("A0", (1, X + 2)), ("F1", (0, X1 + 5)),
                          ("A1", (0, X1 + 5)), ("B1", (0, X1 + 5))):
            for c in range(C):
                for p in planes:
                    zero(r[n], c, p)
        absent = {}

        def when_absent(dx, dy, ref, *idx):
            absent.setdefault((dx, dy), []).append((ref, idx))

        for h in (*self.hE0x, self.hE0, self.hE1, *self.hF0, self.hF1, self.hV1, *self.hV0):
            ref = r[h["target"]]
            for m in h["msgs"]:
                if m[0] == "x" and h["land"]:
                    k = 0 if m[1] > 0 else 1
                    for c in range(h["comps"]):
                        for p in range(h["w"]):
                            when_absent(m[1], 0, r[h["name"] + "_lx"], k, c, p)
                elif m[0] == "x":
                    for c in range(h["base"], h["base"] + h["comps"]):
                        for p in range(m[4], m[4] + h["w"]):
                            when_absent(m[1], 0, ref, c, p, slice(0, h["Y"]))
                elif m[0] == "y":
                    when_absent(0, m[2], r[h["name"] + "_ry"], m[1])
                else:
                    when_absent(*m[2], r[h["name"] + "_rd"], m[1])
        for m in self.aG1["msgs"]:
            when_absent(m[1], m[2], r[m[0] + "_r"], slice(None))
        for k, (dx, t, dy) in enumerate(MEMBERS):
            if dx or dy:
                when_absent(dx, dy, r["Re2"], k)
        for k, (dx, dy) in enumerate(WINDOW):
            for n in ("Rf2", "Rv2"):
                when_absent(dx, dy, r[n], k)
        for k, dy in enumerate(ROWS):
            for t in (0, 1):
                if dy:
                    when_absent(0, dy, r["Rn2"], 3 * t + k)
                when_absent(4 * t - 2, dy, r["Rd2"], 3 * t + k)
        for (dx, dy), spots in absent.items():
            @pl.when(jnp.logical_not(self.exists(-dx, -dy)))
            def _():
                for ref, idx in spots:
                    zero(ref, *idx)

    def edges(self):
        r, C, X, Y, R = self.r, self.C, self.X, self.Y, self.R0
        K = r["C0"]
        for h in self.hF0:
            for c, dx, dy in self.halo_copies(h, "y"):
                pl.when(self.exists(-dx, -dy))(c.wait_recv)
        for c in range(C):
            stage = r[self.hF0[c]["name"] + "_ry"]
            for p in (2, 3, X, X + 1):
                r["D0"][c, p, 0:Y, :] = r["V0"][c, p, 0:Y, :]
                for k, q, f, o in ((0, 0, 3, R - 1), (1, Y - 1, 2, Y)):
                    a = K[6, p, o:o + 1, :] * stage[k, p - 2:p - 1, :]
                    r["D0"][c, p, q:q + 1, :] = r["V0"][c, p, q:q + 1, :] + (
                        K[6, p, q:q + 1, :] * (K[f, p, q:q + 1, :] * a))

    def residual(self, V, K, G, T, px, Xc, ring, a, b):
        V, K, G, T = (self.r[n] for n in (V, K, G, T))
        R = V.shape[-2]
        rows = slice(0, R)
        n = Xc + 2 * ring

        def defect(i, c):
            v, acc = self.stencil(V, K, G, i, c, rows)
            return acc - K[7, i] * v

        @pl.loop(a, b, unroll=True)
        def _(j):
            for c in range(self.C):
                i = px + 2 * j
                start = pl.multiple_of((c * n + j + ring) * R, 8)
                T[pl.ds(start, R), :] = 0.5 * (defect(i, c) + defect(i + 1, c))

    def ring_residual(self, V, K, T, px, Xc, ring):
        V, K, T = (self.r[n] for n in (V, K, T))
        R, n = V.shape[-2], Xc + 2 * ring
        last = px + 2 * Xc + 2 * ring - 2
        for c in range(self.C):
            for near, far, k, j in ((px - 2 * ring + 1, px - 2 * ring, 0, 0), (last, last + 1, 1, n - 1)):
                start = (c * n + j) * R
                if ring == 1:
                    step = 1 if k == 0 else -1
                    v = V[c, near]
                    acc = K[k, near] * V[c, near + step] - K[7, near] * v + K[k, far] * v
                    for f, o in ((2, pltpu.roll(v, R - 1, 0)), (3, pltpu.roll(v, 1, 0)),
                                 (4, pltpu.roll(v, v.shape[1] - 1, 1)), (5, pltpu.roll(v, 1, 1))):
                        acc = acc + K[f, near] * o
                else:
                    acc = K[k, near] * V[c, near + (1 if k == 0 else -1)]
                T[start:start + R, :] = 0.5 * acc

    def spread(self, V, K, G, i, o, k):
        V, K, O = (self.r[n] for n in (V, K, G))
        for c in range(self.C):
            O[c, i] = K[6, i] * (K[k, i] * V[c, o])

    def dot(self, a, b):
        return lax.dot_general(a, b, (((1,), (0,)), ((), ())), preferred_element_type=jnp.float32)

    def split(self, t):
        hi = t.astype(jnp.bfloat16)
        return hi, (t - hi.astype(jnp.float32)).astype(jnp.bfloat16)

    def right(self, t, m):
        hi, lo = self.split(t)
        return self.dot(hi, m) + self.dot(lo, m)

    def left(self, m, t):
        hi, lo = self.split(t)
        return self.dot(m, hi) + self.dot(m, lo)

    def pairs(self, n, m, value, fine_dim):
        r = lax.broadcasted_iota(jnp.int32, (n, m), 0)
        c = lax.broadcasted_iota(jnp.int32, (n, m), 1)
        hit = (r >> 1) == c if fine_dim == 0 else (c >> 1) == r
        return jnp.where(hit, value, 0.0).astype(jnp.bfloat16)

    def squeeze(self, t):
        rows, Z = t.shape
        half = self.right(t, self.pairs(Z, Z // 2, 0.5, 0))
        return self.left(self.pairs(rows // 2, rows, 0.5, 1), half)

    def squeeze0(self, n):
        T, Z, R, R1, Y1 = self.r["T0"], self.Z, self.R0, self.R1, self.Y1
        half = self.right(T[...], self.pairs(Z, Z // 2, 0.5, 0))
        o = lax.broadcasted_iota(jnp.int32, (n * R1, n * R), 0)
        f = lax.broadcasted_iota(jnp.int32, (n * R1, n * R), 1)
        bo, bf = jnp.zeros_like(o), jnp.zeros_like(f)
        for k in range(1, n):
            bo = bo + (o >= k * R1).astype(jnp.int32)
            bf = bf + (f >= k * R).astype(jnp.int32)
        q = o - bo * R1
        q = jnp.where(q <= Y1, q, jnp.where(q == R1 - 1, R // 2 - 1, -1))
        m = jnp.where((bo == bf) & (((f - bf * R) >> 1) == q), 0.5, 0.0).astype(jnp.bfloat16)
        return [self.left(m, half[c * n * R:(c + 1) * n * R]) for c in range(self.C)]

    def prolong(self, W, a, count, U, V, planes, coarse_of, offset, shift=0, widen=True):
        W, U, V = (self.r[n] for n in (W, U, V))
        C, _, Rc, Zc = W.shape
        Rf, Zf = V.shape[-2:]
        if widen:
            src = W[:, pl.ds(a + shift, count)].reshape(C * count * Rc, Zc)
            U[...] = self.right(src, self.pairs(Zc, Zf, 1.0, 1))
        r = lax.broadcasted_iota(jnp.int32, (Rf, Rc), 0)
        c = lax.broadcasted_iota(jnp.int32, (Rf, Rc), 1)
        r = jnp.where(r < Rf - 4, r, r - Rf)
        c = c - offset if offset else jnp.where(c < Rc - 4, c, c - Rc)
        lift = jnp.where((r >> 1) == c, 1.0, 0.0).astype(jnp.bfloat16)
        for comp in range(C):
            for k in range(count):
                if not any(coarse_of(p) == a + k for p in planes):
                    continue
                start = (comp * count + k) * Rc
                block = self.left(lift, U[start:start + Rc, :])
                for p in planes:
                    if coarse_of(p) == a + k:
                        V[comp, p] = V[comp, p] + block

    def body(self, forcing, phase, out, *scratch):
        names = list(self.scratch)
        self.r = r = dict(zip(names, scratch))
        self.ssem, self.rsem, lsem = scratch[len(names):]
        self.gx, self.gy = lax.axis_index("gx"), lax.axis_index("gy")
        self.m = lax.rem(self.gx, 2)
        X, Y, Z, C = self.X, self.Y, self.Z, self.C
        X1, Y1 = self.X1, self.Y1
        block = (pl.ds(2, X), pl.ds(TOP, Y))
        load_p = pltpu.make_async_copy(phase, r["ph"], lsem.at[0])
        load_p.start()
        load_f = pltpu.make_async_copy(forcing, r["F0"].at[:, block[0], block[1], :], lsem.at[1])
        load_f.start()

        barrier = pltpu.get_barrier_semaphore()
        count = jnp.int32(0)
        for dx, t, dy in MEMBERS:
            ok = self.exists(dx, dy) if dx or dy else self.gx >= 0
            count = count + ok.astype(jnp.int32)

            @pl.when(ok)
            def _():
                pl.semaphore_signal(barrier, inc=1, device_id=(self.gx + dx + t * (1 - 2 * self.m), self.gy + dy),
                                    device_id_type=MESH)
        self.clear()
        load_p.wait()

        @pl.loop(0, X)
        def _(i):
            ph = r["ph"][i]
            e = jnp.zeros(ph.shape, jnp.float32)
            for k, value in enumerate(VISCOSITIES):
                e = jnp.where(ph == k, jnp.float32(value), e)
            r["E0"][0, i + 2, TOP:TOP + Y, :] = e
        pl.semaphore_wait(barrier, count)
        self.halo_start(self.hE0x[0])
        self.halo_start(self.hE0)
        load_f.wait()
        for h in self.hF0:
            self.halo_start(h, "y")

        for j in range(X1):
            r["T0"][j * Y:(j + 1) * Y, :] = 0.5 * (
                r["E0"][0, 2 + 2 * j, TOP:TOP + Y, :] + r["E0"][0, 3 + 2 * j, TOP:TOP + Y, :])
        e1 = self.squeeze(r["T0"][0:X1 * Y, :])
        for j in range(X1):
            r["E1"][0, 3 + j, TOP:TOP + Y1, :] = e1[j * Y1:(j + 1) * Y1]
        for j in range(self.X2):
            r["T1"][j * Y1:(j + 1) * Y1, :] = 0.5 * (
                e1[2 * j * Y1:(2 * j + 1) * Y1] + e1[(2 * j + 1) * Y1:(2 * j + 2) * Y1])
        r["Se2"][...] = self.squeeze(r["T1"][0:self.X2 * Y1, :])

        self.halo_start(self.hE1)
        self.halo_start(self.hE0x[1])
        self.member_start()
        for h in self.hF0:
            self.halo_start(h, "x")
        X2, Y2, R1 = self.X2, self.Y2, self.R1
        self.halo_wait(self.hE0, "y")
        self.coefs("E0", "C0", 3, X + 1, 1.0)
        self.first("C0", "F0", "A0", 3, X + 1)
        self.sweep("A0", "C0", "F0", "V0", 4, X)
        self.halo_wait(self.hE0x[0])
        self.halo_wait(self.hE0, "d")
        for p in (2, X + 1):
            self.coefs("E0", "C0", p, p + 1, 1.0)
            self.first("C0", "F0", "A0", p, p + 1)
        self.sweep("A0", "C0", "F0", "V0", 2, 4)
        self.sweep("A0", "C0", "F0", "V0", X, X + 2)
        self.residual("V0", "C0", "F0", "T0", 2, X1, 1, 1, X1 - 1)
        self.halo_wait(self.hE1)
        self.coefs("E1", "C1", 1, X1 + 5, 4.0)
        self.face("E1", "C1", 0, 1, 0, 4.0)
        self.face("E1", "C1", X1 + 5, X1 + 4, 1, 4.0)
        self.halo_wait(self.hE0x[1])
        for p, o, k in ((1, 0, 0), (X + 2, X + 3, 1)):
            self.coefs("E0", "C0", p, p + 1, 1.0)
            self.face("E0", "C0", o, p, k, 1.0)
        self.spread("A0", "C0", "V0", 1, 2, 0)
        self.spread("A0", "C0", "V0", X + 2, X + 1, 1)
        self.residual("V0", "C0", "F0", "T0", 2, X1, 1, 0, 1)
        self.residual("V0", "C0", "F0", "T0", 2, X1, 1, X1 - 1, X1)
        self.ring_residual("V0", "C0", "T0", 2, X1, 1)
        for c, f1 in enumerate(self.squeeze0(X1 + 2)):
            for j in range(X1 + 2):
                r["G1"][c, 2 + j] = f1[j * R1:(j + 1) * R1]
        self.ring_start(self.aG1)

        self.first("C1", "G1", "A1", 1, X1 + 5)
        self.sweep("A1", "C1", "G1", "B1", 1, X1 + 5)
        self.residual("B1", "C1", "G1", "T1", 3, X2, 2, -1, X2 + 1)
        self.ring_residual("B1", "C1", "T1", 3, X2, 2)
        f2 = self.squeeze(r["T1"][...])
        n = self.R1 // 2
        for c in range(C):
            for j in range(X2 + 4):
                s = (c * (X2 + 4) + j) * n
                r["Q2"][c, j] = f2[s:s + n]
        self.share_start()
        self.edges()

        self.ring_wait(self.aG1)
        for c in range(C):
            for j in range(X1):
                r["F1"][c, 3 + j, 0:Y1, :] = r["G1"][c, 3 + j, 0:Y1, :]
        self.ring_add(self.aG1, lambda c, p, q, k: (r["F1"], (c, 3 + p, slice(q, q + k))))
        self.halo_start(self.hF1)

        for h in self.hF0:
            self.halo_wait(h, "x")
            self.halo_place(h)
        rows0 = slice(TOP, TOP + Y)
        self.first("C0", "F0", "A0", 1, X + 3)
        self.sweep("A0", "C0", "F0", "V0", 2, X + 2, rows0)
        for h in self.hV0:
            self.halo_start(h, "yd")

        self.member_wait()
        self.coefs("E2", "C2", 1, self.P2 - 1, 16.0)
        self.share_wait()
        self.win_start("f2")
        self.halo_start(self.hV0[0], "x")

        self.halo_wait(self.hF1)
        self.first("C1", "F1", "A1", 1, X1 + 5)
        self.sweep("A1", "C1", "F1", "B1", 2, X1 + 4)
        for c in range(C):
            for j in range(X1):
                r["V1"][c, 3 + j, TOP:TOP + Y1, :] = r["B1"][c, 3 + j, TOP:TOP + Y1, :]
            for dx in (2, X1 + 3):
                r["V1"][c, dx, 0:Y1, :] = r["B1"][c, dx, 0:Y1, :]
            for j in range(-1, X1 + 1):
                for q in (self.R1 - 1, Y1):
                    r["V1"][c, 3 + j, q:q + 1, :] = r["B1"][c, 3 + j, q:q + 1, :]
        self.halo_start(self.hV1)

        self.win_wait("f2", "F2")
        p2 = self.P2
        self.first("C2", "F2", "A2", 1, p2 - 1)
        self.sweep("A2", "C2", "F2", "B2", 2, p2 - 2)
        self.sweep("B2", "C2", "F2", "A2", 3, p2 - 3)
        self.sweep("A2", "C2", "F2", "B2", 4, p2 - 4)
        for c in range(C):
            for p in range(2 * self.X2):
                i = (c * 2 * self.X2 + p) * self.Y2
                r["Sv2"][i:i + self.Y2, :] = r["B2"][c, 4 + p, self.Y2:2 * self.Y2, :]
        self.win_start("v2")
        self.halo_start(self.hV0[1], "x")
        self.halo_start(self.hV0[2], "x")
        self.win_wait("v2", "A2")
        off = self.m * X2
        self.sweep("A2", "C2", "F2", "B2", 1, X2 + 7, off=off)
        self.sweep("B2", "C2", "F2", "A2", 2, X2 + 6, off=off)

        self.halo_wait(self.hV1)
        self.halo_sent(self.hV1)
        self.prolong("A2", 2, self.X2 + 4, "UZ1", "V1", range(self.P1),
                     lambda p: 4 + (p - 3) // 2, self.Y2, self.m * self.X2)
        self.sweep("V1", "C1", "F1", "A1", 1, X1 + 5)
        self.sweep("A1", "C1", "F1", "B1", 2, X1 + 4)

        for h in self.hV0:
            self.halo_wait(h, "yd")
            self.halo_sent(h, "yd")
        own = range(2, X + 2)
        ends = (0, 1, X + 2, X + 3)
        self.prolong("B1", 2, X1 + 2, "UZ0", "V0", own, lambda p: 3 + (p - 2) // 2, 0)
        self.sweep("V0", "C0", "F0", "B0", 3, X + 1)
        for c, h in enumerate(self.hV0):
            self.halo_wait(h, "x")
            lx, V = r[h["name"] + "_lx"], r["V0"]
            V[c, 0, 0:Y, :] = lx[0, 0, 0]
            V[c, 1, 0:Y, :] = V[c, 1, 0:Y, :] + lx[0, 0, 1]
            V[c, X + 2, 0:Y, :] = V[c, X + 2, 0:Y, :] + lx[1, 0, 0]
            V[c, X + 3, 0:Y, :] = lx[1, 0, 1]
        self.prolong("B1", 2, X1 + 2, "UZ0", "V0", ends, lambda p: 3 + (p - 2) // 2, 0, widen=False)
        self.sweep("V0", "C0", "F0", "B0", 1, 3)
        self.sweep("V0", "C0", "F0", "B0", X + 1, X + 3)
        self.sweep("B0", "C0", "F0", out, 2, X + 2, rows0, shift=2)
        for h in (self.hE0, *self.hE0x, *self.hF0, self.hE1, self.hF1):
            self.halo_sent(h)
        for h in self.hV0:
            self.halo_sent(h, "x")
        self.ring_sent(self.aG1)
        self.share_sent()
        self.member_sent()
        for n in ("f2", "v2"):
            self.win_sent(n)

    def __call__(self, forcing, phase):
        any_space = pl.BlockSpec(memory_space=pl.ANY)
        sems = [pltpu.SemaphoreType.DMA((self.n_sems,)), pltpu.SemaphoreType.DMA((self.n_sems,)),
                pltpu.SemaphoreType.DMA((2,))]
        return pl.pallas_call(
            self.body,
            out_shape=pltpu.VMEM(forcing.shape, jnp.float32),
            in_specs=[any_space, any_space],
            out_specs=pl.BlockSpec(memory_space=pltpu.VMEM),
            scratch_shapes=list(self.scratch.values()) + sems,
            compiler_params=pltpu.CompilerParams(
                collective_id=0, has_side_effects=True, vmem_limit_bytes=60 * 1024 * 1024),
            name="vcycle",
        )(forcing, phase)


def solution(mesh):
    grid = (mesh.shape["gx"], mesh.shape["gy"])

    def per_device(forcing, phase_ids):
        return Kernel(phase_ids.shape, forcing.shape[0], grid)(forcing, phase_ids)

    return jax.shard_map(
        per_device,
        mesh=mesh,
        in_specs=(P(None, "gx", "gy", None), P("gx", "gy", None)),
        out_specs=P(None, "gx", "gy", None),
        check_vma=False,
    )
```

```python
import functools

import jax
import jax.numpy as jnp
from jax import lax
from jax.experimental import pallas as pl
from jax.experimental.pallas import tpu as pltpu
from jax.sharding import PartitionSpec as P

COARSE_SWEEPS = 6
VISCOSITIES = (0.2, 0.6, 1.5, 4.0)
WEIGHT = 2.0 / 3.0
MESH = pl.DeviceIdType.MESH
WINDOW = [(dx, dy) for dx in (-2, 0, 2) for dy in (-1, 0, 1) if (dx, dy) != (0, 0)]
MEMBERS = [(dx, t, dy) for dx in (-2, 0, 2) for t in (0, 1) for dy in (-1, 0, 1) if (dx, t, dy) != (0, 0, 0)]
ROWS = (0, 1, -1)
TOP = 0


def up8(n):
    return -(-n // 8) * 8


def side_slices(step, first, length, lo, hi):
    if step > 0:
        return (first + length - hi, first - hi)
    return (first + lo - 1, first + length + lo - 1)


class Kernel:
    def __init__(self, sizes, comps, grid):
        self.X, self.Y, self.Z = sizes
        self.C = comps
        self.grid = grid
        self.scratch = {}
        self.n_sems = 0
        self.plan()

    def buf(self, name, shape, dtype=jnp.float32):
        self.scratch[name] = pltpu.VMEM(tuple(shape), dtype)

    def halo(self, name, target, comps, px, X, Y, Z, lo, hi, diag, base=0, land=None, only="xyd"):
        w = hi - lo + 1
        msgs = []
        for dx in (1, -1) if "x" in only else ():
            s, d = side_slices(dx, px, X, lo, hi)
            msgs.append(("x", dx, 0, s, d, self.n_sems))
            self.n_sems += 1
        n = comps * X * w
        if "y" in only:
            self.buf(name + "_sy", (2, up8(n), Z))
            self.buf(name + "_ry", (2, up8(n), Z))
        for k, dy in enumerate((1, -1)) if "y" in only else ():
            s, d = side_slices(dy, TOP, Y, lo, hi)
            d %= Y + 8
            msgs.append(("y", k, dy, s, d, self.n_sems))
            self.n_sems += 1
        if diag:
            n = comps * len(diag)
            self.buf(name + "_sd", (4, n, 1, Z))
            self.buf(name + "_rd", (4, n, 1, Z))
            for k, (dx, dy) in enumerate([(1, 1), (1, -1), (-1, 1), (-1, -1)]):
                cells = [[], []]
                for a, b in diag:
                    sx, tx = side_slices(dx, px, X, a, a)
                    sy, ty = side_slices(dy, TOP, Y, b, b)
                    cells[0].append((sx, sy))
                    cells[1].append((tx, ty % (Y + 8)))
                msgs.append(("d", k, (dx, dy), cells[0], cells[1], self.n_sems))
                self.n_sems += 1
        if land:
            self.buf(name + "_lx", (2, comps, w, Y, Z))
        return dict(name=name, land=land, base=base, target=target, comps=comps, px=px, X=X, Y=Y, w=w, diag=diag, msgs=msgs)

    def ring(self, name, source, px, X, Y, Z, w):
        C = self.C
        dirs = [(dx, dy) for dx in (0, 1, -1) for dy in (0, 1, -1) if (dx, dy) != (0, 0)]
        msgs = []
        for dx, dy in dirs:
            px_count, rows = (w if dx else X), (w if dy else Y)
            key = "%s_%d%d" % (name, dx + 1, dy + 1)
            n = up8(C * px_count * rows)
            self.buf(key + "_s", (n, Z))
            self.buf(key + "_r", (n, Z))
            out = (px + (X if dx > 0 else -w if dx < 0 else 0), Y if dy > 0 else -w if dy < 0 else 0)
            into = (X - w if dx < 0 else 0, Y - w if dy < 0 else 0)
            msgs.append((key, dx, dy, px_count, rows, out, into, self.n_sems))
            self.n_sems += 1
        return dict(source=source, msgs=msgs)

    def plan(self):
        X, Y, Z, C = self.X, self.Y, self.Z, self.C
        self.P0, self.R0 = X + 4, Y + 8
        self.X1, self.Y1, self.Z1 = X // 2, Y // 2, Z // 2
        self.P1, self.R1 = self.X1 + 6, self.Y1 + 8
        self.X2, self.Y2, self.Z2 = X // 4, Y // 4, Z // 4
        self.P2, self.R2 = 2 * self.X2 + 8, up8(self.Y2 * 3)
        b = self.buf
        b("ph", (X, Y, Z), jnp.int32)
        b("E0", (1, self.P0, self.R0, Z))
        b("C0", (8, self.P0, self.R0, Z))
        for n in ("F0", "A0", "V0", "B0", "D0"):
            b(n, (C, self.P0, self.R0, Z))
        b("T0", (C * (self.X1 + 2) * self.R0, Z))
        b("E1", (1, self.P1, self.R1, self.Z1))
        b("C1", (8, self.P1, self.R1, self.Z1))
        for n in ("F1", "G1", "A1", "V1", "B1"):
            b(n, (C, self.P1, self.R1, self.Z1))
        b("T1", (C * (self.X2 + 4) * self.R1, self.Z1))
        b("E2", (1, self.P2, self.R2, self.Z2))
        b("C2", (8, self.P2, self.R2, self.Z2))
        for n in ("F2", "A2", "B2"):
            b(n, (C, self.P2, self.R2, self.Z2))
        blk = self.X2 * self.Y2
        b("Se2", (blk, self.Z2))
        b("Re2", (len(MEMBERS), blk, self.Z2))
        for n in ("f2", "v2"):
            b("S" + n, (2 * C * blk, self.Z2))
            b("R" + n, (len(WINDOW), 2 * C * blk, self.Z2))
        near, far = up8(C * (self.X2 + 2) * self.Y2), up8(C * 2 * self.Y2)
        b("Sn2", (3, near, self.Z2))
        b("Rn2", (6, near, self.Z2))
        b("Sd2", (3, far, self.Z2))
        b("Rd2", (6, far, self.Z2))
        b("W2", (C, 2 * self.X2, 8, self.Z2))
        b("Q2", (C, self.X2 + 4, self.R1 // 2, self.Z2))
        b("UZ1", (self.R2 * C * (self.X2 + 4), self.Z1))
        b("UZ0", (self.R1 * C * (self.X1 + 2), self.Z))
        reach = [(1, 1), (1, 2), (2, 1), (1, 3), (2, 2), (3, 1)]
        self.hE0 = self.halo("hE0", "E0", 1, 2, X, Y, Z, 1, 2, [(1, 1)], only="yd")
        self.hE0x = [self.halo("hE0x%d" % k, "E0", 1, 2, X, Y, Z, k, k, [], only="x") for k in (1, 2)]
        self.hF0 = [self.halo("hFc%d" % c, "F0", 1, 2, X, Y, Z, 1, 1, [], c) for c in range(C)]
        self.hV0 = [self.halo("hVc%d" % c, "V0", 1, 2, X, Y, Z, 1, 2, [(1, 1)], c, "D0") for c in range(C)]
        self.hE1 = self.halo("hE1", "E1", 1, 3, self.X1, self.Y1, self.Z1, 1, 3, reach)
        self.hF1 = self.halo("hF1", "F1", C, 3, self.X1, self.Y1, self.Z1, 1, 2, reach[:3])
        self.hV1 = self.halo("hV1", "V1", C, 3, self.X1, self.Y1, self.Z1, 2, 3, reach[1:])
        self.aG1 = self.ring("aG1", "G1", 3, self.X1, self.Y1, self.Z1, 1)
        self.win = {}
        for n, k in (("e2", len(MEMBERS)), ("f2", len(WINDOW)), ("v2", len(WINDOW)), ("n2", 6), ("d2", 6)):
            self.win[n] = self.n_sems
            self.n_sems += k

    def exists(self, dx, dy):
        ok = None
        for step, me, size in ((dx, self.gx, self.grid[0]), (dy, self.gy, self.grid[1])):
            if step:
                t = (me + step >= 0) & (me + step < size)
                ok = t if ok is None else ok & t
        return ok

    def copy(self, src, dst, sem, dx, dy, into=None):
        into = sem if into is None else into
        return pltpu.make_async_remote_copy(
            src_ref=src, dst_ref=dst, send_sem=self.ssem.at[sem], recv_sem=self.rsem.at[into],
            device_id=(self.gx + dx, self.gy + dy), device_id_type=MESH)

    def halo_copies(self, h, kinds="xyd"):
        r = self.r
        ref = r[h["target"]]
        rows = pl.ds(TOP, h["Y"])
        out = []
        for m in h["msgs"]:
            if m[0] not in kinds:
                continue
            if m[0] == "x":
                _, dx, dy, s, d, sem = m
                comps = pl.ds(h["base"], h["comps"])
                src, dst = ref, ref.at[comps, pl.ds(d, h["w"]), rows, :]
                if h["land"]:
                    src, dst = r[h["land"]], r[h["name"] + "_lx"].at[0 if dx > 0 else 1]
                c = self.copy(src.at[comps, pl.ds(s, h["w"]), rows, :], dst, sem, dx, 0)
                out.append((c, dx, 0))
            elif m[0] == "y":
                _, k, dy, s, d, sem = m
                out.append((self.copy(r[h["name"] + "_sy"].at[k], r[h["name"] + "_ry"].at[k], sem, 0, dy), 0, dy))
            else:
                _, k, (dx, dy), _, _, sem = m
                out.append((self.copy(r[h["name"] + "_sd"].at[k], r[h["name"] + "_rd"].at[k], sem, dx, dy), dx, dy))
        return out

    def rows_of(self, h, m, which):
        if m[0] == "y":
            start = m[3 + which]
            return m[1], "y", [(c + h["base"], h["px"] + p, start + q) for c in range(h["comps"])
                               for p in range(h["X"]) for q in range(h["w"])]
        return m[1], "d", [(c + h["base"], p, q) for c in range(h["comps"]) for p, q in m[3 + which]]

    def halo_start(self, h, kinds="xyd"):
        ref = self.r[h["target"]]
        for m in h["msgs"]:
            if m[0] == "x" or m[0] not in kinds:
                continue
            k, kind, rows = self.rows_of(h, m, 0)
            stage = self.r[h["name"] + "_s" + kind]
            for i, (c, p, q) in enumerate(rows):
                row = ref[c, p, q:q + 1, :]
                if kind == "d":
                    stage[k, i] = row
                else:
                    stage[k, i:i + 1, :] = row
        for c, dx, dy in self.halo_copies(h, kinds):
            pl.when(self.exists(dx, dy))(c.start)

    def halo_wait(self, h, kinds="xyd"):
        for c, dx, dy in self.halo_copies(h, kinds):
            pl.when(self.exists(-dx, -dy))(c.wait_recv)
        self.halo_place(h, kinds)

    def halo_place(self, h, kinds="xyd"):
        ref = self.r[h["target"]]
        for m in h["msgs"]:
            if m[0] == "x" or m[0] not in kinds:
                continue
            k, kind, rows = self.rows_of(h, m, 1)
            stage = self.r[h["name"] + "_r" + kind]
            for i, (c, p, q) in enumerate(rows):
                ref[c, p, q:q + 1, :] = stage[k, i] if kind == "d" else stage[k, i:i + 1, :]

    def halo_sent(self, h, kinds="xyd"):
        for c, dx, dy in self.halo_copies(h, kinds):
            pl.when(self.exists(dx, dy))(c.wait_send)

    def ring_copies(self, h):
        r = self.r
        return [(self.copy(r[m[0] + "_s"], r[m[0] + "_r"], m[7], m[1], m[2]), m[1], m[2]) for m in h["msgs"]]

    def ring_start(self, h):
        S = self.r[h["source"]]
        for key, dx, dy, planes, rows, (p, q), _, _ in h["msgs"]:
            q %= S.shape[2]
            i = 0
            for c in range(self.C):
                for k in range(planes):
                    self.r[key + "_s"][i:i + rows, :] = S[c, p + k, q:q + rows, :]
                    i += rows
        for c, dx, dy in self.ring_copies(h):
            pl.when(self.exists(dx, dy))(c.start)

    def ring_wait(self, h):
        for c, dx, dy in self.ring_copies(h):
            pl.when(self.exists(-dx, -dy))(c.wait_recv)

    def ring_add(self, h, place):
        for key, dx, dy, planes, rows, _, (p, q), _ in h["msgs"]:
            i = 0
            for c in range(self.C):
                for k in range(planes):
                    ref, idx = place(c, p + k, q, rows)
                    ref[idx] = ref[idx] + self.r[key + "_r"][i:i + rows, :]
                    i += rows

    def ring_sent(self, h):
        for c, dx, dy in self.ring_copies(h):
            pl.when(self.exists(dx, dy))(c.wait_send)

    def when(self, dx, dy, f):
        if (dx, dy) == (0, 0):
            f()
        else:
            pl.when(self.exists(dx, dy))(f)

    def member_copies(self):
        r = self.r
        return [(self.copy(r["Se2"], r["Re2"].at[k], self.win["e2"] + k, dx + t * (1 - 2 * self.m), dy), dx, t, dy)
                for k, (dx, t, dy) in enumerate(MEMBERS)]

    def member_start(self):
        for c, dx, t, dy in self.member_copies():
            self.when(dx, dy, c.start)

    def member_wait(self):
        for c, dx, t, dy in self.member_copies():
            self.when(-dx, -dy, c.wait_recv)
        E, X2, Y2 = self.r["E2"], self.X2, self.Y2
        for k, (dx, t, dy) in enumerate(MEMBERS + [(0, 0, 0)]):
            member = 1 - self.m if t else self.m
            for p in range(X2):
                v = self.r["Se2"][p * Y2:(p + 1) * Y2] if k == len(MEMBERS) else self.r["Re2"][k, p * Y2:(p + 1) * Y2]
                E[0, 4 + p - dx * X2 + member * X2, Y2 * (1 - dy):Y2 * (2 - dy), :] = v

    def member_sent(self):
        for c, dx, t, dy in self.member_copies():
            self.when(dx, dy, c.wait_send)

    def near_copies(self):
        r, b = self.r, self.win["n2"]
        return [(self.copy(r["Sn2"].at[k], r["Rn2"].at[3 * t + k], b + 3 * t + k, t * (1 - 2 * self.m), dy), t, k, dy)
                for t in (1, 0) for k, dy in enumerate(ROWS) if (t, dy) != (0, 0)]

    def far_sends(self):
        r, b, m = self.r, self.win["d2"], self.m
        return [(self.copy(r["Sd2"].at[k], r["Rd2"].at[3 * m + k], b + 3 * t + k, (2 * m - 1) * (2 - t), dy, b + 3 * m + k), dy)
                for t in (1, 0) for k, dy in enumerate(ROWS)]

    def far_recvs(self):
        r, b = self.r, self.win["d2"]
        return [(self.copy(r["Sd2"].at[k], r["Rd2"].at[3 * s + k], b + 3 * s + k, 2, dy), 2 - 4 * s, k, dy)
                for s in (0, 1) for k, dy in enumerate(ROWS)]

    def far_exists(self, dy):
        x = self.gx + 2 * (2 * self.m - 1)
        ok = (x >= 0) & (x < self.grid[0])
        return ok & self.exists(0, dy) if dy else ok

    def share_start(self):
        r, C, X2, Y2 = self.r, self.C, self.X2, self.Y2
        Q = r["Q2"]
        R = Q.shape[2]
        for k, dy in enumerate(ROWS):
            q, n = ((0, Y2), (Y2, 2), (R - 2, 2))[k]
            i = 0
            for c in range(C):
                for p in range(X2 + 2):
                    r["Sn2"][k, i:i + n, :] = Q[c, 2 * (1 - self.m) + p, q:q + n, :]
                    i += n
            i = 0
            for c in range(C):
                for p in range(2):
                    r["Sd2"][k, i:i + n, :] = Q[c, self.m * (X2 + 2) + p, q:q + n, :]
                    i += n
        for c, t, k, dy in self.near_copies():
            self.when(0, dy, c.start)
        for c, dy in self.far_sends():
            pl.when(self.far_exists(dy))(c.start)

    def share_wait(self):
        r, C, X2, Y2 = self.r, self.C, self.X2, self.Y2
        W, Q = r["W2"], r["Q2"]
        for c, t, k, dy in self.near_copies():
            self.when(0, -dy, c.wait_recv)
        for c, dx, k, dy in self.far_recvs():
            self.when(dx, -dy, c.wait_recv)
        W[...] = jnp.zeros(W.shape, jnp.float32)
        spots = ((0, Y2), (0, 2), (Y2 - 2, 2))
        base = [0, 0] if X2 == 2 else [self.m * (X2 - 2), (1 - self.m) * (X2 - 2)]
        for c in range(C):
            for p in range(X2 + 2):
                W[c, base[0] + p, 0:Y2, :] = W[c, base[0] + p, 0:Y2, :] + Q[c, 2 * (1 - self.m) + p, 0:Y2, :]
        for _, t, k, dy in self.near_copies():
            q, n = spots[k]
            for c in range(C):
                for p in range(X2 + 2):
                    i = (c * (X2 + 2) + p) * n
                    W[c, base[t] + p, q:q + n, :] = W[c, base[t] + p, q:q + n, :] + r["Rn2"][3 * t + k, i:i + n, :]
        for s in (0, 1):
            for k, dy in enumerate(ROWS):
                q, n = spots[k]
                for c in range(C):
                    for p in range(2):
                        i, o = (c * 2 + p) * n, (p if s else 2 * X2 - 2 + p)
                        W[c, o, q:q + n, :] = W[c, o, q:q + n, :] + r["Rd2"][3 * s + k, i:i + n, :]
        for c in range(C):
            for p in range(2 * X2):
                i = (c * 2 * X2 + p) * Y2
                r["Sf2"][i:i + Y2, :] = W[c, p, 0:Y2, :]

    def share_sent(self):
        for c, t, k, dy in self.near_copies():
            self.when(0, dy, c.wait_send)
        for c, dy in self.far_sends():
            pl.when(self.far_exists(dy))(c.wait_send)

    def win_copies(self, n):
        src, dst = self.r["S" + n], self.r["R" + n]
        return [(self.copy(src, dst.at[k], self.win[n] + k, dx, dy), dx, dy) for k, (dx, dy) in enumerate(WINDOW)]

    def win_start(self, n):
        for c, dx, dy in self.win_copies(n):
            pl.when(self.exists(dx, dy))(c.start)

    def win_wait(self, n, target):
        copies = self.win_copies(n)
        for c, dx, dy in copies:
            pl.when(self.exists(-dx, -dy))(c.wait_recv)
        ref = self.r[target]
        X2, Y2 = self.X2, self.Y2
        for k, (dx, dy) in enumerate(WINDOW + [(0, 0)]):
            for c in range(ref.shape[0]):
                for p in range(2 * X2):
                    i = (c * 2 * X2 + p) * Y2
                    if (dx, dy) == (0, 0):
                        v = self.r["S" + n][i:i + Y2, :]
                    else:
                        v = self.r["R" + n][k, i:i + Y2, :]
                    ref[c, 4 + p - dx * X2, Y2 * (1 - dy):Y2 * (2 - dy), :] = v

    def win_sent(self, n):
        for c, dx, dy in self.win_copies(n):
            pl.when(self.exists(dx, dy))(c.wait_send)

    def coefs(self, E, K, a, b, scale):
        E, K = self.r[E], self.r[K]
        Z = E.shape[-1]
        shape = E.shape[-2:]
        R = shape[0]
        s = 1.0 / scale

        @pl.loop(a, b)
        def _(i):
            z = lax.broadcasted_iota(jnp.int32, shape, 1)
            e = E[0, i]

            def face(o):
                t = e + o
                return jnp.where(jnp.minimum(e, o) > 0.0, t * (0.5 * s), t * s)

            zp = jnp.where(z == Z - 1, 0.0, pltpu.roll(e, Z - 1, 1))
            zm = jnp.where(z == 0, 0.0, pltpu.roll(e, 1, 1))
            others = (E[0, i + 1], E[0, i - 1], pltpu.roll(e, R - 1, 0), pltpu.roll(e, 1, 0), zp, zm)
            diag = None
            for k, o in enumerate(others):
                c = face(o)
                diag = c if diag is None else diag + c
                if k == 4:
                    c = jnp.where(z == Z - 1, 0.0, c)
                if k == 5:
                    c = jnp.where(z == 0, 0.0, c)
                K[k, i] = c
            inside = e > 0.0
            K[6, i] = jnp.where(inside, WEIGHT / jnp.where(inside, diag, 1.0), 0.0)
            K[7, i] = diag

    def face(self, E, K, i, o, k, scale):
        e, f = self.r[E][0, i], self.r[E][0, o]
        t, s = e + f, 1.0 / scale
        self.r[K][k, i] = jnp.where(jnp.minimum(e, f) > 0.0, t * (0.5 * s), t * s)

    def stencil(self, V, K, G, i, c, rows):
        R, Z = V.shape[-2:]
        n = rows.stop - rows.start
        v = V[c, i, rows, :]
        if n == R:
            yp, ym = pltpu.roll(v, R - 1, 0), pltpu.roll(v, 1, 0)
        else:
            yp, ym = V[c, i, 1:n + 1, :], pltpu.roll(V[c, i], 1, 0)[:n]
        acc = G[c, i, rows, :]
        parts = (V[c, i + 1, rows, :], V[c, i - 1, rows, :], yp, ym, pltpu.roll(v, Z - 1, 1), pltpu.roll(v, 1, 1))
        for k, o in enumerate(parts):
            acc = acc + K[k, i, rows, :] * o
        return v, acc

    def first(self, K, G, O, a, b, comps=None):
        K, G, O = (self.r[n] for n in (K, G, O))

        @pl.loop(a, b, unroll=2 if (b - a) % 2 == 0 else 1)
        def _(i):
            w = K[6, i]
            for c in comps or range(self.C):
                O[c, i] = w * G[c, i]

    def sweep(self, V, K, G, O, a, b, rows=None, shift=0, comps=None, off=0):
        V, K, G = (self.r[n] for n in (V, K, G))
        O = self.r[O] if isinstance(O, str) else O
        rows = rows or slice(0, V.shape[-2])
        out_rows = rows if shift == 0 else slice(0, rows.stop - rows.start)

        @pl.loop(a, b, unroll=True)
        def _(i):
            i = i + off
            for c in comps or range(self.C):
                v, acc = self.stencil(V, K, G, i, c, rows)
                O[c, i - shift, out_rows, :] = (1.0 - WEIGHT) * v + K[6, i, rows, :] * acc

    def clear(self):
        r, C, X, Y, X1, Y1 = self.r, self.C, self.X, self.Y, self.X1, self.Y1

        def zero(ref, *idx):
            ref[idx] = jnp.zeros(ref.at[idx].shape, ref.dtype)

        for n, rows in (("E0", Y), ("F0", Y), ("V0", Y), ("E1", Y1), ("F1", Y1), ("V1", Y1), ("G1", 0), ("E2", 0), ("F2", 0), ("A2", 0)):
            ref = r[n]

            @pl.loop(0, ref.shape[1])
            def _(i):
                for c in range(ref.shape[0]):
                    zero(ref, c, i, slice(rows, ref.shape[2]))
        for n, planes in (("V0", (0, 1, X + 2, X + 3)), ("A0", (1, X + 2)), ("F1", (0, X1 + 5)),
                          ("A1", (0, X1 + 5)), ("B1", (0, X1 + 5))):
            for c in range(C):
                for p in planes:
                    zero(r[n], c, p)
        absent = {}

        def when_absent(dx, dy, ref, *idx):
            absent.setdefault((dx, dy), []).append((ref, idx))

        for h in (*self.hE0x, self.hE0, self.hE1, *self.hF0, self.hF1, self.hV1, *self.hV0):
            ref = r[h["target"]]
            for m in h["msgs"]:
                if m[0] == "x" and h["land"]:
                    k = 0 if m[1] > 0 else 1
                    for c in range(h["comps"]):
                        for p in range(h["w"]):
                            when_absent(m[1], 0, r[h["name"] + "_lx"], k, c, p)
                elif m[0] == "x":
                    for c in range(h["base"], h["base"] + h["comps"]):
                        for p in range(m[4], m[4] + h["w"]):
                            when_absent(m[1], 0, ref, c, p, slice(0, h["Y"]))
                elif m[0] == "y":
                    when_absent(0, m[2], r[h["name"] + "_ry"], m[1])
                else:
                    when_absent(*m[2], r[h["name"] + "_rd"], m[1])
        for m in self.aG1["msgs"]:
            when_absent(m[1], m[2], r[m[0] + "_r"], slice(None))
        for k, (dx, t, dy) in enumerate(MEMBERS):
            if dx or dy:
                when_absent(dx, dy, r["Re2"], k)
        for k, (dx, dy) in enumerate(WINDOW):
            for n in ("Rf2", "Rv2"):
                when_absent(dx, dy, r[n], k)
        for k, dy in enumerate(ROWS):
            for t in (0, 1):
                if dy:
                    when_absent(0, dy, r["Rn2"], 3 * t + k)
                when_absent(4 * t - 2, dy, r["Rd2"], 3 * t + k)
        for (dx, dy), spots in absent.items():
            @pl.when(jnp.logical_not(self.exists(-dx, -dy)))
            def _():
                for ref, idx in spots:
                    zero(ref, *idx)

    def edges(self):
        r, C, X, Y, R = self.r, self.C, self.X, self.Y, self.R0
        K = r["C0"]
        for h in self.hF0:
            for c, dx, dy in self.halo_copies(h, "y"):
                pl.when(self.exists(-dx, -dy))(c.wait_recv)
        for c in range(C):
            stage = r[self.hF0[c]["name"] + "_ry"]
            for p in (2, 3, X, X + 1):
                r["D0"][c, p, 0:Y, :] = r["V0"][c, p, 0:Y, :]
                for k, q, f, o in ((0, 0, 3, R - 1), (1, Y - 1, 2, Y)):
                    a = K[6, p, o:o + 1, :] * stage[k, p - 2:p - 1, :]
                    r["D0"][c, p, q:q + 1, :] = r["V0"][c, p, q:q + 1, :] + (
                        K[6, p, q:q + 1, :] * (K[f, p, q:q + 1, :] * a))

    def residual(self, V, K, G, T, px, Xc, ring, a, b):
        V, K, G, T = (self.r[n] for n in (V, K, G, T))
        R = V.shape[-2]
        rows = slice(0, R)
        n = Xc + 2 * ring

        def defect(i, c):
            v, acc = self.stencil(V, K, G, i, c, rows)
            return acc - K[7, i] * v

        @pl.loop(a, b, unroll=True)
        def _(j):
            for c in range(self.C):
                i = px + 2 * j
                start = pl.multiple_of((c * n + j + ring) * R, 8)
                T[pl.ds(start, R), :] = 0.5 * (defect(i, c) + defect(i + 1, c))

    def ring_residual(self, V, K, T, px, Xc, ring):
        V, K, T = (self.r[n] for n in (V, K, T))
        R, n = V.shape[-2], Xc + 2 * ring
        last = px + 2 * Xc + 2 * ring - 2
        for c in range(self.C):
            for near, far, k, j in ((px - 2 * ring + 1, px - 2 * ring, 0, 0), (last, last + 1, 1, n - 1)):
                start = (c * n + j) * R
                if ring == 1:
                    step = 1 if k == 0 else -1
                    v = V[c, near]
                    acc = K[k, near] * V[c, near + step] - K[7, near] * v + K[k, far] * v
                    for f, o in ((2, pltpu.roll(v, R - 1, 0)), (3, pltpu.roll(v, 1, 0)),
                                 (4, pltpu.roll(v, v.shape[1] - 1, 1)), (5, pltpu.roll(v, 1, 1))):
                        acc = acc + K[f, near] * o
                else:
                    acc = K[k, near] * V[c, near + (1 if k == 0 else -1)]
                T[start:start + R, :] = 0.5 * acc

    def spread(self, V, K, G, i, o, k):
        V, K, O = (self.r[n] for n in (V, K, G))
        for c in range(self.C):
            O[c, i] = K[6, i] * (K[k, i] * V[c, o])

    def dot(self, a, b):
        return lax.dot_general(a, b, (((1,), (0,)), ((), ())), preferred_element_type=jnp.float32)

    def split(self, t):
        hi = t.astype(jnp.bfloat16)
        return hi, (t - hi.astype(jnp.float32)).astype(jnp.bfloat16)

    def right(self, t, m):
        hi, lo = self.split(t)
        return self.dot(hi, m) + self.dot(lo, m)

    def left(self, m, t):
        hi, lo = self.split(t)
        return self.dot(m, hi) + self.dot(m, lo)

    def pairs(self, n, m, value, fine_dim):
        r = lax.broadcasted_iota(jnp.int32, (n, m), 0)
        c = lax.broadcasted_iota(jnp.int32, (n, m), 1)
        hit = (r >> 1) == c if fine_dim == 0 else (c >> 1) == r
        return jnp.where(hit, value, 0.0).astype(jnp.bfloat16)

    def squeeze(self, t):
        rows, Z = t.shape
        half = self.right(t, self.pairs(Z, Z // 2, 0.5, 0))
        return self.left(self.pairs(rows // 2, rows, 0.5, 1), half)

    def squeeze0(self, n):
        T, Z, R, R1, Y1 = self.r["T0"], self.Z, self.R0, self.R1, self.Y1
        half = self.right(T[...], self.pairs(Z, Z // 2, 0.5, 0))
        o = lax.broadcasted_iota(jnp.int32, (n * R1, n * R), 0)
        f = lax.broadcasted_iota(jnp.int32, (n * R1, n * R), 1)
        bo, bf = jnp.zeros_like(o), jnp.zeros_like(f)
        for k in range(1, n):
            bo = bo + (o >= k * R1).astype(jnp.int32)
            bf = bf + (f >= k * R).astype(jnp.int32)
        q = o - bo * R1
        q = jnp.where(q <= Y1, q, jnp.where(q == R1 - 1, R // 2 - 1, -1))
        m = jnp.where((bo == bf) & (((f - bf * R) >> 1) == q), 0.5, 0.0).astype(jnp.bfloat16)
        return [self.left(m, half[c * n * R:(c + 1) * n * R]) for c in range(self.C)]

    def prolong(self, W, a, count, U, V, planes, coarse_of, offset, shift=0, widen=True):
        W, U, V = (self.r[n] for n in (W, U, V))
        C, _, Rc, Zc = W.shape
        Rf, Zf = V.shape[-2:]
        if widen:
            src = W[:, pl.ds(a + shift, count)].reshape(C * count * Rc, Zc)
            U[...] = self.right(src, self.pairs(Zc, Zf, 1.0, 1))
        r = lax.broadcasted_iota(jnp.int32, (Rf, Rc), 0)
        c = lax.broadcasted_iota(jnp.int32, (Rf, Rc), 1)
        r = jnp.where(r < Rf - 4, r, r - Rf)
        c = c - offset if offset else jnp.where(c < Rc - 4, c, c - Rc)
        lift = jnp.where((r >> 1) == c, 1.0, 0.0).astype(jnp.bfloat16)
        for comp in range(C):
            for k in range(count):
                if not any(coarse_of(p) == a + k for p in planes):
                    continue
                start = (comp * count + k) * Rc
                block = self.left(lift, U[start:start + Rc, :])
                for p in planes:
                    if coarse_of(p) == a + k:
                        V[comp, p] = V[comp, p] + block

    def body(self, forcing, phase, out, *scratch):
        names = list(self.scratch)
        self.r = r = dict(zip(names, scratch))
        self.ssem, self.rsem, lsem = scratch[len(names):]
        self.gx, self.gy = lax.axis_index("gx"), lax.axis_index("gy")
        self.m = lax.rem(self.gx, 2)
        X, Y, Z, C = self.X, self.Y, self.Z, self.C
        X1, Y1 = self.X1, self.Y1
        block = (pl.ds(2, X), pl.ds(TOP, Y))
        load_p = pltpu.make_async_copy(phase, r["ph"], lsem.at[0])
        load_p.start()
        load_f = pltpu.make_async_copy(forcing, r["F0"].at[:, block[0], block[1], :], lsem.at[1])
        load_f.start()

        barrier = pltpu.get_barrier_semaphore()
        count = jnp.int32(0)
        for dx, t, dy in MEMBERS:
            ok = self.exists(dx, dy) if dx or dy else self.gx >= 0
            count = count + ok.astype(jnp.int32)

            @pl.when(ok)
            def _():
                pl.semaphore_signal(barrier, inc=1, device_id=(self.gx + dx + t * (1 - 2 * self.m), self.gy + dy),
                                    device_id_type=MESH)
        self.clear()
        load_p.wait()

        @pl.loop(0, X)
        def _(i):
            ph = r["ph"][i]
            e = jnp.zeros(ph.shape, jnp.float32)
            for k, value in enumerate(VISCOSITIES):
                e = jnp.where(ph == k, jnp.float32(value), e)
            r["E0"][0, i + 2, TOP:TOP + Y, :] = e
        pl.semaphore_wait(barrier, count)
        self.halo_start(self.hE0x[0])
        self.halo_start(self.hE0)
        load_f.wait()
        for h in self.hF0:
            self.halo_start(h, "y")

        for j in range(X1):
            r["T0"][j * Y:(j + 1) * Y, :] = 0.5 * (
                r["E0"][0, 2 + 2 * j, TOP:TOP + Y, :] + r["E0"][0, 3 + 2 * j, TOP:TOP + Y, :])
        e1 = self.squeeze(r["T0"][0:X1 * Y, :])
        for j in range(X1):
            r["E1"][0, 3 + j, TOP:TOP + Y1, :] = e1[j * Y1:(j + 1) * Y1]
        for j in range(self.X2):
            r["T1"][j * Y1:(j + 1) * Y1, :] = 0.5 * (
                e1[2 * j * Y1:(2 * j + 1) * Y1] + e1[(2 * j + 1) * Y1:(2 * j + 2) * Y1])
        r["Se2"][...] = self.squeeze(r["T1"][0:self.X2 * Y1, :])

        self.halo_start(self.hE1)
        self.halo_start(self.hE0x[1])
        self.member_start()
        for h in self.hF0:
            self.halo_start(h, "x")
        X2, Y2, R1 = self.X2, self.Y2, self.R1
        self.halo_wait(self.hE0, "y")
        self.coefs("E0", "C0", 3, X + 1, 1.0)
        self.first("C0", "F0", "A0", 3, X + 1)
        self.sweep("A0", "C0", "F0", "V0", 4, X)
        self.halo_wait(self.hE0x[0])
        self.halo_wait(self.hE0, "d")
        for p in (2, X + 1):
            self.coefs("E0", "C0", p, p + 1, 1.0)
            self.first("C0", "F0", "A0", p, p + 1)
        self.sweep("A0", "C0", "F0", "V0", 2, 4)
        self.sweep("A0", "C0", "F0", "V0", X, X + 2)
        self.residual("V0", "C0", "F0", "T0", 2, X1, 1, 1, X1 - 1)
        self.halo_wait(self.hE1)
        self.coefs("E1", "C1", 1, X1 + 5, 4.0)
        self.face("E1", "C1", 0, 1, 0, 4.0)
        self.face("E1", "C1", X1 + 5, X1 + 4, 1, 4.0)
        self.halo_wait(self.hE0x[1])
        for p, o, k in ((1, 0, 0), (X + 2, X + 3, 1)):
            self.coefs("E0", "C0", p, p + 1, 1.0)
            self.face("E0", "C0", o, p, k, 1.0)
        self.spread("A0", "C0", "V0", 1, 2, 0)
        self.spread("A0", "C0", "V0", X + 2, X + 1, 1)
        self.residual("V0", "C0", "F0", "T0", 2, X1, 1, 0, 1)
        self.residual("V0", "C0", "F0", "T0", 2, X1, 1, X1 - 1, X1)
        self.ring_residual("V0", "C0", "T0", 2, X1, 1)
        for c, f1 in enumerate(self.squeeze0(X1 + 2)):
            for j in range(X1 + 2):
                r["G1"][c, 2 + j] = f1[j * R1:(j + 1) * R1]
        self.ring_start(self.aG1)

        self.first("C1", "G1", "A1", 1, X1 + 5)
        self.sweep("A1", "C1", "G1", "B1", 1, X1 + 5)
        self.residual("B1", "C1", "G1", "T1", 3, X2, 2, -1, X2 + 1)
        self.ring_residual("B1", "C1", "T1", 3, X2, 2)
        f2 = self.squeeze(r["T1"][...])
        n = self.R1 // 2
        for c in range(C):
            for j in range(X2 + 4):
                s = (c * (X2 + 4) + j) * n
                r["Q2"][c, j] = f2[s:s + n]
        self.share_start()

        self.ring_wait(self.aG1)
        for c in range(C):
            for j in range(X1):
                r["F1"][c, 3 + j, 0:Y1, :] = r["G1"][c, 3 + j, 0:Y1, :]
        self.ring_add(self.aG1, lambda c, p, q, k: (r["F1"], (c, 3 + p, slice(q, q + k))))
        self.halo_start(self.hF1)
        self.edges()

        for h in self.hF0:
            self.halo_wait(h, "x")
            self.halo_place(h)
        rows0 = slice(TOP, TOP + Y)
        self.first("C0", "F0", "A0", 1, X + 3)
        self.sweep("A0", "C0", "F0", "V0", 2, X + 2, rows0)
        for h in self.hV0:
            self.halo_start(h, "yd")

        self.member_wait()
        self.coefs("E2", "C2", 1, self.P2 - 1, 16.0)
        self.share_wait()
        self.win_start("f2")
        self.halo_start(self.hV0[0], "x")

        self.halo_wait(self.hF1)
        self.first("C1", "F1", "A1", 1, X1 + 5)
        self.sweep("A1", "C1", "F1", "B1", 2, X1 + 4)
        for c in range(C):
            for j in range(X1):
                r["V1"][c, 3 + j, TOP:TOP + Y1, :] = r["B1"][c, 3 + j, TOP:TOP + Y1, :]
            for dx in (2, X1 + 3):
                r["V1"][c, dx, 0:Y1, :] = r["B1"][c, dx, 0:Y1, :]
            for j in range(-1, X1 + 1):
                for q in (self.R1 - 1, Y1):
                    r["V1"][c, 3 + j, q:q + 1, :] = r["B1"][c, 3 + j, q:q + 1, :]
        self.halo_start(self.hV1)

        self.win_wait("f2", "F2")
        p2 = self.P2
        self.first("C2", "F2", "A2", 1, p2 - 1)
        self.sweep("A2", "C2", "F2", "B2", 2, p2 - 2)
        self.sweep("B2", "C2", "F2", "A2", 3, p2 - 3)
        self.sweep("A2", "C2", "F2", "B2", 4, p2 - 4)
        for c in range(C):
            for p in range(2 * self.X2):
                i = (c * 2 * self.X2 + p) * self.Y2
                r["Sv2"][i:i + self.Y2, :] = r["B2"][c, 4 + p, self.Y2:2 * self.Y2, :]
        self.win_start("v2")
        self.halo_start(self.hV0[1], "x")
        self.halo_start(self.hV0[2], "x")
        self.win_wait("v2", "A2")
        off = self.m * X2
        self.sweep("A2", "C2", "F2", "B2", 1, X2 + 7, off=off)
        self.sweep("B2", "C2", "F2", "A2", 2, X2 + 6, off=off)

        self.halo_wait(self.hV1)
        self.halo_sent(self.hV1)
        self.prolong("A2", 2, self.X2 + 4, "UZ1", "V1", range(self.P1),
                     lambda p: 4 + (p - 3) // 2, self.Y2, self.m * self.X2)
        self.sweep("V1", "C1", "F1", "A1", 1, X1 + 5)
        self.sweep("A1", "C1", "F1", "B1", 2, X1 + 4)

        for h in self.hV0:
            self.halo_wait(h, "yd")
            self.halo_sent(h, "yd")
        own = range(2, X + 2)
        ends = (0, 1, X + 2, X + 3)
        self.prolong("B1", 2, X1 + 2, "UZ0", "V0", own, lambda p: 3 + (p - 2) // 2, 0)
        self.sweep("V0", "C0", "F0", "B0", 3, X + 1)
        for c, h in enumerate(self.hV0):
            self.halo_wait(h, "x")
            lx, V = r[h["name"] + "_lx"], r["V0"]
            V[c, 0, 0:Y, :] = lx[0, 0, 0]
            V[c, 1, 0:Y, :] = V[c, 1, 0:Y, :] + lx[0, 0, 1]
            V[c, X + 2, 0:Y, :] = V[c, X + 2, 0:Y, :] + lx[1, 0, 0]
            V[c, X + 3, 0:Y, :] = lx[1, 0, 1]
        self.prolong("B1", 2, X1 + 2, "UZ0", "V0", ends, lambda p: 3 + (p - 2) // 2, 0, widen=False)
        self.sweep("V0", "C0", "F0", "B0", 1, 3)
        self.sweep("V0", "C0", "F0", "B0", X + 1, X + 3)
        self.sweep("B0", "C0", "F0", out, 2, X + 2, rows0, shift=2)
        for h in (self.hE0, *self.hE0x, *self.hF0, self.hE1, self.hF1):
            self.halo_sent(h)
        for h in self.hV0:
            self.halo_sent(h, "x")
        self.ring_sent(self.aG1)
        self.share_sent()
        self.member_sent()
        for n in ("f2", "v2"):
            self.win_sent(n)

    def __call__(self, forcing, phase):
        any_space = pl.BlockSpec(memory_space=pl.ANY)
        sems = [pltpu.SemaphoreType.DMA((self.n_sems,)), pltpu.SemaphoreType.DMA((self.n_sems,)),
                pltpu.SemaphoreType.DMA((2,))]
        return pl.pallas_call(
            self.body,
            out_shape=pltpu.VMEM(forcing.shape, jnp.float32),
            in_specs=[any_space, any_space],
            out_specs=pl.BlockSpec(memory_space=pltpu.VMEM),
            scratch_shapes=list(self.scratch.values()) + sems,
            compiler_params=pltpu.CompilerParams(
                collective_id=0, has_side_effects=True, vmem_limit_bytes=60 * 1024 * 1024),
            name="vcycle",
        )(forcing, phase)


def solution(mesh):
    grid = (mesh.shape["gx"], mesh.shape["gy"])

    def per_device(forcing, phase_ids):
        return Kernel(phase_ids.shape, forcing.shape[0], grid)(forcing, phase_ids)

    return jax.shard_map(
        per_device,
        mesh=mesh,
        in_specs=(P(None, "gx", "gy", None), P("gx", "gy", None)),
        out_specs=P(None, "gx", "gy", None),
        check_vma=False,
    )
```
